128 devices in a mesh: gauss: 8 (over y, core), tile: 16 (over z, x).
Axes of the slice: x: 4, y: 4, z: 4, core: 2. Of those that a mesh axis runs over, the one named last changes fastest.
Arguments:
- params: float32 [59, 65536], P(None, ('gauss', 'tile')), as said below
- moment_one: float32 [59, 65536], P(None, ('gauss', 'tile')), may hold values from -1.8 to 1.8
- moment_two: float32 [59, 65536], P(None, ('gauss', 'tile')), may hold values from 1e-06 to 0.01
- camera: float32 [3, 11], replicated, as said below
- target: float32 [3, 3, 128, 256], P(None, None, ('gauss', 'tile')), may hold values from 0 to 1
- tile_ids: int32 [3, 128], P(None, ('gauss', 'tile')), may hold values from 0 to 127, as said below
- splat_lists: int32 [3, 128, 256], P(None, ('gauss', 'tile')), may hold values from 0 to 65535, as said below
- counts: int32 [3, 128], P(None, ('gauss', 'tile')), may hold values from 32 to 256, as said below
Outputs:
- new_params: float32 [59, 65536], P(None, ('gauss', 'tile'))
- new_first: float32 [59, 65536], P(None, ('gauss', 'tile'))
- new_second: float32 [59, 65536], P(None, ('gauss', 'tile'))
- rendered: float32 [3, 3, 128, 256], P(None, None, ('gauss', 'tile'))
- view_losses: float32 [3], replicated
The draws below stay inside these ranges and needn't reach their ends.
Inputs may be any that keep to these rules, and one draw needn't show every extreme that they name: `splat_lists`: entries of slot q lie in [b * 8192, (b + 1) * 8192) with b = q // 16; entries at or past the slot's count are padding. `counts`: every view has a slot whose count is 256. `tile_ids`: in each view the slots q with q // 16 = b hold each tile of b * 16 to (b + 1) * 16 - 1 once. `params`: row 6 lies in [0.5, 1.5]. `camera`: entries 8 to 10 of each row form a unit vector.
All inputs are finite; a program needn't handle non-finite values.
Results may differ from the reference program's by a relative error of at most 0.0003.
Values sent between devices are 32-bit elements; how exact they have to be, the bound alone decides.
No kernel may reach another device: no remote copies, remote signals or barrier semaphores. Data moves between devices by JAX's collectives and lax.ppermute only.
A program may use at most 64 MiB of HBM per device.

```python
import math
import jax
import jax.numpy as jnp
from jax import lax

PARAMS = 59
LIST = 256
VIEWS = 3
TILES_WIDE = 4
BAND_G = 8192
BAND_TILES = 16
GAUSS = 65536
TILES = 128


def layout(key):
    base = jax.random.fold_in(key, 11)
    bands = GAUSS // BAND_G
    order = jax.vmap(lambda subkey: jax.random.permutation(subkey, BAND_G))(jax.random.split(jax.random.fold_in(base, 1), bands))
    shuffled = jax.vmap(lambda subkey: jax.random.permutation(subkey, BAND_TILES))(jax.random.split(jax.random.fold_in(base, 2), VIEWS * bands))
    tiles = shuffled.reshape(VIEWS, bands, BAND_TILES) + (jnp.arange(bands) * BAND_TILES)[None, :, None]
    return (order.astype(jnp.int32), tiles.reshape(VIEWS, TILES).astype(jnp.int32))


def draw_params(key, part):
    order, tiles = layout(key)
    bands = GAUSS // BAND_G
    per_home = BAND_G // BAND_TILES
    spread = jnp.broadcast_to(jnp.arange(BAND_G, dtype=jnp.int32)[None, :] // per_home, (bands, BAND_G))
    home = jnp.zeros((bands, BAND_G), jnp.int32).at[jnp.arange(bands)[:, None], order].set(spread)
    home = (home + jnp.arange(bands, dtype=jnp.int32)[:, None] * BAND_TILES).reshape(GAUSS)
    keys = jax.random.split(jax.random.fold_in(key, 21), 8)
    place_x = (home % TILES_WIDE * 16).astype(jnp.float32) + 16.0 * jax.random.uniform(keys[0], (GAUSS,))
    place_y = (home // TILES_WIDE * 16).astype(jnp.float32) + 16.0 * jax.random.uniform(keys[1], (GAUSS,))
    depth = jax.random.uniform(keys[2], (GAUSS,), minval=-1.0, maxval=1.0)
    log_scale = jax.random.uniform(keys[3], (3, GAUSS), minval=-3.8, maxval=-2.4)
    quat_w = jax.random.uniform(keys[4], (1, GAUSS), minval=0.5, maxval=1.5)
    quat_rest = jnp.clip(0.5 * jax.random.normal(keys[5], (3, GAUSS)), -1.5, 1.5)
    logit = jnp.clip(-4.0 + jax.random.normal(keys[6], (1, GAUSS)), -8.0, 0.0)
    coeffs = 0.6 * jax.random.normal(keys[7], (48, GAUSS))
    centres = jnp.stack([place_x / 64.0, place_y / 64.0, depth])
    return jnp.concatenate([centres, log_scale, quat_w, quat_rest, logit, coeffs], axis=0).astype(jnp.float32)


def draw_tile_ids(key, part):
    return layout(key)[1]


def draw_splat_lists(key, part):
    order, tiles = layout(key)
    per_home = BAND_G // BAND_TILES
    rows_band = BAND_TILES // TILES_WIDE
    keys = jax.random.split(jax.random.fold_in(key, 31), 3)
    band = jnp.arange(TILES, dtype=jnp.int32) // BAND_TILES
    local_tile = tiles - band[None, :] * BAND_TILES
    step_row = (jax.random.randint(keys[0], (VIEWS, TILES, LIST), 0, 4) + 1) // 2 - 1
    step_col = (jax.random.randint(keys[1], (VIEWS, TILES, LIST), 0, 4) + 1) // 2 - 1
    near_row = jnp.clip(local_tile[:, :, None] // TILES_WIDE + step_row, 0, rows_band - 1)
    near_col = jnp.clip(local_tile[:, :, None] % TILES_WIDE + step_col, 0, TILES_WIDE - 1)
    chosen = (near_row * TILES_WIDE + near_col) * per_home + jax.random.randint(keys[2], (VIEWS, TILES, LIST), 0, per_home)
    band_full = jnp.broadcast_to(band[None, :, None], (VIEWS, TILES, LIST))
    return (order[band_full, chosen] + band_full * BAND_G).astype(jnp.int32)


def draw_counts(key, part):
    divisor = jax.random.randint(jax.random.fold_in(key, 41), (VIEWS, TILES), 1, 9)
    filled = (LIST // divisor).at[:, 0].set(LIST)
    return filled.astype(jnp.int32)


def draw_camera(key, part):
    keys = jax.random.split(jax.random.fold_in(key, 51), 4)
    jitter = jax.random.uniform(keys[0], (VIEWS, 4), minval=-0.02, maxval=0.02)
    shear = jax.random.uniform(keys[1], (VIEWS, 2), minval=-4.0, maxval=4.0)
    offset = jax.random.uniform(keys[2], (VIEWS, 2), minval=-3.0, maxval=3.0)
    tilt = jax.random.uniform(keys[3], (VIEWS, 2), minval=-0.4, maxval=0.4)
    length = jnp.sqrt(1.0 + tilt[:, 0] * tilt[:, 0] + tilt[:, 1] * tilt[:, 1])
    rows = jnp.stack([64.0 * (1.0 + jitter[:, 0]), 64.0 * jitter[:, 1], shear[:, 0], 64.0 * jitter[:, 2], 64.0 * (1.0 + jitter[:, 3]), shear[:, 1], offset[:, 0], offset[:, 1], tilt[:, 0] / length, tilt[:, 1] / length, 1.0 / length], axis=1)
    return rows.astype(jnp.float32)


def level_of(rng, shape, cuts, low, largest):
    def one(position, shards_of):
        draws = jax.random.uniform(jax.random.fold_in(jax.random.fold_in(rng, 6), position), (shards_of,), jnp.float32, low / len(cuts), largest / len(cuts))
        return jnp.repeat(jnp.exp(draws), shape[position] // shards_of).reshape((-1,) + (1,) * (len(shape) - position - 1))

    gain = one(*cuts[0])
    for cut in cuts[1:]:
        gain = gain * one(*cut)
    return gain


def normal_values(own_key, dims, scale, most, cuts=(), kind=jnp.bfloat16):
    values = jax.random.normal(own_key, dims, jnp.float32) * scale
    if len(cuts) > 0:
        values = level_of(own_key, dims, cuts, -0.22, 0.18) * values
    return jnp.clip(values, min=-most, max=most).astype(kind)


def setup_inputs(seed: int = 0) -> dict:
    streams_of = jax.random.split(jax.random.key(seed), 9)
    return {
        "params": draw_params(jax.random.fold_in(streams_of[8], 71), 0),
        "moment_one": normal_values(streams_of[1], (PARAMS, GAUSS), 0.3, 1.8, ((1, 128),), jnp.float32),
        "moment_two": jnp.clip(jnp.exp(math.log(0.01) - 9.2103404 * jax.random.uniform(streams_of[2], (PARAMS, GAUSS), jnp.float32) ** level_of(streams_of[2], (PARAMS, GAUSS), ((1, 128),), -0.2, 0.2)), 9.999999974752427e-07, 0.01),
        "camera": draw_camera(jax.random.fold_in(streams_of[8], 71), 0),
        "target": jnp.clip(1.0 * jax.random.uniform(streams_of[4], (VIEWS, 3, TILES, 256), jnp.float32) ** level_of(streams_of[4], (VIEWS, 3, TILES, 256), ((2, 128),), -0.2, 0.2), 0.0, 1.0),
        "tile_ids": draw_tile_ids(jax.random.fold_in(streams_of[8], 71), 0),
        "splat_lists": draw_splat_lists(jax.random.fold_in(streams_of[8], 71), 0),
        "counts": draw_counts(jax.random.fold_in(streams_of[8], 71), 0),
    }


band_zero = 0.28209479177387814
band_one = 0.4886025119029199
band_two = (1.0925484305920792, -1.0925484305920792, 0.31539156525252005, -1.0925484305920792, 0.5462742152960396)
band_three = (-0.5900435899266435, 2.890611442640554, -0.4570457994644658, 0.3731763325901154, -0.4570457994644658, 1.445305721320277, -0.5900435899266435)
learning_rates = (0.00016,) * 3 + (0.005,) * 3 + (0.001,) * 4 + (0.05,) + (0.0025,) * 3 + (0.000125,) * 45
highest = lax.Precision.HIGHEST

def harmonics(facing):
    facing_x, facing_y, facing_z = (facing[0], facing[1], facing[2])
    square_x, square_y, square_z = (facing_x * facing_x, facing_y * facing_y, facing_z * facing_z)
    return jnp.stack([band_zero + 0.0 * facing_x, -band_one * facing_y, band_one * facing_z, -band_one * facing_x, band_two[0] * facing_x * facing_y, band_two[1] * facing_y * facing_z, band_two[2] * (2.0 * square_z - square_x - square_y), band_two[3] * facing_x * facing_z, band_two[4] * (square_x - square_y), band_three[0] * facing_y * (3.0 * square_x - square_y), band_three[1] * facing_x * facing_y * facing_z, band_three[2] * facing_y * (4.0 * square_z - square_x - square_y), band_three[3] * facing_z * (2.0 * square_z - 3.0 * square_x - 3.0 * square_y), band_three[4] * facing_x * (4.0 * square_z - square_x - square_y), band_three[5] * facing_z * (square_x - square_y), band_three[6] * facing_x * (square_x - 3.0 * square_y)])

def project(params, camera):
    quaternion = params[6:10]
    quat_norm = jnp.sqrt(lax.optimization_barrier(jnp.sum(quaternion * quaternion, axis=0)))
    quat_w, quat_x, quat_y, quat_z = [quaternion[component] / quat_norm for component in range(4)]
    rotation = jnp.stack([1.0 - 2.0 * (quat_y * quat_y + quat_z * quat_z), 2.0 * (quat_x * quat_y - quat_w * quat_z), 2.0 * (quat_x * quat_z + quat_w * quat_y), 2.0 * (quat_x * quat_y + quat_w * quat_z), 1.0 - 2.0 * (quat_x * quat_x + quat_z * quat_z), 2.0 * (quat_y * quat_z - quat_w * quat_x), 2.0 * (quat_x * quat_z - quat_w * quat_y), 2.0 * (quat_y * quat_z + quat_w * quat_x), 1.0 - 2.0 * (quat_x * quat_x + quat_y * quat_y)]).reshape(3, 3, -1)
    stretched = rotation * jnp.exp(params[3:6])[None, :, :]
    affine = camera[0:6].reshape(2, 3)
    screen_axes = jnp.einsum('ki,ijn->kjn', affine, stretched, precision=highest)
    cov_a = lax.optimization_barrier(jnp.sum(screen_axes[0] * screen_axes[0], axis=0)) + 0.3
    cov_b = lax.optimization_barrier(jnp.sum(screen_axes[0] * screen_axes[1], axis=0))
    cov_c = lax.optimization_barrier(jnp.sum(screen_axes[1] * screen_axes[1], axis=0)) + 0.3
    determinant = cov_a * cov_c - cov_b * cov_b
    centre_px = jnp.einsum('ki,in->kn', affine, params[0:3], precision=highest) + camera[6:8][:, None]
    opacity = jax.nn.sigmoid(params[10])
    coeffs = params[11:59].reshape(16, 3, -1)
    colour = jnp.maximum(jnp.einsum('i,ikn->kn', harmonics(camera[8:11]), coeffs, precision=highest) + 0.5, 0.0)
    return jnp.concatenate([centre_px, jnp.stack([cov_c / determinant, -cov_b / determinant, cov_a / determinant, opacity]), colour], axis=0)

def shade(splat_attrs, live_count, tile_id):
    pixel_index = jnp.arange(256, dtype=jnp.int32)
    pixel_x = (tile_id % TILES_WIDE * 16 + pixel_index % 16).astype(jnp.float32) + 0.5
    pixel_y = (tile_id // TILES_WIDE * 16 + pixel_index // 16).astype(jnp.float32) + 0.5
    offset_x = pixel_x[:, None] - splat_attrs[0][None, :]
    offset_y = pixel_y[:, None] - splat_attrs[1][None, :]
    exponent = -0.5 * (splat_attrs[2] * offset_x * offset_x + splat_attrs[4] * offset_y * offset_y) - splat_attrs[3] * offset_x * offset_y
    live_slots = jnp.arange(splat_attrs.shape[1], dtype=jnp.int32) < live_count
    coverage = jnp.where(live_slots[None, :], jnp.minimum(0.99, splat_attrs[5] * jnp.exp(exponent)), 0.0)
    log_keep = jnp.log(1.0 - coverage)
    before = jnp.concatenate([jnp.zeros_like(log_keep[:, :1]), jnp.cumsum(log_keep[:, :-1], axis=1)], axis=1)
    weights = coverage * jnp.exp(before)
    return jnp.einsum('pj,kj->kp', weights, splat_attrs[6:9], precision=highest)

def adam(params, moment_one, moment_two, gradient):
    rates = jnp.array(learning_rates, dtype=jnp.float32)[:, None]
    first = 0.9 * moment_one + 0.1 * gradient
    second = 0.999 * moment_two + 0.001 * gradient * gradient
    return (params - rates * first / (jnp.sqrt(second) + 1e-15), first, second)

def reference(params, moment_one, moment_two, camera, target, tile_ids, splat_lists, counts):
    grad_scale = 1.0 / (VIEWS * 256)
    gradient = jnp.zeros_like(params)
    images_all = []
    losses = []
    for view_index in range(VIEWS):
        attrs_all, pullback = jax.vjp(lambda values: project(values, camera[view_index]), params)

        def one_tile(item):
            splat_ids, live_count, tile_id, target_tile = item
            splat_attrs = jnp.take(attrs_all, splat_ids, axis=1)
            colours, tile_back = jax.vjp(lambda values: shade(values, live_count, tile_id), splat_attrs)
            residual = colours - target_tile
            attr_grad, = tile_back(residual * grad_scale)
            return (colours, jnp.sum(residual * residual), attr_grad)
        colours, squared, attr_grads = lax.map(one_tile, (splat_lists[view_index], counts[view_index], tile_ids[view_index], jnp.transpose(target[view_index], (1, 0, 2))))
        flat_grad = jnp.transpose(attr_grads, (1, 0, 2)).reshape(9, -1)
        summed = jnp.zeros_like(attrs_all).at[:, splat_lists[view_index].reshape(-1)].add(flat_grad)
        gradient = gradient + pullback(summed)[0]
        images_all.append(jnp.transpose(colours, (1, 0, 2)))
        losses.append(0.5 * jnp.sum(squared) / (3 * 256 * TILES))
    return adam(params, moment_one, moment_two, gradient) + (jnp.stack(images_all), jnp.stack(losses))
```

```python
import jax
import jax.numpy as jnp
from jax import lax
from jax.experimental import pallas as pl
from jax.experimental.pallas import tpu as pltpu
from jax.sharding import Mesh
from jax.sharding import PartitionSpec as P

VIEWS = 3
TILES_WIDE = 4
TILE = ("tile_0", "tile_1")
GAUSS_TILE = ("gauss_0", "gauss_1", "tile_0", "tile_1")
OWNERS = 16
OWN = 512
GEOMETRY = 11
ROWS = 20
SEND = 4 * ROWS
BACK = SEND + 8
GROUPS = 6
LOG2E = 1.4426950408889634

band_zero = 0.28209479177387814
band_one = 0.4886025119029199
band_two = (
    1.0925484305920792,
    -1.0925484305920792,
    0.31539156525252005,
    -1.0925484305920792,
    0.5462742152960396,
)
band_three = (
    -0.5900435899266435,
    2.890611442640554,
    -0.4570457994644658,
    0.3731763325901154,
    -0.4570457994644658,
    1.445305721320277,
    -0.5900435899266435,
)

f32 = jnp.float32
bf16 = jnp.bfloat16


def iota(shape, dim):
    return lax.broadcasted_iota(jnp.int32, shape, dim)


def harmonic_halves(camera_ref, view):
    x, y, z = [jnp.full((8, 128), camera_ref[view, 8 + i], f32) for i in range(3)]
    xx, yy, zz = x * x, y * y, z * z
    values = [
        jnp.full((8, 128), band_zero, f32),
        -band_one * y,
        band_one * z,
        -band_one * x,
        band_two[0] * x * y,
        band_two[1] * y * z,
        band_two[2] * (2.0 * zz - xx - yy),
        band_two[3] * x * z,
        band_two[4] * (xx - yy),
        band_three[0] * y * (3.0 * xx - yy),
        band_three[1] * x * y * z,
        band_three[2] * y * (4.0 * zz - xx - yy),
        band_three[3] * z * (2.0 * zz - 3.0 * xx - 3.0 * yy),
        band_three[4] * x * (4.0 * zz - xx - yy),
        band_three[5] * z * (xx - yy),
        band_three[6] * x * (xx - 3.0 * yy),
    ]
    row = iota((8, 128), 0)
    halves = []
    for half in range(2):
        column = values[8 * half]
        for i in range(1, 8):
            column = jnp.where(row == i, values[8 * half + i], column)
        halves.append(column)
    return halves


def pack_kernel(params_ref, camera_ref, send_ref, slope_ref, pack_ref, tall_ref):
    for quarter in range(4):
        lanes = pl.ds(128 * quarter, 128)
        pack_ref[pl.ds(quarter, 8, stride=4), :] = params_ref[0:8, lanes]
        pack_ref[pl.ds(32 + quarter, 3, stride=4), :] = params_ref[8:11, lanes]
        tall_ref[pl.ds(64 * quarter, 59), :] = params_ref[:, lanes]
    columns = [harmonic_halves(camera_ref, view) for view in range(VIEWS)]
    for k in range(3):
        for quarter in range(4):
            low = tall_ref[pl.ds(64 * quarter + 11 + k, 8, stride=3), :]
            high = tall_ref[pl.ds(64 * quarter + 35 + k, 8, stride=3), :]
            for view in range(VIEWS):
                terms = columns[view][0] * low + columns[view][1] * high
                raw = jnp.sum(terms, axis=0, keepdims=True) + 0.5
                row = 4 * (3 * view + k) + quarter
                pack_ref[pl.ds(4 * GEOMETRY + row, 1), :] = jnp.maximum(raw, 0.0)
                slope_ref[pl.ds(row, 1), :] = jnp.where(
                    raw > 0.0, 1.0, jnp.where(raw == 0.0, 0.5, 0.0)
                )
    packed = pack_ref[...]
    for owner in range(OWNERS):
        send_ref[pl.ds(SEND * owner, SEND), :] = packed


def split(value):
    high = value.astype(bf16)
    return high, (value - high.astype(f32)).astype(bf16)


def nn(lhs, rhs):
    return lax.dot_general(lhs, rhs, (((1,), (0,)), ((), ())), preferred_element_type=f32)


def nt(lhs, rhs):
    return lax.dot_general(lhs, rhs, (((1,), (1,)), ((), ())), preferred_element_type=f32)


def tn(lhs, rhs):
    return lax.dot_general(lhs, rhs, (((0,), (0,)), ((), ())), preferred_element_type=f32)


def render_kernel(
    table_ref,
    lists_ref,
    counts_ref,
    tiles_ref,
    camera_ref,
    target_ref,
    rendered_ref,
    back_ref,
    found_ref,
    lane_ref,
    rows_ref,
    colour_ref,
    shade_ref,
    logs_ref,
    keep_ref,
    high_ref,
    low_ref,
    moment_ref,
    tint_ref,
    grads_ref,
    spread_ref,
    places_ref,
    tri_ref,
    loss_ref,
):
    quarter = iota((8, 128), 0) & 3
    for group in range(GROUPS):
        view, half = divmod(group, 2)
        local = lists_ref[view, :, 128 * half : 128 * half + 128] & 8191
        local = jnp.broadcast_to(local, (8, 128))
        lane = local & 127
        block = (local >> 7) - quarter
        first = (4 * (GEOMETRY + 3 * view)) // 8
        last = (4 * (GEOMETRY + 3 * view + 3) - 1) // 8
        pieces = sorted(set(range(6)) | set(range(first, last + 1)))
        found = {piece: jnp.zeros((8, 128), f32) for piece in pieces}
        for owner in range(OWNERS):
            here = block == 4 * owner
            for piece in pieces:
                rows = table_ref[pl.ds(SEND * owner + 8 * piece, 8), :]
                picked = jnp.take_along_axis(rows, lane, axis=1, mode="promise_in_bounds")
                found[piece] = jnp.where(here, picked, found[piece])
        for piece in pieces:
            found_ref[pl.ds(SEND * group + 8 * piece, 8), :] = found[piece]

    def entry_row(row):
        parts = [found_ref[pl.ds(4 * row + q, GROUPS, stride=SEND), :] for q in range(4)]
        return (parts[0] + parts[1]) + (parts[2] + parts[3])

    for group in range(GROUPS):
        view, half = divmod(group, 2)
        for k in range(3):
            start = SEND * group + 4 * (GEOMETRY + 3 * view + k)
            value = jnp.sum(found_ref[pl.ds(start, 4), :], axis=0, keepdims=True)
            colour_ref[pl.ds(8 * view + k, 1), pl.ds(128 * half, 128)] = value

    place = iota((GROUPS, 128), 0)

    def per_view(values):
        return jnp.where(place < 2, values[0], jnp.where(place < 4, values[1], values[2]))

    camera = [per_view([camera_ref[view, i] for view in range(VIEWS)]) for i in range(8)]
    affine = (camera[0:3], camera[3:6])
    centre = [entry_row(i) for i in range(3)]
    scale = [jnp.exp(entry_row(3 + i)) for i in range(3)]
    raw = [entry_row(6 + i) for i in range(4)]
    logit = entry_row(10)
    inverse_norm = 1.0 / jnp.sqrt(
        raw[0] * raw[0] + raw[1] * raw[1] + raw[2] * raw[2] + raw[3] * raw[3]
    )
    qw, qx, qy, qz = [component * inverse_norm for component in raw]
    rotation = [
        [1.0 - 2.0 * (qy * qy + qz * qz), 2.0 * (qx * qy - qw * qz), 2.0 * (qx * qz + qw * qy)],
        [2.0 * (qx * qy + qw * qz), 1.0 - 2.0 * (qx * qx + qz * qz), 2.0 * (qy * qz - qw * qx)],
        [2.0 * (qx * qz - qw * qy), 2.0 * (qy * qz + qw * qx), 1.0 - 2.0 * (qx * qx + qy * qy)],
    ]
    stretched = [[rotation[i][j] * scale[j] for j in range(3)] for i in range(3)]
    screen = [
        [sum(affine[k][i] * stretched[i][j] for i in range(3)) for j in range(3)] for k in range(2)
    ]
    cov_a = sum(screen[0][j] * screen[0][j] for j in range(3)) + 0.3
    cov_b = sum(screen[0][j] * screen[1][j] for j in range(3))
    cov_c = sum(screen[1][j] * screen[1][j] for j in range(3)) + 0.3
    inverse_det = 1.0 / (cov_a * cov_c - cov_b * cov_b)
    position = (place & 1) * 128 + iota((GROUPS, 128), 1)
    live = position < per_view([counts_ref[view, 0] for view in range(VIEWS)])
    conic = [
        jnp.where(live, value * inverse_det, 0.0) for value in (cov_c, -cov_b, cov_a)
    ]
    mean = [sum(affine[k][i] * centre[i] for i in range(3)) + camera[6 + k] for k in range(2)]
    opacity = 1.0 / (1.0 + jnp.exp(-logit))
    shown = jnp.where(live, opacity, 0.0)
    tile = per_view([tiles_ref[view, 0] for view in range(VIEWS)])
    middle_x = (tile % TILES_WIDE * 16 + 8).astype(f32)
    middle_y = (tile // TILES_WIDE * 16 + 8).astype(f32)
    shift_x = mean[0] - middle_x
    shift_y = mean[1] - middle_y
    quantities = [
        shift_x,
        shift_y,
        (-0.5 * LOG2E) * conic[0],
        (-LOG2E) * conic[1],
        (-0.5 * LOG2E) * conic[2],
        shown,
    ]
    for n, value in enumerate(quantities):
        lane_ref[pl.ds(8 * n, GROUPS), :] = value
    for n in range(len(quantities)):
        for half in range(2):
            rows_ref[pl.ds(8 * n, VIEWS), pl.ds(128 * half, 128)] = lane_ref[
                pl.ds(8 * n + half, VIEWS, stride=2), :
            ]

    before = iota((256, 256), 0)
    after = iota((256, 256), 1)
    strictly = jnp.where(before < after, 1.0, 0.0).astype(bf16)
    tri_ref[0:256, :] = strictly
    tri_ref[256:512, :] = strictly
    strictly = jnp.where(before > after, 1.0, 0.0).astype(bf16)
    tri_ref[512:768, :] = strictly
    tri_ref[768:1024, :] = strictly
    pixel = iota((16, 256), 1)
    power = iota((16, 256), 0)
    pixel_u = (pixel % 16).astype(f32) - 7.5
    pixel_v = (pixel // 16).astype(f32) - 7.5
    basis = jnp.where(power == 0, 1.0, jnp.where(power == 1, pixel_u, pixel_v))
    basis = jnp.where(power == 3, pixel_u * pixel_u, basis)
    basis = jnp.where(power == 4, pixel_u * pixel_v, basis)
    basis = jnp.where(power == 5, pixel_v * pixel_v, basis)
    basis = jnp.where(power > 5, 0.0, basis).astype(bf16)
    offset = iota((16, 256), 0).astype(f32) - 7.5
    loss_ref[...] = jnp.zeros_like(loss_ref)
    kinds = iota((16, 256), 0)

    def one_view(view, carry):
        def row(n):
            return rows_ref[pl.ds(8 * n + view, 1), :]

        mean_u, mean_v = row(0), row(1)
        opaque = jnp.broadcast_to(row(5), (16, 256))
        dx = offset - mean_u
        along = row(2) * dx * dx
        across = row(3) * dx
        upright = row(4)
        for line in range(16):
            dy = (line - 7.5) - mean_v
            exponent = along + (upright * dy * dy + across * dy)
            shade = opaque * jnp.exp2(exponent)
            shade_ref[pl.ds(16 * line, 16), :] = shade
            high, low = split(jnp.log(1.0 - jnp.minimum(shade, 0.99)))
            logs_ref[pl.ds(16 * line, 16), 0:256] = high
            logs_ref[pl.ds(16 * line, 16), 256:512] = low
        for part in range(4):
            rows = pl.ds(64 * part, 64)
            keep = jnp.exp(nn(logs_ref[rows, :], tri_ref[0:512, :]))
            keep_ref[rows, :] = keep
            high, low = split(jnp.minimum(shade_ref[rows, :], 0.99) * keep)
            high_ref[rows, :] = high
            low_ref[rows, :] = low
        colour = colour_ref[pl.ds(pl.multiple_of(8 * view, 8), 8), :]
        colour_high, colour_low = [part.astype(f32) for part in split(colour)]
        stacked = jnp.concatenate(
            [
                colour_high[0:3],
                colour_high[0:3],
                colour_low[0:3],
                jnp.zeros((7, 256), f32),
            ],
            axis=0,
        ).astype(bf16)
        image_high = nt(stacked, high_ref[...])
        image_low = nt(stacked, low_ref[...])
        image = image_high[0:3] + image_high[6:9] + image_low[0:3]
        residuals = []
        total = jnp.zeros((1, 256), f32)
        for k in range(3):
            rendered_ref[view, k, :, :] = image[k : k + 1]
            residual = image[k : k + 1] - target_ref[view, k, :, :]
            total = total + residual * residual
            residuals.append(residual * (1.0 / (VIEWS * 256)))
        loss_ref[...] += jnp.where(
            iota((8, 128), 1) == view, jnp.sum(total, axis=1, keepdims=True), 0.0
        )
        error = jnp.concatenate(residuals, axis=0)
        error_high, error_low = [part.astype(f32) for part in split(error)]
        pulled = jnp.concatenate(
            [error_high, error_low, error_high, jnp.zeros((7, 256), f32)], axis=0
        ).astype(bf16)
        tint = nn(pulled, high_ref[...])
        tint_low = nn(pulled, low_ref[...])
        tint_ref[pl.ds(pl.multiple_of(8 * view, 8), 3), :] = (
            tint[0:3] + tint[3:6] + tint_low[0:3]
        )
        pull = tn(pulled, stacked)
        for part in range(4):
            rows = pl.ds(64 * part, 64)
            weight = jnp.minimum(shade_ref[rows, :], 0.99) * keep_ref[rows, :]
            high, low = split(pull[64 * part : 64 * part + 64] * weight)
            logs_ref[rows, 0:256] = high
            logs_ref[rows, 256:512] = low
        for part in range(4):
            rows = pl.ds(64 * part, 64)
            behind = nn(logs_ref[rows, :], tri_ref[512:1024, :])
            shade = shade_ref[rows, :]
            alpha = jnp.minimum(shade, 0.99)
            slope = pull[64 * part : 64 * part + 64] * keep_ref[rows, :] - behind / (1.0 - alpha)
            passed = jnp.where(shade < 0.99, shade, jnp.where(shade == 0.99, 0.5 * shade, 0.0))
            high, low = split(slope * passed)
            high_ref[rows, :] = high
            low_ref[rows, :] = low
        moments = nn(basis, high_ref[...]) + nn(basis, low_ref[...])
        for half in range(2):
            moment_ref[pl.ds(2 * view + half, 8, stride=8), :] = moments[
                0:8, 128 * half : 128 * half + 128
            ]
        return carry

    lax.fori_loop(0, VIEWS, one_view, 0)

    m_0, m_u, m_v, m_uu, m_uv, m_vv = [
        moment_ref[pl.ds(8 * n, GROUPS), :] for n in range(6)
    ]
    m_x = m_u - shift_x * m_0
    m_y = m_v - shift_y * m_0
    m_xx = m_uu - 2.0 * shift_x * m_u + shift_x * shift_x * m_0
    m_xy = m_uv - shift_x * m_v - shift_y * m_u + shift_x * shift_y * m_0
    m_yy = m_vv - 2.0 * shift_y * m_v + shift_y * shift_y * m_0
    d_mean = (conic[0] * m_x + conic[1] * m_y, conic[1] * m_x + conic[2] * m_y)
    left = (
        (conic[0] * m_xx + conic[1] * m_xy, conic[0] * m_xy + conic[1] * m_yy),
        (conic[1] * m_xx + conic[2] * m_xy, conic[1] * m_xy + conic[2] * m_yy),
    )
    d_a = 0.5 * (left[0][0] * conic[0] + left[0][1] * conic[1])
    d_b = left[0][0] * conic[1] + left[0][1] * conic[2]
    d_c = 0.5 * (left[1][0] * conic[1] + left[1][1] * conic[2])
    d_screen = [
        [2.0 * d_a * screen[0][j] + d_b * screen[1][j] for j in range(3)],
        [2.0 * d_c * screen[1][j] + d_b * screen[0][j] for j in range(3)],
    ]
    d_stretched = [
        [affine[0][i] * d_screen[0][j] + affine[1][i] * d_screen[1][j] for j in range(3)]
        for i in range(3)
    ]
    d_scale = [sum(d_stretched[i][j] * stretched[i][j] for i in range(3)) for j in range(3)]
    r = [[d_stretched[i][j] * scale[j] for j in range(3)] for i in range(3)]
    d_unit = [
        2.0 * (qz * (r[1][0] - r[0][1]) + qy * (r[0][2] - r[2][0]) + qx * (r[2][1] - r[1][2])),
        2.0
        * (
            qy * (r[0][1] + r[1][0])
            + qz * (r[0][2] + r[2][0])
            + qw * (r[2][1] - r[1][2])
            - 2.0 * qx * (r[1][1] + r[2][2])
        ),
        2.0
        * (
            qx * (r[0][1] + r[1][0])
            + qz * (r[1][2] + r[2][1])
            + qw * (r[0][2] - r[2][0])
            - 2.0 * qy * (r[0][0] + r[2][2])
        ),
        2.0
        * (
            qx * (r[0][2] + r[2][0])
            + qy * (r[1][2] + r[2][1])
            + qw * (r[1][0] - r[0][1])
            - 2.0 * qz * (r[0][0] + r[1][1])
        ),
    ]
    unit = (qw, qx, qy, qz)
    radial = sum(unit[i] * d_unit[i] for i in range(4))
    gradients = (
        [affine[0][i] * d_mean[0] + affine[1][i] * d_mean[1] for i in range(3)]
        + d_scale
        + [(d_unit[i] - unit[i] * radial) * inverse_norm for i in range(4)]
        + [m_0 * (1.0 - opacity)]
    )
    for n, value in enumerate(gradients):
        high = value.astype(bf16).astype(f32)
        grads_ref[pl.ds(16 * n, GROUPS), :] = high
        grads_ref[pl.ds(16 * n + 8, GROUPS), :] = value - high

    coarse = iota((32, 128), 0)
    fine = iota((256, 128), 0)
    kinds_of = GEOMETRY * 32
    for group in range(GROUPS):
        view, half = divmod(group, 2)
        local = lists_ref[view, :, 128 * half : 128 * half + 128] & 8191
        lanes = pl.ds(128 * group, 128)
        places_ref[:, lanes] = jnp.where((local & 255) == fine, 1.0, 0.0).astype(bf16)
        owner_part = ((local >> 8) & 1) * 16 + (local >> 9)
        chosen = jnp.where(owner_part == coarse, 1.0, 0.0).astype(bf16)
        for n in range(GEOMETRY):
            for part in range(2):
                value = grads_ref[pl.ds(16 * n + 8 * part + group, 1), :]
                spread_ref[pl.ds(kinds_of * part + 32 * n, 32), lanes] = (
                    chosen * jnp.broadcast_to(value, (32, 128)).astype(bf16)
                )
        for k in range(3):
            value = tint_ref[pl.ds(8 * view + k, 1), pl.ds(128 * half, 128)]
            high = value.astype(bf16).astype(f32)
            for part, piece in enumerate((high, value - high)):
                spread_ref[pl.ds(2 * kinds_of + 96 * part + 32 * k, 32), lanes] = (
                    chosen * jnp.broadcast_to(piece, (32, 128)).astype(bf16)
                )

    def store(row, value):
        for upper in range(2):
            for side in range(2):
                back_ref[pl.ds(4 * row + 2 * upper + side, 16, stride=BACK), :] = value[
                    16 * upper : 16 * upper + 16, 128 * side : 128 * side + 128
                ]

    dense = nt(spread_ref[0 : 2 * kinds_of, :], places_ref[...])
    for n in range(GEOMETRY):
        store(n, dense[32 * n : 32 * n + 32] + dense[kinds_of + 32 * n : kinds_of + 32 * n + 32])
    for view in range(VIEWS):
        lanes = slice(256 * view, 256 * view + 256)
        dense = nt(spread_ref[2 * kinds_of : 2 * kinds_of + 192, lanes], places_ref[:, lanes])
        for k in range(3):
            store(
                GEOMETRY + 3 * view + k,
                dense[32 * k : 32 * k + 32] + dense[96 + 32 * k : 96 + 32 * k + 32],
            )
    for owner in range(OWNERS):
        back_ref[pl.ds(BACK * owner + SEND, 8), :] = loss_ref[...]


def adam_kernel(
    back_ref,
    slope_ref,
    params_ref,
    moment_one_ref,
    moment_two_ref,
    camera_ref,
    params_out,
    first_out,
    second_out,
    loss_out,
    total_ref,
    gradient_ref,
):
    total = back_ref[0:BACK, :]
    for owner in range(1, OWNERS):
        total = total + back_ref[pl.ds(BACK * owner, BACK), :]
    total_ref[...] = total
    loss_out[...] = total[SEND : SEND + 8]
    columns = [harmonic_halves(camera_ref, view) for view in range(VIEWS)]
    row = iota((59, 128), 0)
    rates = jnp.where(row < 14, 0.0025, 0.000125)
    rates = jnp.where(row < 11, 0.05, rates)
    rates = jnp.where(row < 10, 0.001, rates)
    rates = jnp.where(row < 6, 0.005, rates)
    rates = jnp.where(row < 3, 0.00016, rates)
    for quarter in range(4):
        lanes = pl.ds(128 * quarter, 128)
        base = 64 * quarter
        gradient_ref[pl.ds(base, 8), :] = total_ref[pl.ds(quarter, 8, stride=4), :]
        gradient_ref[pl.ds(base + 8, 3), :] = total_ref[pl.ds(32 + quarter, 3, stride=4), :]
        for k in range(3):
            tints = []
            for view in range(VIEWS):
                row = 4 * (3 * view + k) + quarter
                tint = total_ref[pl.ds(4 * GEOMETRY + row, 1), :] * slope_ref[pl.ds(row, 1), :]
                tints.append(jnp.broadcast_to(tint, (8, 128)))
            for half in range(2):
                gradient_ref[pl.ds(base + 11 + 24 * half + k, 8, stride=3), :] = sum(
                    columns[view][half] * tints[view] for view in range(VIEWS)
                )
        gradient = gradient_ref[pl.ds(base, 59), :]
        first = 0.9 * moment_one_ref[:, lanes] + 0.1 * gradient
        second = 0.999 * moment_two_ref[:, lanes] + 0.001 * gradient * gradient
        first_out[:, lanes] = first
        second_out[:, lanes] = second
        params_out[:, lanes] = params_ref[:, lanes] - rates * first / (jnp.sqrt(second) + 1e-15)


VM = pl.BlockSpec(memory_space=pltpu.VMEM)
SM = pl.BlockSpec(memory_space=pltpu.SMEM)


def shape(*dims):
    return jax.ShapeDtypeStruct(dims, f32)


def over_pairs(value, axis, pairs):
    both = [(a, b) for a, b in pairs] + [(b, a) for a, b in pairs]
    return value + lax.ppermute(value, axis, both)


def shards(params, moment_one, moment_two, camera, target, tile_ids, splat_lists, counts):
    sent, slope = pl.pallas_call(
        pack_kernel,
        out_shape=(shape(OWNERS * SEND, 128), shape(36, 128)),
        in_specs=[VM, SM],
        out_specs=(VM, VM),
        scratch_shapes=[pltpu.VMEM((SEND, 128), f32), pltpu.VMEM((256, 128), f32)],
        name="pack",
    )(params, camera)
    table = lax.all_to_all(
        sent.reshape(OWNERS, SEND, 128), TILE, split_axis=0, concat_axis=0, tiled=True
    ).reshape(OWNERS * SEND, 128)
    rendered, back = pl.pallas_call(
        render_kernel,
        out_shape=(shape(VIEWS, 3, 1, 256), shape(OWNERS * BACK, 128)),
        in_specs=[VM, VM, SM, SM, SM, VM],
        out_specs=(VM, VM),
        scratch_shapes=[
            pltpu.VMEM((GROUPS * SEND, 128), f32),
            pltpu.VMEM((48, 128), f32),
            pltpu.VMEM((48, 256), f32),
            pltpu.VMEM((24, 256), f32),
            pltpu.VMEM((256, 256), f32),
            pltpu.VMEM((256, 512), bf16),
            pltpu.VMEM((256, 256), f32),
            pltpu.VMEM((256, 256), bf16),
            pltpu.VMEM((256, 256), bf16),
            pltpu.VMEM((64, 128), f32),
            pltpu.VMEM((24, 256), f32),
            pltpu.VMEM((16 * GEOMETRY, 128), f32),
            pltpu.VMEM((2 * 32 * GEOMETRY + 192, 768), bf16),
            pltpu.VMEM((256, 768), bf16),
            pltpu.VMEM((1024, 256), bf16),
            pltpu.VMEM((8, 128), f32),
        ],
        name="render",
    )(table, splat_lists, counts, tile_ids, camera, target)
    arrived = lax.all_to_all(
        back.reshape(OWNERS, BACK, 128), TILE, split_axis=0, concat_axis=0, tiled=True
    ).reshape(OWNERS * BACK, 128)
    updated, first, second, loss = pl.pallas_call(
        adam_kernel,
        out_shape=(shape(59, 512), shape(59, 512), shape(59, 512), shape(8, 128)),
        in_specs=[VM, VM, VM, VM, VM, SM],
        out_specs=(VM, VM, VM, VM),
        scratch_shapes=[pltpu.VMEM((BACK, 128), f32), pltpu.VMEM((256, 128), f32)],
        name="adam",
    )(arrived, slope, params, moment_one, moment_two, camera)
    loss = over_pairs(loss, "gauss_1", [(0, 1)])
    loss = over_pairs(loss, "gauss_0", [(0, 1), (2, 3)])
    loss = over_pairs(loss, "gauss_0", [(0, 3), (1, 2)])
    return (updated, first, second, rendered, loss[0, :VIEWS] * (0.5 / (3 * 256 * 128)))


def solution(mesh):
    finer = Mesh(mesh.devices.reshape(4, 2, 4, 4), GAUSS_TILE)
    in_specs = (
        P(None, GAUSS_TILE),
        P(None, GAUSS_TILE),
        P(None, GAUSS_TILE),
        P(),
        P(None, None, GAUSS_TILE, None),
        P(None, GAUSS_TILE),
        P(None, GAUSS_TILE, None),
        P(None, GAUSS_TILE),
    )
    out_specs = (
        P(None, GAUSS_TILE),
        P(None, GAUSS_TILE),
        P(None, GAUSS_TILE),
        P(None, None, GAUSS_TILE, None),
        P(),
    )
    return jax.shard_map(
        shards, mesh=finer, in_specs=in_specs, out_specs=out_specs, check_vma=False
    )
```

```python
import jax
import jax.numpy as jnp
from jax import lax
from jax.experimental import pallas as pl
from jax.experimental.pallas import tpu as pltpu
from jax.sharding import Mesh
from jax.sharding import PartitionSpec as P

VIEWS = 3
TILES_WIDE = 4
TILE = ("tile_0", "tile_1")
GAUSS = ("gauss_0", "gauss_1")
GAUSS_TILE = ("gauss_0", "gauss_1", "tile_0", "tile_1")
OWNERS = 16
OWN = 512
GEOMETRY = 11
ROWS = 20
SEND = 4 * ROWS
BACK = SEND + 8
GROUPS = 6
KEPT = 33
LOG2E = 1.4426950408889634

band_zero = 0.28209479177387814
band_one = 0.4886025119029199
band_two = (
    1.0925484305920792,
    -1.0925484305920792,
    0.31539156525252005,
    -1.0925484305920792,
    0.5462742152960396,
)
band_three = (
    -0.5900435899266435,
    2.890611442640554,
    -0.4570457994644658,
    0.3731763325901154,
    -0.4570457994644658,
    1.445305721320277,
    -0.5900435899266435,
)

f32 = jnp.float32
bf16 = jnp.bfloat16


def iota(shape, dim):
    return lax.broadcasted_iota(jnp.int32, shape, dim)


def harmonic_halves(camera_ref, view):
    x, y, z = [jnp.full((8, 128), camera_ref[view, 8 + i], f32) for i in range(3)]
    xx, yy, zz = x * x, y * y, z * z
    values = [
        jnp.full((8, 128), band_zero, f32),
        -band_one * y,
        band_one * z,
        -band_one * x,
        band_two[0] * x * y,
        band_two[1] * y * z,
        band_two[2] * (2.0 * zz - xx - yy),
        band_two[3] * x * z,
        band_two[4] * (xx - yy),
        band_three[0] * y * (3.0 * xx - yy),
        band_three[1] * x * y * z,
        band_three[2] * y * (4.0 * zz - xx - yy),
        band_three[3] * z * (2.0 * zz - 3.0 * xx - 3.0 * yy),
        band_three[4] * x * (4.0 * zz - xx - yy),
        band_three[5] * z * (xx - yy),
        band_three[6] * x * (xx - 3.0 * yy),
    ]
    row = iota((8, 128), 0)
    halves = []
    for half in range(2):
        column = values[8 * half]
        for i in range(1, 8):
            column = jnp.where(row == i, values[8 * half + i], column)
        halves.append(column)
    return halves


def pack_kernel(params_ref, camera_ref, send_ref, slope_ref, pack_ref, tall_ref):
    for quarter in range(4):
        lanes = pl.ds(128 * quarter, 128)
        pack_ref[pl.ds(quarter, 8, stride=4), :] = params_ref[0:8, lanes]
        pack_ref[pl.ds(32 + quarter, 3, stride=4), :] = params_ref[8:11, lanes]
        tall_ref[pl.ds(64 * quarter, 59), :] = params_ref[:, lanes]
    columns = [harmonic_halves(camera_ref, view) for view in range(VIEWS)]
    for k in range(3):
        for quarter in range(4):
            low = tall_ref[pl.ds(64 * quarter + 11 + k, 8, stride=3), :]
            high = tall_ref[pl.ds(64 * quarter + 35 + k, 8, stride=3), :]
            for view in range(VIEWS):
                terms = columns[view][0] * low + columns[view][1] * high
                raw = jnp.sum(terms, axis=0, keepdims=True) + 0.5
                row = 4 * (3 * view + k) + quarter
                pack_ref[pl.ds(4 * GEOMETRY + row, 1), :] = jnp.maximum(raw, 0.0)
                slope_ref[pl.ds(row, 1), :] = jnp.where(
                    raw > 0.0, 1.0, jnp.where(raw == 0.0, 0.5, 0.0)
                )
    packed = pack_ref[...]
    for owner in range(OWNERS):
        send_ref[pl.ds(SEND * owner, SEND), :] = packed


def split(value):
    high = value.astype(bf16)
    return high, (value - high.astype(f32)).astype(bf16)


def nn(lhs, rhs):
    return lax.dot_general(lhs, rhs, (((1,), (0,)), ((), ())), preferred_element_type=f32)


def nt(lhs, rhs):
    return lax.dot_general(lhs, rhs, (((1,), (1,)), ((), ())), preferred_element_type=f32)


def tn(lhs, rhs):
    return lax.dot_general(lhs, rhs, (((0,), (0,)), ((), ())), preferred_element_type=f32)


def per_view(values):
    place = iota((GROUPS, 128), 0)
    return jnp.where(place < 2, values[0], jnp.where(place < 4, values[1], values[2]))


def front_kernel(
    table_ref,
    lists_ref,
    counts_ref,
    tiles_ref,
    camera_ref,
    target_ref,
    rendered_ref,
    loss_ref,
    shade_ref,
    keep_ref,
    pulled_ref,
    stacked_ref,
    tint_ref,
    entry_ref,
    found_ref,
    rows_ref,
    colour_ref,
    logs_ref,
    high_ref,
    low_ref,
    tri_ref,
):
    quarter = iota((8, 128), 0) & 3
    for group in range(GROUPS):
        view, half = divmod(group, 2)
        local = lists_ref[view, :, 128 * half : 128 * half + 128] & 8191
        local = jnp.broadcast_to(local, (8, 128))
        lane = local & 127
        block = (local >> 7) - quarter
        first = (4 * (GEOMETRY + 3 * view)) // 8
        last = (4 * (GEOMETRY + 3 * view + 3) - 1) // 8
        pieces = sorted(set(range(6)) | set(range(first, last + 1)))
        found = {piece: jnp.zeros((8, 128), f32) for piece in pieces}
        for owner in range(OWNERS):
            here = block == 4 * owner
            for piece in pieces:
                rows = table_ref[pl.ds(SEND * owner + 8 * piece, 8), :]
                picked = jnp.take_along_axis(rows, lane, axis=1, mode="promise_in_bounds")
                found[piece] = jnp.where(here, picked, found[piece])
        for piece in pieces:
            found_ref[pl.ds(SEND * group + 8 * piece, 8), :] = found[piece]

    def entry_row(row):
        parts = [found_ref[pl.ds(4 * row + q, GROUPS, stride=SEND), :] for q in range(4)]
        return (parts[0] + parts[1]) + (parts[2] + parts[3])

    for group in range(GROUPS):
        view, half = divmod(group, 2)
        for k in range(3):
            start = SEND * group + 4 * (GEOMETRY + 3 * view + k)
            value = jnp.sum(found_ref[pl.ds(start, 4), :], axis=0, keepdims=True)
            colour_ref[pl.ds(8 * view + k, 1), pl.ds(128 * half, 128)] = value

    place = iota((GROUPS, 128), 0)
    camera = [per_view([camera_ref[view, i] for view in range(VIEWS)]) for i in range(8)]
    affine = (camera[0:3], camera[3:6])
    centre = [entry_row(i) for i in range(3)]
    scale = [jnp.exp(entry_row(3 + i)) for i in range(3)]
    raw = [entry_row(6 + i) for i in range(4)]
    logit = entry_row(10)
    inverse_norm = 1.0 / jnp.sqrt(
        raw[0] * raw[0] + raw[1] * raw[1] + raw[2] * raw[2] + raw[3] * raw[3]
    )
    qw, qx, qy, qz = [component * inverse_norm for component in raw]
    rotation = [
        [1.0 - 2.0 * (qy * qy + qz * qz), 2.0 * (qx * qy - qw * qz), 2.0 * (qx * qz + qw * qy)],
        [2.0 * (qx * qy + qw * qz), 1.0 - 2.0 * (qx * qx + qz * qz), 2.0 * (qy * qz - qw * qx)],
        [2.0 * (qx * qz - qw * qy), 2.0 * (qy * qz + qw * qx), 1.0 - 2.0 * (qx * qx + qy * qy)],
    ]
    stretched = [[rotation[i][j] * scale[j] for j in range(3)] for i in range(3)]
    screen = [
        [sum(affine[k][i] * stretched[i][j] for i in range(3)) for j in range(3)] for k in range(2)
    ]
    cov_a = sum(screen[0][j] * screen[0][j] for j in range(3)) + 0.3
    cov_b = sum(screen[0][j] * screen[1][j] for j in range(3))
    cov_c = sum(screen[1][j] * screen[1][j] for j in range(3)) + 0.3
    inverse_det = 1.0 / (cov_a * cov_c - cov_b * cov_b)
    position = (place & 1) * 128 + iota((GROUPS, 128), 1)
    live = position < per_view([counts_ref[view, 0] for view in range(VIEWS)])
    conic = [
        jnp.where(live, value * inverse_det, 0.0) for value in (cov_c, -cov_b, cov_a)
    ]
    mean = [sum(affine[k][i] * centre[i] for i in range(3)) + camera[6 + k] for k in range(2)]
    opacity = 1.0 / (1.0 + jnp.exp(-logit))
    shown = jnp.where(live, opacity, 0.0)
    tile = per_view([tiles_ref[view, 0] for view in range(VIEWS)])
    middle_x = (tile % TILES_WIDE * 16 + 8).astype(f32)
    middle_y = (tile // TILES_WIDE * 16 + 8).astype(f32)
    shift_x = mean[0] - middle_x
    shift_y = mean[1] - middle_y
    kept = (
        [shift_x, shift_y]
        + [(-0.5 * LOG2E) * conic[0], (-LOG2E) * conic[1], (-0.5 * LOG2E) * conic[2]]
        + [shown, opacity, inverse_norm, qw, qx, qy, qz]
        + conic
        + scale
        + screen[0]
        + screen[1]
        + stretched[0]
        + stretched[1]
        + stretched[2]
    )
    for n, value in enumerate(kept):
        entry_ref[pl.ds(8 * n, GROUPS), :] = value
    for n in range(6):
        for half in range(2):
            rows_ref[pl.ds(8 * n, VIEWS), pl.ds(128 * half, 128)] = entry_ref[
                pl.ds(8 * n + half, VIEWS, stride=2), :
            ]

    before = iota((256, 256), 0)
    after = iota((256, 256), 1)
    strictly = jnp.where(before < after, 1.0, 0.0).astype(bf16)
    tri_ref[0:256, :] = strictly
    tri_ref[256:512, :] = strictly
    offset = iota((16, 256), 0).astype(f32) - 7.5
    loss_ref[...] = jnp.zeros_like(loss_ref)

    def one_view(view, carry):
        def row(n):
            return rows_ref[pl.ds(8 * n + view, 1), :]

        mean_u, mean_v = row(0), row(1)
        opaque = jnp.broadcast_to(row(5), (16, 256))
        dx = offset - mean_u
        along = row(2) * dx * dx
        across = row(3) * dx
        upright = row(4)
        base = pl.multiple_of(256 * view, 256)
        for line in range(16):
            dy = (line - 7.5) - mean_v
            exponent = along + (upright * dy * dy + across * dy)
            shade = opaque * jnp.exp2(exponent)
            shade_ref[pl.ds(base + 16 * line, 16), :] = shade
            high, low = split(jnp.log(1.0 - jnp.minimum(shade, 0.99)))
            logs_ref[pl.ds(16 * line, 16), 0:256] = high
            logs_ref[pl.ds(16 * line, 16), 256:512] = low
        for part in range(4):
            rows = pl.ds(64 * part, 64)
            there = pl.ds(base + 64 * part, 64)
            keep = jnp.exp(nn(logs_ref[rows, :], tri_ref[...]))
            keep_ref[there, :] = keep
            high, low = split(jnp.minimum(shade_ref[there, :], 0.99) * keep)
            high_ref[rows, :] = high
            low_ref[rows, :] = low
        colour = colour_ref[pl.ds(pl.multiple_of(8 * view, 8), 8), :]
        colour_high, colour_low = [part.astype(f32) for part in split(colour)]
        stacked = jnp.concatenate(
            [
                colour_high[0:3],
                colour_high[0:3],
                colour_low[0:3],
                jnp.zeros((7, 256), f32),
            ],
            axis=0,
        ).astype(bf16)
        image_high = nt(stacked, high_ref[...])
        image_low = nt(stacked, low_ref[...])
        image = image_high[0:3] + image_high[6:9] + image_low[0:3]
        residuals = []
        total = jnp.zeros((1, 256), f32)
        for k in range(3):
            rendered_ref[view, k, :, :] = image[k : k + 1]
            residual = image[k : k + 1] - target_ref[view, k, :, :]
            total = total + residual * residual
            residuals.append(residual * (1.0 / (VIEWS * 256)))
        loss_ref[...] += jnp.where(
            iota((8, 128), 1) == view, jnp.sum(total, axis=1, keepdims=True), 0.0
        )
        error = jnp.concatenate(residuals, axis=0)
        error_high, error_low = [part.astype(f32) for part in split(error)]
        pulled = jnp.concatenate(
            [error_high, error_low, error_high, jnp.zeros((7, 256), f32)], axis=0
        ).astype(bf16)
        tint = nn(pulled, high_ref[...])
        tint_low = nn(pulled, low_ref[...])
        tint_ref[pl.ds(pl.multiple_of(8 * view, 8), 3), :] = (
            tint[0:3] + tint[3:6] + tint_low[0:3]
        )
        pulled_ref[pl.ds(pl.multiple_of(16 * view, 16), 16), :] = pulled
        stacked_ref[pl.ds(pl.multiple_of(16 * view, 16), 16), :] = stacked
        return carry

    lax.fori_loop(0, VIEWS, one_view, 0)


def back_kernel(
    shade_ref,
    keep_ref,
    pulled_ref,
    stacked_ref,
    entry_ref,
    camera_ref,
    grads_ref,
    logs_ref,
    high_ref,
    low_ref,
    moment_ref,
    tri_ref,
):
    before = iota((256, 256), 0)
    after = iota((256, 256), 1)
    strictly = jnp.where(before > after, 1.0, 0.0).astype(bf16)
    tri_ref[0:256, :] = strictly
    tri_ref[256:512, :] = strictly
    pixel = iota((16, 256), 1)
    power = iota((16, 256), 0)
    pixel_u = (pixel % 16).astype(f32) - 7.5
    pixel_v = (pixel // 16).astype(f32) - 7.5
    basis = jnp.where(power == 0, 1.0, jnp.where(power == 1, pixel_u, pixel_v))
    basis = jnp.where(power == 3, pixel_u * pixel_u, basis)
    basis = jnp.where(power == 4, pixel_u * pixel_v, basis)
    basis = jnp.where(power == 5, pixel_v * pixel_v, basis)
    basis = jnp.where(power > 5, 0.0, basis).astype(bf16)

    def one_view(view, carry):
        base = pl.multiple_of(256 * view, 256)
        small = pl.ds(pl.multiple_of(16 * view, 16), 16)
        pull = tn(pulled_ref[small, :], stacked_ref[small, :])
        for part in range(4):
            rows = pl.ds(64 * part, 64)
            there = pl.ds(base + 64 * part, 64)
            weight = jnp.minimum(shade_ref[there, :], 0.99) * keep_ref[there, :]
            high, low = split(pull[64 * part : 64 * part + 64] * weight)
            logs_ref[rows, 0:256] = high
            logs_ref[rows, 256:512] = low
        for part in range(4):
            rows = pl.ds(64 * part, 64)
            there = pl.ds(base + 64 * part, 64)
            behind = nn(logs_ref[rows, :], tri_ref[...])
            shade = shade_ref[there, :]
            alpha = jnp.minimum(shade, 0.99)
            slope = pull[64 * part : 64 * part + 64] * keep_ref[there, :] - behind / (1.0 - alpha)
            passed = jnp.where(shade < 0.99, shade, jnp.where(shade == 0.99, 0.5 * shade, 0.0))
            high, low = split(slope * passed)
            high_ref[rows, :] = high
            low_ref[rows, :] = low
        moments = nn(basis, high_ref[...]) + nn(basis, low_ref[...])
        for half in range(2):
            moment_ref[pl.ds(2 * view + half, 8, stride=8), :] = moments[
                0:8, 128 * half : 128 * half + 128
            ]
        return carry

    lax.fori_loop(0, VIEWS, one_view, 0)

    kept = [entry_ref[pl.ds(8 * n, GROUPS), :] for n in range(KEPT)]
    shift_x, shift_y = kept[0:2]
    opacity, inverse_norm, qw, qx, qy, qz = kept[6:12]
    conic = kept[12:15]
    scale = kept[15:18]
    screen = (kept[18:21], kept[21:24])
    stretched = (kept[24:27], kept[27:30], kept[30:33])
    camera = [per_view([camera_ref[view, i] for view in range(VIEWS)]) for i in range(6)]
    affine = (camera[0:3], camera[3:6])
    m_0, m_u, m_v, m_uu, m_uv, m_vv = [
        moment_ref[pl.ds(8 * n, GROUPS), :] for n in range(6)
    ]
    m_x = m_u - shift_x * m_0
    m_y = m_v - shift_y * m_0
    m_xx = m_uu - 2.0 * shift_x * m_u + shift_x * shift_x * m_0
    m_xy = m_uv - shift_x * m_v - shift_y * m_u + shift_x * shift_y * m_0
    m_yy = m_vv - 2.0 * shift_y * m_v + shift_y * shift_y * m_0
    d_mean = (conic[0] * m_x + conic[1] * m_y, conic[1] * m_x + conic[2] * m_y)
    left = (
        (conic[0] * m_xx + conic[1] * m_xy, conic[0] * m_xy + conic[1] * m_yy),
        (conic[1] * m_xx + conic[2] * m_xy, conic[1] * m_xy + conic[2] * m_yy),
    )
    d_a = 0.5 * (left[0][0] * conic[0] + left[0][1] * conic[1])
    d_b = left[0][0] * conic[1] + left[0][1] * conic[2]
    d_c = 0.5 * (left[1][0] * conic[1] + left[1][1] * conic[2])
    d_screen = [
        [2.0 * d_a * screen[0][j] + d_b * screen[1][j] for j in range(3)],
        [2.0 * d_c * screen[1][j] + d_b * screen[0][j] for j in range(3)],
    ]
    d_stretched = [
        [affine[0][i] * d_screen[0][j] + affine[1][i] * d_screen[1][j] for j in range(3)]
        for i in range(3)
    ]
    d_scale = [sum(d_stretched[i][j] * stretched[i][j] for i in range(3)) for j in range(3)]
    r = [[d_stretched[i][j] * scale[j] for j in range(3)] for i in range(3)]
    d_unit = [
        2.0 * (qz * (r[1][0] - r[0][1]) + qy * (r[0][2] - r[2][0]) + qx * (r[2][1] - r[1][2])),
        2.0
        * (
            qy * (r[0][1] + r[1][0])
            + qz * (r[0][2] + r[2][0])
            + qw * (r[2][1] - r[1][2])
            - 2.0 * qx * (r[1][1] + r[2][2])
        ),
        2.0
        * (
            qx * (r[0][1] + r[1][0])
            + qz * (r[1][2] + r[2][1])
            + qw * (r[0][2] - r[2][0])
            - 2.0 * qy * (r[0][0] + r[2][2])
        ),
        2.0
        * (
            qx * (r[0][2] + r[2][0])
            + qy * (r[1][2] + r[2][1])
            + qw * (r[1][0] - r[0][1])
            - 2.0 * qz * (r[0][0] + r[1][1])
        ),
    ]
    unit = (qw, qx, qy, qz)
    radial = sum(unit[i] * d_unit[i] for i in range(4))
    gradients = (
        [affine[0][i] * d_mean[0] + affine[1][i] * d_mean[1] for i in range(3)]
        + d_scale
        + [(d_unit[i] - unit[i] * radial) * inverse_norm for i in range(4)]
        + [m_0 * (1.0 - opacity)]
    )
    for n, value in enumerate(gradients):
        high = value.astype(bf16).astype(f32)
        grads_ref[pl.ds(16 * n, GROUPS), :] = high
        grads_ref[pl.ds(16 * n + 8, GROUPS), :] = value - high


def scatter_kernel(
    lists_ref,
    grads_ref,
    tint_ref,
    loss_ref,
    core_ref,
    side_ref,
    across_ref,
    back_ref,
    spread_ref,
    places_ref,
):
    coarse = iota((32, 128), 0)
    fine = iota((256, 128), 0)
    kinds_of = GEOMETRY * 32
    for group in range(GROUPS):
        view, half = divmod(group, 2)
        local = lists_ref[view, :, 128 * half : 128 * half + 128] & 8191
        lanes = pl.ds(128 * group, 128)
        places_ref[:, lanes] = jnp.where((local & 255) == fine, 1.0, 0.0).astype(bf16)
        owner_part = ((local >> 8) & 1) * 16 + (local >> 9)
        chosen = jnp.where(owner_part == coarse, 1.0, 0.0).astype(bf16)
        for n in range(GEOMETRY):
            for part in range(2):
                value = grads_ref[pl.ds(16 * n + 8 * part + group, 1), :]
                spread_ref[pl.ds(kinds_of * part + 32 * n, 32), lanes] = (
                    chosen * jnp.broadcast_to(value, (32, 128)).astype(bf16)
                )
        for k in range(3):
            value = tint_ref[pl.ds(8 * view + k, 1), pl.ds(128 * half, 128)]
            high = value.astype(bf16).astype(f32)
            for part, piece in enumerate((high, value - high)):
                spread_ref[pl.ds(2 * kinds_of + 96 * part + 32 * k, 32), lanes] = (
                    chosen * jnp.broadcast_to(piece, (32, 128)).astype(bf16)
                )

    losses = (loss_ref[...] + core_ref[...]) + (side_ref[...] + across_ref[...])

    def store(row, value):
        for upper in range(2):
            for side in range(2):
                back_ref[pl.ds(4 * row + 2 * upper + side, 16, stride=BACK), :] = value[
                    16 * upper : 16 * upper + 16, 128 * side : 128 * side + 128
                ]

    dense = nt(spread_ref[0 : 2 * kinds_of, :], places_ref[...])
    for n in range(GEOMETRY):
        store(n, dense[32 * n : 32 * n + 32] + dense[kinds_of + 32 * n : kinds_of + 32 * n + 32])
    for view in range(VIEWS):
        lanes = slice(256 * view, 256 * view + 256)
        dense = nt(spread_ref[2 * kinds_of : 2 * kinds_of + 192, lanes], places_ref[:, lanes])
        for k in range(3):
            store(
                GEOMETRY + 3 * view + k,
                dense[32 * k : 32 * k + 32] + dense[96 + 32 * k : 96 + 32 * k + 32],
            )
    for owner in range(OWNERS):
        back_ref[pl.ds(BACK * owner + SEND, 8), :] = losses


def fold_kernel(back_ref, total_ref, loss_ref):
    total = back_ref[0:BACK, :]
    for owner in range(1, OWNERS):
        total = total + back_ref[pl.ds(BACK * owner, BACK), :]
    total_ref[...] = total[0:SEND]
    loss_ref[...] = total[SEND:BACK]


def adam_kernel(
    total_ref,
    slope_ref,
    params_ref,
    moment_one_ref,
    moment_two_ref,
    camera_ref,
    params_out,
    first_out,
    second_out,
    gradient_ref,
):
    columns = [harmonic_halves(camera_ref, view) for view in range(VIEWS)]
    row = iota((59, 128), 0)
    rates = jnp.where(row < 14, 0.0025, 0.000125)
    rates = jnp.where(row < 11, 0.05, rates)
    rates = jnp.where(row < 10, 0.001, rates)
    rates = jnp.where(row < 6, 0.005, rates)
    rates = jnp.where(row < 3, 0.00016, rates)
    for quarter in range(4):
        lanes = pl.ds(128 * quarter, 128)
        base = 64 * quarter
        gradient_ref[pl.ds(base, 8), :] = total_ref[pl.ds(quarter, 8, stride=4), :]
        gradient_ref[pl.ds(base + 8, 3), :] = total_ref[pl.ds(32 + quarter, 3, stride=4), :]
        for k in range(3):
            tints = []
            for view in range(VIEWS):
                row = 4 * (3 * view + k) + quarter
                tint = total_ref[pl.ds(4 * GEOMETRY + row, 1), :] * slope_ref[pl.ds(row, 1), :]
                tints.append(jnp.broadcast_to(tint, (8, 128)))
            for half in range(2):
                gradient_ref[pl.ds(base + 11 + 24 * half + k, 8, stride=3), :] = sum(
                    columns[view][half] * tints[view] for view in range(VIEWS)
                )
        gradient = gradient_ref[pl.ds(base, 59), :]
        first = 0.9 * moment_one_ref[:, lanes] + 0.1 * gradient
        second = 0.999 * moment_two_ref[:, lanes] + 0.001 * gradient * gradient
        first_out[:, lanes] = first
        second_out[:, lanes] = second
        params_out[:, lanes] = params_ref[:, lanes] - rates * first / (jnp.sqrt(second) + 1e-15)


VM = pl.BlockSpec(memory_space=pltpu.VMEM)
SM = pl.BlockSpec(memory_space=pltpu.SMEM)


def shape(*dims):
    return jax.ShapeDtypeStruct(dims, f32)


def swapped(value, partner):
    return lax.ppermute(value, GAUSS, [(i, partner(i)) for i in range(8)])


def limit(mib):
    return pltpu.CompilerParams(vmem_limit_bytes=mib << 20)


def shards(params, moment_one, moment_two, camera, target, tile_ids, splat_lists, counts):
    sent, slope = pl.pallas_call(
        pack_kernel,
        out_shape=(shape(OWNERS * SEND, 128), shape(36, 128)),
        in_specs=[VM, SM],
        out_specs=(VM, VM),
        scratch_shapes=[pltpu.VMEM((SEND, 128), f32), pltpu.VMEM((256, 128), f32)],
        name="pack",
    )(params, camera)
    table = lax.all_to_all(
        sent.reshape(OWNERS, SEND, 128), TILE, split_axis=0, concat_axis=0, tiled=True
    ).reshape(OWNERS * SEND, 128)
    half = jax.ShapeDtypeStruct((48, 256), bf16)
    rendered, loss, shade, keep, pulled, stacked, tint, entries = pl.pallas_call(
        front_kernel,
        out_shape=(
            shape(VIEWS, 3, 1, 256),
            shape(8, 128),
            shape(VIEWS * 256, 256),
            shape(VIEWS * 256, 256),
            half,
            half,
            shape(24, 256),
            shape(8 * KEPT, 128),
        ),
        in_specs=[VM, VM, SM, SM, SM, VM],
        out_specs=(VM,) * 8,
        scratch_shapes=[
            pltpu.VMEM((GROUPS * SEND, 128), f32),
            pltpu.VMEM((48, 256), f32),
            pltpu.VMEM((24, 256), f32),
            pltpu.VMEM((256, 512), bf16),
            pltpu.VMEM((256, 256), bf16),
            pltpu.VMEM((256, 256), bf16),
            pltpu.VMEM((512, 256), bf16),
        ],
        compiler_params=limit(16),
        name="front",
    )(table, splat_lists, counts, tile_ids, camera, target)
    core = swapped(loss, lambda i: i ^ 1)
    side = swapped(loss, lambda i: i ^ 2)
    across = swapped(loss, lambda i: i ^ 3)
    grads = pl.pallas_call(
        back_kernel,
        out_shape=shape(16 * GEOMETRY, 128),
        in_specs=[VM, VM, VM, VM, VM, SM],
        out_specs=VM,
        scratch_shapes=[
            pltpu.VMEM((256, 512), bf16),
            pltpu.VMEM((256, 256), bf16),
            pltpu.VMEM((256, 256), bf16),
            pltpu.VMEM((64, 128), f32),
            pltpu.VMEM((512, 256), bf16),
        ],
        compiler_params=limit(12),
        cost_estimate=pl.CostEstimate(
            flops=1 << 31, bytes_accessed=1 << 23, transcendentals=1 << 20
        ),
        name="back",
    )(shade, keep, pulled, stacked, entries, camera)
    back = pl.pallas_call(
        scatter_kernel,
        out_shape=shape(OWNERS * BACK, 128),
        in_specs=[VM] * 7,
        out_specs=VM,
        scratch_shapes=[
            pltpu.VMEM((2 * 32 * GEOMETRY + 192, 768), bf16),
            pltpu.VMEM((256, 768), bf16),
        ],
        compiler_params=limit(12),
        name="scatter",
    )(splat_lists, grads, tint, loss, core, side, across)
    arrived = lax.all_to_all(
        back.reshape(OWNERS, BACK, 128), TILE, split_axis=0, concat_axis=0, tiled=True
    ).reshape(OWNERS * BACK, 128)
    total, loss = pl.pallas_call(
        fold_kernel,
        out_shape=(shape(SEND, 128), shape(8, 128)),
        in_specs=[VM],
        out_specs=(VM, VM),
        compiler_params=limit(4),
        name="fold",
    )(arrived)
    other = swapped(loss, lambda i: 6 - (i & 6) + (i & 1))
    updated, first, second = pl.pallas_call(
        adam_kernel,
        out_shape=(shape(59, 512), shape(59, 512), shape(59, 512)),
        in_specs=[VM, VM, VM, VM, VM, SM],
        out_specs=(VM, VM, VM),
        scratch_shapes=[pltpu.VMEM((256, 128), f32)],
        compiler_params=limit(4),
        cost_estimate=pl.CostEstimate(
            flops=1 << 30, bytes_accessed=1 << 22, transcendentals=1 << 16
        ),
        name="adam",
    )(total, slope, params, moment_one, moment_two, camera)
    losses = (loss + other)[0, :VIEWS] * (0.5 / (3 * 256 * 128))
    return (updated, first, second, rendered, losses)


def solution(mesh):
    finer = Mesh(mesh.devices.reshape(4, 2, 4, 4), GAUSS_TILE)
    in_specs = (
        P(None, GAUSS_TILE),
        P(None, GAUSS_TILE),
        P(None, GAUSS_TILE),
        P(),
        P(None, None, GAUSS_TILE, None),
        P(None, GAUSS_TILE),
        P(None, GAUSS_TILE, None),
        P(None, GAUSS_TILE),
    )
    out_specs = (
        P(None, GAUSS_TILE),
        P(None, GAUSS_TILE),
        P(None, GAUSS_TILE),
        P(None, None, GAUSS_TILE, None),
        P(),
    )
    return jax.shard_map(
        shards, mesh=finer, in_specs=in_specs, out_specs=out_specs, check_vma=False
    )
```

```python
import jax
import jax.numpy as jnp
from jax import lax
from jax.experimental import pallas as pl
from jax.experimental.pallas import tpu as pltpu
from jax.sharding import Mesh
from jax.sharding import PartitionSpec as P

VIEWS = 3
TILES_WIDE = 4
TILE = ("tile_0", "tile_1")
GAUSS = ("gauss_0", "gauss_1")
GAUSS_TILE = ("gauss_0", "gauss_1", "tile_0", "tile_1")
OWNERS = 16
OWN = 512
GEOMETRY = 10
COLOURS = 4 * GEOMETRY
ERRORS = COLOURS + 36
SEND = ERRORS + 4
GROUPS = 6
KEPT = 32
LOG2E = 1.4426950408889634

band_zero = 0.28209479177387814
band_one = 0.4886025119029199
band_two = (
    1.0925484305920792,
    -1.0925484305920792,
    0.31539156525252005,
    -1.0925484305920792,
    0.5462742152960396,
)
band_three = (
    -0.5900435899266435,
    2.890611442640554,
    -0.4570457994644658,
    0.3731763325901154,
    -0.4570457994644658,
    1.445305721320277,
    -0.5900435899266435,
)

f32 = jnp.float32
bf16 = jnp.bfloat16


def iota(shape, dim):
    return lax.broadcasted_iota(jnp.int32, shape, dim)


def harmonic_halves(camera_ref, view):
    x, y, z = [jnp.full((8, 128), camera_ref[view, 8 + i], f32) for i in range(3)]
    xx, yy, zz = x * x, y * y, z * z
    values = [
        jnp.full((8, 128), band_zero, f32),
        -band_one * y,
        band_one * z,
        -band_one * x,
        band_two[0] * x * y,
        band_two[1] * y * z,
        band_two[2] * (2.0 * zz - xx - yy),
        band_two[3] * x * z,
        band_two[4] * (xx - yy),
        band_three[0] * y * (3.0 * xx - yy),
        band_three[1] * x * y * z,
        band_three[2] * y * (4.0 * zz - xx - yy),
        band_three[3] * z * (2.0 * zz - 3.0 * xx - 3.0 * yy),
        band_three[4] * x * (4.0 * zz - xx - yy),
        band_three[5] * z * (xx - yy),
        band_three[6] * x * (xx - 3.0 * yy),
    ]
    row = iota((8, 128), 0)
    halves = []
    for half in range(2):
        column = values[8 * half]
        for i in range(1, 8):
            column = jnp.where(row == i, values[8 * half + i], column)
        halves.append(column)
    return halves


def per_view(values):
    place = iota((GROUPS, 128), 0)
    return jnp.where(place < 2, values[0], jnp.where(place < 4, values[1], values[2]))


def pack_kernel(
    params_hbm, camera_hbm, send_ref, slope_ref, params_ref, pack_ref, tall_ref, camera_ref, sems
):
    copies = [
        pltpu.make_async_copy(camera_hbm, camera_ref, sems.at[0]),
        pltpu.make_async_copy(params_hbm, params_ref, sems.at[1]),
    ]
    for copy in copies:
        copy.start()
    copies[0].wait()
    columns = [harmonic_halves(camera_ref, view) for view in range(VIEWS)]
    copies[1].wait()
    for quarter in range(4):
        lanes = pl.ds(128 * quarter, 128)
        pack_ref[pl.ds(quarter, 6, stride=4), :] = params_ref[0:6, lanes]
        pack_ref[pl.ds(24 + quarter, 3, stride=4), :] = (
            params_ref[7:10, lanes] / params_ref[6:7, lanes]
        )
        pack_ref[pl.ds(36 + quarter, 1), :] = params_ref[10:11, lanes]
        tall_ref[pl.ds(64 * quarter, 59), :] = params_ref[:, lanes]
    for k in range(3):
        for quarter in range(4):
            low = tall_ref[pl.ds(64 * quarter + 11 + k, 8, stride=3), :]
            high = tall_ref[pl.ds(64 * quarter + 35 + k, 8, stride=3), :]
            for view in range(VIEWS):
                terms = columns[view][0] * low + columns[view][1] * high
                raw = jnp.sum(terms, axis=0, keepdims=True) + 0.5
                row = 4 * (3 * view + k) + quarter
                pack_ref[pl.ds(COLOURS + row, 1), :] = jnp.maximum(raw, 0.0)
                slope_ref[pl.ds(row, 1), :] = jnp.where(
                    raw > 0.0, 1.0, jnp.where(raw == 0.0, 0.5, 0.0)
                )
    pack_ref[pl.ds(ERRORS, 4), :] = jnp.zeros((4, 128), f32)
    packed = pack_ref[...]
    for owner in range(OWNERS):
        send_ref[pl.ds(SEND * owner, SEND), :] = packed


def prepare_kernel(
    lists_ref,
    counts_ref,
    tiles_ref,
    camera_ref,
    lane_ref,
    block_ref,
    cast_ref,
    column_ref,
    places_ref,
    chosen_ref,
    before_ref,
    behind_ref,
    basis_ref,
):
    quarter = iota((8, 128), 0) & 3
    fine = iota((256, 128), 0)
    coarse = iota((32, 128), 0)
    for group in range(GROUPS):
        view, half = divmod(group, 2)
        local = lists_ref[view, :, 128 * half : 128 * half + 128] & 8191
        spread = jnp.broadcast_to(local, (8, 128))
        lane_ref[pl.ds(8 * group, 8), :] = spread & 127
        block_ref[pl.ds(8 * group, 8), :] = (spread >> 7) - quarter
        lanes = pl.ds(128 * group, 128)
        places_ref[:, lanes] = jnp.where((local & 255) == fine, 1.0, 0.0).astype(bf16)
        owner_part = ((local >> 8) & 1) * 16 + (local >> 9)
        chosen_ref[:, lanes] = jnp.where(owner_part == coarse, 1.0, 0.0).astype(bf16)
    for i in range(8):
        cast_ref[pl.ds(8 * i, GROUPS), :] = per_view(
            [camera_ref[view, i] for view in range(VIEWS)]
        )
    place = iota((GROUPS, 128), 0)
    position = (place & 1) * 128 + iota((GROUPS, 128), 1)
    live = position < per_view([counts_ref[view, 0] for view in range(VIEWS)])
    cast_ref[pl.ds(64, GROUPS), :] = jnp.where(live, 1.0, 0.0)
    tile = per_view([tiles_ref[view, 0] for view in range(VIEWS)])
    cast_ref[pl.ds(72, GROUPS), :] = (tile % TILES_WIDE * 16 + 8).astype(f32)
    cast_ref[pl.ds(80, GROUPS), :] = (tile // TILES_WIDE * 16 + 8).astype(f32)
    for view in range(VIEWS):
        for half, column in enumerate(harmonic_halves(camera_ref, view)):
            column_ref[pl.ds(16 * view + 8 * half, 8), :] = column
    first = iota((256, 256), 0)
    second = iota((256, 256), 1)
    for ref, strictly in ((before_ref, first < second), (behind_ref, first > second)):
        ones = jnp.where(strictly, 1.0, 0.0).astype(bf16)
        ref[0:256, :] = ones
        ref[256:512, :] = ones
    pixel = iota((16, 256), 1)
    power = iota((16, 256), 0)
    pixel_u = (pixel % 16).astype(f32) - 7.5
    pixel_v = (pixel // 16).astype(f32) - 7.5
    basis = jnp.where(power == 0, 1.0, jnp.where(power == 1, pixel_u, pixel_v))
    basis = jnp.where(power == 3, pixel_u * pixel_u, basis)
    basis = jnp.where(power == 4, pixel_u * pixel_v, basis)
    basis = jnp.where(power == 5, pixel_v * pixel_v, basis)
    basis_ref[...] = jnp.where(power > 5, 0.0, basis).astype(bf16)


def split(value):
    high = value.astype(bf16)
    return high, (value - high.astype(f32)).astype(bf16)


def nn(lhs, rhs):
    return lax.dot_general(lhs, rhs, (((1,), (0,)), ((), ())), preferred_element_type=f32)


def nt(lhs, rhs):
    return lax.dot_general(lhs, rhs, (((1,), (1,)), ((), ())), preferred_element_type=f32)


def tn(lhs, rhs):
    return lax.dot_general(lhs, rhs, (((0,), (0,)), ((), ())), preferred_element_type=f32)


def front_kernel(
    table_ref,
    lane_ref,
    block_ref,
    cast_ref,
    before_ref,
    target_ref,
    image_ref,
    loss_ref,
    shade_ref,
    keep_ref,
    pulled_ref,
    stacked_ref,
    tint_ref,
    entry_ref,
    found_ref,
    rows_ref,
    colour_ref,
    logs_ref,
    high_ref,
    low_ref,
):
    for group in range(GROUPS):
        view, half = divmod(group, 2)
        lane = lane_ref[pl.ds(8 * group, 8), :]
        block = block_ref[pl.ds(8 * group, 8), :]
        first = (COLOURS + 12 * view) // 8
        last = (COLOURS + 12 * view + 11) // 8
        pieces = list(range(5)) + list(range(first, last + 1))
        found = {piece: jnp.zeros((8, 128), f32) for piece in pieces}
        for owner in range(OWNERS):
            here = block == 4 * owner
            for piece in pieces:
                rows = table_ref[pl.ds(SEND * owner + 8 * piece, 8), :]
                picked = jnp.take_along_axis(rows, lane, axis=1, mode="promise_in_bounds")
                found[piece] = jnp.where(here, picked, found[piece])
        for piece in pieces:
            found_ref[pl.ds(SEND * group + 8 * piece, 8), :] = found[piece]

    def entry_row(row):
        parts = [found_ref[pl.ds(4 * row + q, GROUPS, stride=SEND), :] for q in range(4)]
        return (parts[0] + parts[1]) + (parts[2] + parts[3])

    for group in range(GROUPS):
        view, half = divmod(group, 2)
        for k in range(3):
            start = SEND * group + COLOURS + 4 * (3 * view + k)
            value = jnp.sum(found_ref[pl.ds(start, 4), :], axis=0, keepdims=True)
            colour_ref[pl.ds(8 * view + k, 1), pl.ds(128 * half, 128)] = value

    camera = [cast_ref[pl.ds(8 * i, GROUPS), :] for i in range(8)]
    affine = (camera[0:3], camera[3:6])
    centre = [entry_row(i) for i in range(3)]
    scale = [jnp.exp(entry_row(3 + i)) for i in range(3)]
    ratio = [entry_row(6 + i) for i in range(3)]
    logit = entry_row(9)
    inverse_norm = 1.0 / jnp.sqrt(
        1.0 + ratio[0] * ratio[0] + ratio[1] * ratio[1] + ratio[2] * ratio[2]
    )
    qw = inverse_norm
    qx, qy, qz = [component * inverse_norm for component in ratio]
    rotation = [
        [1.0 - 2.0 * (qy * qy + qz * qz), 2.0 * (qx * qy - qw * qz), 2.0 * (qx * qz + qw * qy)],
        [2.0 * (qx * qy + qw * qz), 1.0 - 2.0 * (qx * qx + qz * qz), 2.0 * (qy * qz - qw * qx)],
        [2.0 * (qx * qz - qw * qy), 2.0 * (qy * qz + qw * qx), 1.0 - 2.0 * (qx * qx + qy * qy)],
    ]
    stretched = [[rotation[i][j] * scale[j] for j in range(3)] for i in range(3)]
    screen = [
        [sum(affine[k][i] * stretched[i][j] for i in range(3)) for j in range(3)] for k in range(2)
    ]
    cov_a = sum(screen[0][j] * screen[0][j] for j in range(3)) + 0.3
    cov_b = sum(screen[0][j] * screen[1][j] for j in range(3))
    cov_c = sum(screen[1][j] * screen[1][j] for j in range(3)) + 0.3
    inverse_det = 1.0 / (cov_a * cov_c - cov_b * cov_b)
    live = cast_ref[pl.ds(64, GROUPS), :] > 0.5
    conic = [
        jnp.where(live, value * inverse_det, 0.0) for value in (cov_c, -cov_b, cov_a)
    ]
    mean = [sum(affine[k][i] * centre[i] for i in range(3)) + camera[6 + k] for k in range(2)]
    opacity = 1.0 / (1.0 + jnp.exp(-logit))
    shown = jnp.where(live, opacity, 0.0)
    shift_x = mean[0] - cast_ref[pl.ds(72, GROUPS), :]
    shift_y = mean[1] - cast_ref[pl.ds(80, GROUPS), :]
    kept = (
        [shift_x, shift_y]
        + [(-0.5 * LOG2E) * conic[0], (-LOG2E) * conic[1], (-0.5 * LOG2E) * conic[2]]
        + [shown, opacity, qw, qx, qy, qz]
        + conic
        + scale
        + screen[0]
        + screen[1]
        + stretched[0]
        + stretched[1]
        + stretched[2]
    )
    for n, value in enumerate(kept):
        entry_ref[pl.ds(8 * n, GROUPS), :] = value
    for n in range(6):
        for half in range(2):
            rows_ref[pl.ds(8 * n, VIEWS), pl.ds(128 * half, 128)] = entry_ref[
                pl.ds(8 * n + half, VIEWS, stride=2), :
            ]

    offset = iota((16, 256), 0).astype(f32) - 7.5
    losses = jnp.zeros((8, 128), f32)

    for view in range(VIEWS):

        def row(n, view=view):
            return rows_ref[pl.ds(8 * n + view, 1), :]

        mean_u, mean_v = row(0), row(1)
        opaque = jnp.broadcast_to(row(5), (16, 256))
        dx = offset - mean_u
        along = row(2) * dx * dx
        across = row(3) * dx
        upright = row(4)
        base = 256 * view
        for line in range(16):
            dy = (line - 7.5) - mean_v
            exponent = along + (upright * dy * dy + across * dy)
            shade = opaque * jnp.exp2(exponent)
            shade_ref[pl.ds(base + 16 * line, 16), :] = shade
            high, low = split(jnp.log(1.0 - jnp.minimum(shade, 0.99)))
            logs_ref[pl.ds(16 * line, 16), 0:256] = high
            logs_ref[pl.ds(16 * line, 16), 256:512] = low
        for part in range(4):
            rows = pl.ds(64 * part, 64)
            there = pl.ds(base + 64 * part, 64)
            keep = jnp.exp(nn(logs_ref[rows, :], before_ref[...]))
            keep_ref[there, :] = keep
            high, low = split(jnp.minimum(shade_ref[there, :], 0.99) * keep)
            high_ref[rows, :] = high
            low_ref[rows, :] = low
        colour = colour_ref[pl.ds(8 * view, 8), :]
        colour_high, colour_low = [part.astype(f32) for part in split(colour)]
        stacked = jnp.concatenate(
            [
                colour_high[0:3],
                colour_high[0:3],
                colour_low[0:3],
                jnp.zeros((7, 256), f32),
            ],
            axis=0,
        ).astype(bf16)
        image_high = nt(stacked, high_ref[...])
        image_low = nt(stacked, low_ref[...])
        image = image_high[0:3] + image_high[6:9] + image_low[0:3]
        residuals = []
        total = jnp.zeros((1, 256), f32)
        for k in range(3):
            image_ref[pl.ds(3 * view + k, 1), :] = image[k : k + 1]
            residual = image[k : k + 1] - target_ref[view, k, :, :]
            total = total + residual * residual
            residuals.append(residual * (1.0 / (VIEWS * 256)))
        losses = jnp.where(iota((8, 128), 1) == view, jnp.sum(total, axis=1, keepdims=True), losses)
        error = jnp.concatenate(residuals, axis=0)
        error_high, error_low = [part.astype(f32) for part in split(error)]
        pulled = jnp.concatenate(
            [error_high, error_low, error_high, jnp.zeros((7, 256), f32)], axis=0
        ).astype(bf16)
        tint = nn(pulled, high_ref[...])
        tint_low = nn(pulled, low_ref[...])
        tint_ref[pl.ds(8 * view, 3), :] = (
            tint[0:3] + tint[3:6] + tint_low[0:3]
        )
        pulled_ref[pl.ds(16 * view, 16), :] = pulled
        stacked_ref[pl.ds(16 * view, 16), :] = stacked
    loss_ref[...] = losses


def back_kernel(
    shade_ref,
    keep_ref,
    pulled_ref,
    stacked_ref,
    entry_ref,
    cast_ref,
    behind_ref,
    basis_ref,
    grads_ref,
    logs_ref,
    high_ref,
    low_ref,
    moment_ref,
):
    basis = basis_ref[...]

    for view in range(VIEWS):
        base = 256 * view
        small = pl.ds(16 * view, 16)
        pull = tn(pulled_ref[small, :], stacked_ref[small, :])
        for part in range(4):
            rows = pl.ds(64 * part, 64)
            there = pl.ds(base + 64 * part, 64)
            weight = jnp.minimum(shade_ref[there, :], 0.99) * keep_ref[there, :]
            high, low = split(pull[64 * part : 64 * part + 64] * weight)
            logs_ref[rows, 0:256] = high
            logs_ref[rows, 256:512] = low
        for part in range(4):
            rows = pl.ds(64 * part, 64)
            there = pl.ds(base + 64 * part, 64)
            behind = nn(logs_ref[rows, :], behind_ref[...])
            shade = shade_ref[there, :]
            alpha = jnp.minimum(shade, 0.99)
            slope = pull[64 * part : 64 * part + 64] * keep_ref[there, :] - behind / (1.0 - alpha)
            passed = jnp.where(shade < 0.99, shade, jnp.where(shade == 0.99, 0.5 * shade, 0.0))
            high, low = split(slope * passed)
            high_ref[rows, :] = high
            low_ref[rows, :] = low
        moments = nn(basis, high_ref[...]) + nn(basis, low_ref[...])
        for half in range(2):
            moment_ref[pl.ds(2 * view + half, 8, stride=8), :] = moments[
                0:8, 128 * half : 128 * half + 128
            ]

    kept = [entry_ref[pl.ds(8 * n, GROUPS), :] for n in range(KEPT)]
    shift_x, shift_y = kept[0:2]
    opacity, qw, qx, qy, qz = kept[6:11]
    conic = kept[11:14]
    scale = kept[14:17]
    screen = (kept[17:20], kept[20:23])
    stretched = (kept[23:26], kept[26:29], kept[29:32])
    camera = [cast_ref[pl.ds(8 * i, GROUPS), :] for i in range(6)]
    affine = (camera[0:3], camera[3:6])
    m_0, m_u, m_v, m_uu, m_uv, m_vv = [
        moment_ref[pl.ds(8 * n, GROUPS), :] for n in range(6)
    ]
    m_x = m_u - shift_x * m_0
    m_y = m_v - shift_y * m_0
    m_xx = m_uu - 2.0 * shift_x * m_u + shift_x * shift_x * m_0
    m_xy = m_uv - shift_x * m_v - shift_y * m_u + shift_x * shift_y * m_0
    m_yy = m_vv - 2.0 * shift_y * m_v + shift_y * shift_y * m_0
    d_mean = (conic[0] * m_x + conic[1] * m_y, conic[1] * m_x + conic[2] * m_y)
    left = (
        (conic[0] * m_xx + conic[1] * m_xy, conic[0] * m_xy + conic[1] * m_yy),
        (conic[1] * m_xx + conic[2] * m_xy, conic[1] * m_xy + conic[2] * m_yy),
    )
    d_a = 0.5 * (left[0][0] * conic[0] + left[0][1] * conic[1])
    d_b = left[0][0] * conic[1] + left[0][1] * conic[2]
    d_c = 0.5 * (left[1][0] * conic[1] + left[1][1] * conic[2])
    d_screen = [
        [2.0 * d_a * screen[0][j] + d_b * screen[1][j] for j in range(3)],
        [2.0 * d_c * screen[1][j] + d_b * screen[0][j] for j in range(3)],
    ]
    d_stretched = [
        [affine[0][i] * d_screen[0][j] + affine[1][i] * d_screen[1][j] for j in range(3)]
        for i in range(3)
    ]
    d_scale = [sum(d_stretched[i][j] * stretched[i][j] for i in range(3)) for j in range(3)]
    r = [[d_stretched[i][j] * scale[j] for j in range(3)] for i in range(3)]
    d_unit = [
        2.0 * (qz * (r[1][0] - r[0][1]) + qy * (r[0][2] - r[2][0]) + qx * (r[2][1] - r[1][2])),
        2.0
        * (
            qy * (r[0][1] + r[1][0])
            + qz * (r[0][2] + r[2][0])
            + qw * (r[2][1] - r[1][2])
            - 2.0 * qx * (r[1][1] + r[2][2])
        ),
        2.0
        * (
            qx * (r[0][1] + r[1][0])
            + qz * (r[1][2] + r[2][1])
            + qw * (r[0][2] - r[2][0])
            - 2.0 * qy * (r[0][0] + r[2][2])
        ),
        2.0
        * (
            qx * (r[0][2] + r[2][0])
            + qy * (r[1][2] + r[2][1])
            + qw * (r[1][0] - r[0][1])
            - 2.0 * qz * (r[0][0] + r[1][1])
        ),
    ]
    unit = (qw, qx, qy, qz)
    radial = sum(unit[i] * d_unit[i] for i in range(4))
    gradients = (
        [affine[0][i] * d_mean[0] + affine[1][i] * d_mean[1] for i in range(3)]
        + d_scale
        + [(d_unit[i] - unit[i] * radial) * qw for i in range(1, 4)]
        + [m_0 * (1.0 - opacity)]
    )
    for n, value in enumerate(gradients):
        high = value.astype(bf16).astype(f32)
        grads_ref[pl.ds(16 * n, GROUPS), :] = high
        grads_ref[pl.ds(16 * n + 8, GROUPS), :] = value - high


def scatter_kernel(
    places_ref,
    chosen_ref,
    grads_ref,
    tint_ref,
    loss_ref,
    core_ref,
    side_ref,
    across_ref,
    back_ref,
    spread_ref,
):
    kinds_of = GEOMETRY * 32
    for group in range(GROUPS):
        view, half = divmod(group, 2)
        lanes = pl.ds(128 * group, 128)
        chosen = chosen_ref[:, lanes]
        for n in range(GEOMETRY):
            for part in range(2):
                value = grads_ref[pl.ds(16 * n + 8 * part + group, 1), :]
                spread_ref[pl.ds(kinds_of * part + 32 * n, 32), lanes] = (
                    chosen * jnp.broadcast_to(value, (32, 128)).astype(bf16)
                )
        for k in range(3):
            value = tint_ref[pl.ds(8 * view + k, 1), pl.ds(128 * half, 128)]
            high = value.astype(bf16).astype(f32)
            for part, piece in enumerate((high, value - high)):
                spread_ref[pl.ds(2 * kinds_of + 96 * part + 32 * k, 32), lanes] = (
                    chosen * jnp.broadcast_to(piece, (32, 128)).astype(bf16)
                )

    losses = (loss_ref[...] + core_ref[...]) + (side_ref[...] + across_ref[...])

    def store(row, value):
        for upper in range(2):
            for side in range(2):
                back_ref[pl.ds(4 * row + 2 * upper + side, 16, stride=SEND), :] = value[
                    16 * upper : 16 * upper + 16, 128 * side : 128 * side + 128
                ]

    dense = nt(spread_ref[0 : 2 * kinds_of, :], places_ref[...])
    for n in range(GEOMETRY):
        store(n, dense[32 * n : 32 * n + 32] + dense[kinds_of + 32 * n : kinds_of + 32 * n + 32])
    for view in range(VIEWS):
        lanes = slice(256 * view, 256 * view + 256)
        dense = nt(spread_ref[2 * kinds_of : 2 * kinds_of + 192, lanes], places_ref[:, lanes])
        for k in range(3):
            store(
                GEOMETRY + 3 * view + k,
                dense[32 * k : 32 * k + 32] + dense[96 + 32 * k : 96 + 32 * k + 32],
            )
    for owner in range(OWNERS):
        back_ref[pl.ds(SEND * owner + ERRORS, 4), :] = losses[0:4]


def fold_kernel(back_ref, total_ref, loss_ref):
    total = back_ref[0:SEND, :]
    for owner in range(1, OWNERS):
        total = total + back_ref[pl.ds(SEND * owner, SEND), :]
    total_ref[...] = total
    loss_ref[...] = total[SEND - 8 : SEND]


def adam_kernel(
    total_ref,
    slope_ref,
    column_ref,
    image_ref,
    params_ref,
    moment_one_ref,
    moment_two_ref,
    params_hbm,
    first_hbm,
    second_hbm,
    rendered_hbm,
    gradient_ref,
    params_out,
    first_out,
    second_out,
    rendered_out,
    sems,
):
    for view in range(VIEWS):
        for k in range(3):
            rendered_out[view, k, :, :] = image_ref[pl.ds(3 * view + k, 1), :]
    copies = [pltpu.make_async_copy(rendered_out, rendered_hbm, sems.at[0])]
    copies[0].start()
    columns = [
        [column_ref[pl.ds(16 * view + 8 * half, 8), :] for half in range(2)]
        for view in range(VIEWS)
    ]
    row = iota((59, 128), 0)
    rates = jnp.where(row < 14, 0.0025, 0.000125)
    rates = jnp.where(row < 11, 0.05, rates)
    rates = jnp.where(row < 10, 0.001, rates)
    rates = jnp.where(row < 6, 0.005, rates)
    rates = jnp.where(row < 3, 0.00016, rates)
    for quarter in range(4):
        lanes = pl.ds(128 * quarter, 128)
        base = 64 * quarter
        gradient_ref[pl.ds(base, 6), :] = total_ref[pl.ds(quarter, 6, stride=4), :]
        w = params_ref[6:7, lanes]
        d_ratio = total_ref[pl.ds(24 + quarter, 3, stride=4), :] / w
        lean = jnp.sum(d_ratio * params_ref[7:10, lanes], axis=0, keepdims=True)
        gradient_ref[pl.ds(base + 6, 1), :] = -lean / w
        gradient_ref[pl.ds(base + 7, 3), :] = d_ratio
        gradient_ref[pl.ds(base + 10, 1), :] = total_ref[pl.ds(36 + quarter, 1), :]
        for k in range(3):
            tints = []
            for view in range(VIEWS):
                place = 4 * (3 * view + k) + quarter
                tint = total_ref[pl.ds(COLOURS + place, 1), :] * slope_ref[pl.ds(place, 1), :]
                tints.append(jnp.broadcast_to(tint, (8, 128)))
            for half in range(2):
                gradient_ref[pl.ds(base + 11 + 24 * half + k, 8, stride=3), :] = sum(
                    columns[view][half] * tints[view] for view in range(VIEWS)
                )
        gradient = gradient_ref[pl.ds(base, 59), :]
        first = 0.9 * moment_one_ref[:, lanes] + 0.1 * gradient
        second = 0.999 * moment_two_ref[:, lanes] + 0.001 * gradient * gradient
        first_out[:, lanes] = first
        second_out[:, lanes] = second
        params_out[:, lanes] = params_ref[:, lanes] - rates * first / (jnp.sqrt(second) + 1e-15)
        pairs = ((params_out, params_hbm), (first_out, first_hbm), (second_out, second_hbm))
        for n, (source, target) in enumerate(pairs):
            copy = pltpu.make_async_copy(
                source.at[:, lanes], target.at[:, lanes], sems.at[1 + 3 * quarter + n]
            )
            copy.start()
            copies.append(copy)
    for copy in copies:
        copy.wait()


VM = pl.BlockSpec(memory_space=pltpu.VMEM)
SM = pl.BlockSpec(memory_space=pltpu.SMEM)
HB = pl.BlockSpec(memory_space=pltpu.HBM)


def shape(*dims):
    return jax.ShapeDtypeStruct(dims, f32)


def swapped(value, partner):
    return lax.ppermute(value, GAUSS, [(i, partner(i)) for i in range(8)])


def in_hbm(array):
    return pltpu.with_memory_space_constraint(array, pltpu.HBM)


def limit(mib):
    return pltpu.CompilerParams(vmem_limit_bytes=mib << 20)


def shards(params, moment_one, moment_two, camera, target, tile_ids, splat_lists, counts):
    sent, slope = pl.pallas_call(
        pack_kernel,
        out_shape=(shape(OWNERS * SEND, 128), shape(36, 128)),
        in_specs=[HB, HB],
        out_specs=(VM, VM),
        scratch_shapes=[
            pltpu.VMEM((59, 512), f32),
            pltpu.VMEM((SEND, 128), f32),
            pltpu.VMEM((256, 128), f32),
            pltpu.SMEM((3, 11), f32),
            pltpu.SemaphoreType.DMA((2,)),
        ],
        compiler_params=limit(4),
        name="pack",
    )(in_hbm(params), in_hbm(camera))
    table = lax.all_to_all(
        sent.reshape(OWNERS, SEND, 128), TILE, split_axis=0, concat_axis=0, tiled=True
    ).reshape(OWNERS * SEND, 128)
    late = lax.optimization_barrier((slope, splat_lists, counts, tile_ids, camera))
    slope = late[0]
    lane, block, cast, column, places, chosen, before, behind, basis = pl.pallas_call(
        prepare_kernel,
        out_shape=(
            jax.ShapeDtypeStruct((48, 128), jnp.int32),
            jax.ShapeDtypeStruct((48, 128), jnp.int32),
            shape(88, 128),
            shape(48, 128),
            jax.ShapeDtypeStruct((256, 768), bf16),
            jax.ShapeDtypeStruct((32, 768), bf16),
            jax.ShapeDtypeStruct((512, 256), bf16),
            jax.ShapeDtypeStruct((512, 256), bf16),
            jax.ShapeDtypeStruct((16, 256), bf16),
        ),
        in_specs=[VM, SM, SM, SM],
        out_specs=(VM,) * 9,
        compiler_params=limit(4),
        cost_estimate=pl.CostEstimate(flops=1 << 28, bytes_accessed=1 << 20, transcendentals=0),
        name="prepare",
    )(*late[1:])
    half = jax.ShapeDtypeStruct((48, 256), bf16)
    image, loss, shade, keep, pulled, stacked, tint, entries = pl.pallas_call(
        front_kernel,
        out_shape=(
            shape(16, 256),
            shape(8, 128),
            shape(VIEWS * 256, 256),
            shape(VIEWS * 256, 256),
            half,
            half,
            shape(24, 256),
            shape(8 * KEPT, 128),
        ),
        in_specs=[VM] * 6,
        out_specs=(VM,) * 8,
        scratch_shapes=[
            pltpu.VMEM((GROUPS * SEND, 128), f32),
            pltpu.VMEM((48, 256), f32),
            pltpu.VMEM((24, 256), f32),
            pltpu.VMEM((256, 512), bf16),
            pltpu.VMEM((256, 256), bf16),
            pltpu.VMEM((256, 256), bf16),
        ],
        compiler_params=limit(16),
        name="front",
    )(table, lane, block, cast, before, target)
    core = swapped(loss, lambda i: i ^ 1)
    side = swapped(loss, lambda i: i ^ 2)
    across = swapped(loss, lambda i: i ^ 3)
    grads = pl.pallas_call(
        back_kernel,
        out_shape=shape(16 * GEOMETRY, 128),
        in_specs=[VM] * 8,
        out_specs=VM,
        scratch_shapes=[
            pltpu.VMEM((256, 512), bf16),
            pltpu.VMEM((256, 256), bf16),
            pltpu.VMEM((256, 256), bf16),
            pltpu.VMEM((64, 128), f32),
        ],
        compiler_params=limit(12),
        cost_estimate=pl.CostEstimate(
            flops=1 << 31, bytes_accessed=1 << 23, transcendentals=1 << 20
        ),
        name="back",
    )(shade, keep, pulled, stacked, entries, cast, behind, basis)
    back = pl.pallas_call(
        scatter_kernel,
        out_shape=shape(OWNERS * SEND, 128),
        in_specs=[VM] * 8,
        out_specs=VM,
        scratch_shapes=[pltpu.VMEM((2 * 32 * GEOMETRY + 192, 768), bf16)],
        compiler_params=limit(12),
        name="scatter",
    )(places, chosen, grads, tint, loss, core, side, across)
    arrived = lax.all_to_all(
        back.reshape(OWNERS, SEND, 128), TILE, split_axis=0, concat_axis=0, tiled=True
    ).reshape(OWNERS * SEND, 128)
    total, loss = pl.pallas_call(
        fold_kernel,
        out_shape=(shape(SEND, 128), shape(8, 128)),
        in_specs=[VM],
        out_specs=(VM, VM),
        compiler_params=limit(4),
        name="fold",
    )(arrived)
    other = swapped(loss, lambda i: 6 - (i & 6) + (i & 1))
    wide = shape(59, 512)
    updated, first, second, rendered = pl.pallas_call(
        adam_kernel,
        out_shape=(wide, wide, wide, shape(VIEWS, 3, 1, 256)),
        in_specs=[VM] * 7,
        out_specs=(HB,) * 4,
        scratch_shapes=[
            pltpu.VMEM((256, 128), f32),
            pltpu.VMEM((59, 512), f32),
            pltpu.VMEM((59, 512), f32),
            pltpu.VMEM((59, 512), f32),
            pltpu.VMEM((VIEWS, 3, 1, 256), f32),
            pltpu.SemaphoreType.DMA((13,)),
        ],
        compiler_params=limit(4),
        cost_estimate=pl.CostEstimate(
            flops=1 << 30, bytes_accessed=1 << 22, transcendentals=1 << 16
        ),
        name="adam",
    )(total, slope, column, image, params, moment_one, moment_two)
    losses = (loss + other)[4, :VIEWS] * (0.5 / (3 * 256 * 128))
    return (updated, first, second, rendered, losses)


def solution(mesh):
    finer = Mesh(mesh.devices.reshape(4, 2, 4, 4), GAUSS_TILE)
    in_specs = (
        P(None, GAUSS_TILE),
        P(None, GAUSS_TILE),
        P(None, GAUSS_TILE),
        P(),
        P(None, None, GAUSS_TILE, None),
        P(None, GAUSS_TILE),
        P(None, GAUSS_TILE, None),
        P(None, GAUSS_TILE),
    )
    out_specs = (
        P(None, GAUSS_TILE),
        P(None, GAUSS_TILE),
        P(None, GAUSS_TILE),
        P(None, None, GAUSS_TILE, None),
        P(),
    )
    return jax.shard_map(
        shards, mesh=finer, in_specs=in_specs, out_specs=out_specs, check_vma=False
    )
```

```python
import jax
import jax.numpy as jnp
from jax import lax
from jax.experimental import pallas as pl
from jax.experimental.pallas import tpu as pltpu
from jax.sharding import Mesh
from jax.sharding import PartitionSpec as P

VIEWS = 3
TILES_WIDE = 4
TILE = ("tile_0", "tile_1")
GAUSS = ("gauss_0", "gauss_1")
GAUSS_TILE = ("gauss_0", "gauss_1", "tile_0", "tile_1")
OWNERS = 16
OWN = 512
GEOMETRY = 10
COLOURS = 4 * GEOMETRY
ERRORS = COLOURS + 36
SEND = ERRORS + 4
GROUPS = 6
KEPT = 32
LOG2E = 1.4426950408889634

band_zero = 0.28209479177387814
band_one = 0.4886025119029199
band_two = (
    1.0925484305920792,
    -1.0925484305920792,
    0.31539156525252005,
    -1.0925484305920792,
    0.5462742152960396,
)
band_three = (
    -0.5900435899266435,
    2.890611442640554,
    -0.4570457994644658,
    0.3731763325901154,
    -0.4570457994644658,
    1.445305721320277,
    -0.5900435899266435,
)

f32 = jnp.float32
bf16 = jnp.bfloat16


def iota(shape, dim):
    return lax.broadcasted_iota(jnp.int32, shape, dim)


def harmonic_halves(camera_ref, view):
    x, y, z = [jnp.full((8, 128), camera_ref[view, 8 + i], f32) for i in range(3)]
    xx, yy, zz = x * x, y * y, z * z
    values = [
        jnp.full((8, 128), band_zero, f32),
        -band_one * y,
        band_one * z,
        -band_one * x,
        band_two[0] * x * y,
        band_two[1] * y * z,
        band_two[2] * (2.0 * zz - xx - yy),
        band_two[3] * x * z,
        band_two[4] * (xx - yy),
        band_three[0] * y * (3.0 * xx - yy),
        band_three[1] * x * y * z,
        band_three[2] * y * (4.0 * zz - xx - yy),
        band_three[3] * z * (2.0 * zz - 3.0 * xx - 3.0 * yy),
        band_three[4] * x * (4.0 * zz - xx - yy),
        band_three[5] * z * (xx - yy),
        band_three[6] * x * (xx - 3.0 * yy),
    ]
    row = iota((8, 128), 0)
    halves = []
    for half in range(2):
        column = values[8 * half]
        for i in range(1, 8):
            column = jnp.where(row == i, values[8 * half + i], column)
        halves.append(column)
    return halves


def per_view(values):
    place = iota((GROUPS, 128), 0)
    return jnp.where(place < 2, values[0], jnp.where(place < 4, values[1], values[2]))


def pack_kernel(
    params_hbm,
    camera_hbm,
    lists_hbm,
    counts_hbm,
    tiles_hbm,
    send_ref,
    slope_ref,
    lane_ref,
    block_ref,
    cast_ref,
    column_ref,
    places_ref,
    chosen_ref,
    before_ref,
    behind_ref,
    basis_ref,
    params_ref,
    pack_ref,
    tall_ref,
    camera_ref,
    lists_ref,
    counts_ref,
    tiles_ref,
    sems,
):
    sources = [camera_hbm, counts_hbm, tiles_hbm, lists_hbm]
    targets = [camera_ref, counts_ref, tiles_ref, lists_ref]
    for quarter in range(4):
        lanes = pl.ds(128 * quarter, 128)
        sources.append(params_hbm.at[:, lanes])
        targets.append(params_ref.at[:, lanes])
    copies = [
        pltpu.make_async_copy(source, target, sems.at[n])
        for n, (source, target) in enumerate(zip(sources, targets))
    ]
    for copy in copies:
        copy.start()

    first = iota((256, 256), 0)
    second = iota((256, 256), 1)
    for ref, strictly in ((before_ref, first < second), (behind_ref, first > second)):
        ones = jnp.where(strictly, 1.0, 0.0).astype(bf16)
        ref[0:256, :] = ones
        ref[256:512, :] = ones
    pixel = iota((16, 256), 1)
    power = iota((16, 256), 0)
    pixel_u = (pixel % 16).astype(f32) - 7.5
    pixel_v = (pixel // 16).astype(f32) - 7.5
    basis = jnp.where(power == 0, 1.0, jnp.where(power == 1, pixel_u, pixel_v))
    basis = jnp.where(power == 3, pixel_u * pixel_u, basis)
    basis = jnp.where(power == 4, pixel_u * pixel_v, basis)
    basis = jnp.where(power == 5, pixel_v * pixel_v, basis)
    basis_ref[...] = jnp.where(power > 5, 0.0, basis).astype(bf16)
    for copy in copies[0:4]:
        copy.wait()
    columns = [harmonic_halves(camera_ref, view) for view in range(VIEWS)]
    quarter = iota((8, 128), 0) & 3
    fine = iota((256, 128), 0)
    coarse = iota((32, 128), 0)
    for group in range(GROUPS):
        view, half = divmod(group, 2)
        local = lists_ref[view, :, 128 * half : 128 * half + 128] & 8191
        spread = jnp.broadcast_to(local, (8, 128))
        lane_ref[pl.ds(8 * group, 8), :] = spread & 127
        block_ref[pl.ds(8 * group, 8), :] = (spread >> 7) - quarter
        lanes = pl.ds(128 * group, 128)
        places_ref[:, lanes] = jnp.where((local & 255) == fine, 1.0, 0.0).astype(bf16)
        owner_part = ((local >> 8) & 1) * 16 + (local >> 9)
        chosen_ref[:, lanes] = jnp.where(owner_part == coarse, 1.0, 0.0).astype(bf16)
    for i in range(8):
        cast_ref[pl.ds(8 * i, GROUPS), :] = per_view(
            [camera_ref[view, i] for view in range(VIEWS)]
        )
    place = iota((GROUPS, 128), 0)
    position = (place & 1) * 128 + iota((GROUPS, 128), 1)
    live = position < per_view([counts_ref[0, view] for view in range(VIEWS)])
    cast_ref[pl.ds(64, GROUPS), :] = jnp.where(live, 1.0, 0.0)
    tile = per_view([tiles_ref[0, view] for view in range(VIEWS)])
    cast_ref[pl.ds(72, GROUPS), :] = (tile % TILES_WIDE * 16 + 8).astype(f32)
    cast_ref[pl.ds(80, GROUPS), :] = (tile // TILES_WIDE * 16 + 8).astype(f32)
    for view in range(VIEWS):
        for half in range(2):
            column_ref[pl.ds(16 * view + 8 * half, 8), :] = columns[view][half]
    for quarter in range(4):
        copies[4 + quarter].wait()
        lanes = pl.ds(128 * quarter, 128)
        pack_ref[pl.ds(quarter, 6, stride=4), :] = params_ref[0:6, lanes]
        pack_ref[pl.ds(24 + quarter, 3, stride=4), :] = (
            params_ref[7:10, lanes] / params_ref[6:7, lanes]
        )
        pack_ref[pl.ds(36 + quarter, 1), :] = params_ref[10:11, lanes]
        tall_ref[pl.ds(64 * quarter, 59), :] = params_ref[:, lanes]
    for k in range(3):
        for quarter in range(4):
            low = tall_ref[pl.ds(64 * quarter + 11 + k, 8, stride=3), :]
            high = tall_ref[pl.ds(64 * quarter + 35 + k, 8, stride=3), :]
            for view in range(VIEWS):
                terms = columns[view][0] * low + columns[view][1] * high
                raw = jnp.sum(terms, axis=0, keepdims=True) + 0.5
                row = 4 * (3 * view + k) + quarter
                pack_ref[pl.ds(COLOURS + row, 1), :] = jnp.maximum(raw, 0.0)
                slope_ref[pl.ds(row, 1), :] = jnp.where(
                    raw > 0.0, 1.0, jnp.where(raw == 0.0, 0.5, 0.0)
                )
    pack_ref[pl.ds(ERRORS, 4), :] = jnp.zeros((4, 128), f32)
    packed = pack_ref[...]
    for owner in range(OWNERS):
        send_ref[pl.ds(SEND * owner, SEND), :] = packed


def split(value):
    high = value.astype(bf16)
    return high, (value - high.astype(f32)).astype(bf16)


def nn(lhs, rhs):
    return lax.dot_general(lhs, rhs, (((1,), (0,)), ((), ())), preferred_element_type=f32)


def nt(lhs, rhs):
    return lax.dot_general(lhs, rhs, (((1,), (1,)), ((), ())), preferred_element_type=f32)


def tn(lhs, rhs):
    return lax.dot_general(lhs, rhs, (((0,), (0,)), ((), ())), preferred_element_type=f32)


def front_kernel(
    table_ref,
    lane_ref,
    block_ref,
    cast_ref,
    before_ref,
    target_hbm,
    image_ref,
    loss_ref,
    shade_ref,
    keep_ref,
    pulled_ref,
    stacked_ref,
    tint_ref,
    entry_ref,
    found_ref,
    rows_ref,
    colour_ref,
    logs_ref,
    high_ref,
    low_ref,
    target_ref,
    sem,
):
    goal = pltpu.make_async_copy(target_hbm, target_ref, sem.at[0])
    goal.start()
    for group in range(GROUPS):
        view, half = divmod(group, 2)
        lane = lane_ref[pl.ds(8 * group, 8), :]
        block = block_ref[pl.ds(8 * group, 8), :]
        first = (COLOURS + 12 * view) // 8
        last = (COLOURS + 12 * view + 11) // 8
        pieces = list(range(5)) + list(range(first, last + 1))
        found = {piece: jnp.zeros((8, 128), f32) for piece in pieces}
        for owner in range(OWNERS):
            here = block == 4 * owner
            for piece in pieces:
                rows = table_ref[pl.ds(SEND * owner + 8 * piece, 8), :]
                picked = jnp.take_along_axis(rows, lane, axis=1, mode="promise_in_bounds")
                found[piece] = jnp.where(here, picked, found[piece])
        for piece in pieces:
            found_ref[pl.ds(SEND * group + 8 * piece, 8), :] = found[piece]

    def entry_row(row):
        parts = [found_ref[pl.ds(4 * row + q, GROUPS, stride=SEND), :] for q in range(4)]
        return (parts[0] + parts[1]) + (parts[2] + parts[3])

    for group in range(GROUPS):
        view, half = divmod(group, 2)
        for k in range(3):
            start = SEND * group + COLOURS + 4 * (3 * view + k)
            value = jnp.sum(found_ref[pl.ds(start, 4), :], axis=0, keepdims=True)
            colour_ref[pl.ds(8 * view + k, 1), pl.ds(128 * half, 128)] = value

    camera = [cast_ref[pl.ds(8 * i, GROUPS), :] for i in range(8)]
    affine = (camera[0:3], camera[3:6])
    centre = [entry_row(i) for i in range(3)]
    scale = [jnp.exp(entry_row(3 + i)) for i in range(3)]
    ratio = [entry_row(6 + i) for i in range(3)]
    logit = entry_row(9)
    inverse_norm = 1.0 / jnp.sqrt(
        1.0 + ratio[0] * ratio[0] + ratio[1] * ratio[1] + ratio[2] * ratio[2]
    )
    qw = inverse_norm
    qx, qy, qz = [component * inverse_norm for component in ratio]
    rotation = [
        [1.0 - 2.0 * (qy * qy + qz * qz), 2.0 * (qx * qy - qw * qz), 2.0 * (qx * qz + qw * qy)],
        [2.0 * (qx * qy + qw * qz), 1.0 - 2.0 * (qx * qx + qz * qz), 2.0 * (qy * qz - qw * qx)],
        [2.0 * (qx * qz - qw * qy), 2.0 * (qy * qz + qw * qx), 1.0 - 2.0 * (qx * qx + qy * qy)],
    ]
    stretched = [[rotation[i][j] * scale[j] for j in range(3)] for i in range(3)]
    screen = [
        [sum(affine[k][i] * stretched[i][j] for i in range(3)) for j in range(3)] for k in range(2)
    ]
    cov_a = sum(screen[0][j] * screen[0][j] for j in range(3)) + 0.3
    cov_b = sum(screen[0][j] * screen[1][j] for j in range(3))
    cov_c = sum(screen[1][j] * screen[1][j] for j in range(3)) + 0.3
    inverse_det = 1.0 / (cov_a * cov_c - cov_b * cov_b)
    live = cast_ref[pl.ds(64, GROUPS), :] > 0.5
    conic = [
        jnp.where(live, value * inverse_det, 0.0) for value in (cov_c, -cov_b, cov_a)
    ]
    mean = [sum(affine[k][i] * centre[i] for i in range(3)) + camera[6 + k] for k in range(2)]
    opacity = 1.0 / (1.0 + jnp.exp(-logit))
    shown = jnp.where(live, opacity, 0.0)
    shift_x = mean[0] - cast_ref[pl.ds(72, GROUPS), :]
    shift_y = mean[1] - cast_ref[pl.ds(80, GROUPS), :]
    kept = (
        [shift_x, shift_y]
        + [(-0.5 * LOG2E) * conic[0], (-LOG2E) * conic[1], (-0.5 * LOG2E) * conic[2]]
        + [shown, opacity, qw, qx, qy, qz]
        + conic
        + scale
        + screen[0]
        + screen[1]
        + stretched[0]
        + stretched[1]
        + stretched[2]
    )
    for n, value in enumerate(kept):
        entry_ref[pl.ds(8 * n, GROUPS), :] = value
    for n in range(6):
        for half in range(2):
            rows_ref[pl.ds(8 * n, VIEWS), pl.ds(128 * half, 128)] = entry_ref[
                pl.ds(8 * n + half, VIEWS, stride=2), :
            ]

    goal.wait()
    offset = iota((16, 256), 0).astype(f32) - 7.5
    losses = jnp.zeros((8, 128), f32)

    for view in range(VIEWS):

        def row(n, view=view):
            return rows_ref[pl.ds(8 * n + view, 1), :]

        mean_u, mean_v = row(0), row(1)
        opaque = jnp.broadcast_to(row(5), (16, 256))
        dx = offset - mean_u
        along = row(2) * dx * dx
        across = row(3) * dx
        upright = row(4)
        base = 256 * view
        for line in range(16):
            dy = (line - 7.5) - mean_v
            exponent = along + (upright * dy * dy + across * dy)
            shade = opaque * jnp.exp2(exponent)
            shade_ref[pl.ds(base + 16 * line, 16), :] = shade
            high, low = split(jnp.log(1.0 - jnp.minimum(shade, 0.99)))
            logs_ref[pl.ds(16 * line, 16), 0:256] = high
            logs_ref[pl.ds(16 * line, 16), 256:512] = low
        for part in range(4):
            rows = pl.ds(64 * part, 64)
            there = pl.ds(base + 64 * part, 64)
            keep = jnp.exp(nn(logs_ref[rows, :], before_ref[...]))
            keep_ref[there, :] = keep
            high, low = split(jnp.minimum(shade_ref[there, :], 0.99) * keep)
            high_ref[rows, :] = high
            low_ref[rows, :] = low
        colour = colour_ref[pl.ds(8 * view, 8), :]
        colour_high, colour_low = [part.astype(f32) for part in split(colour)]
        stacked = jnp.concatenate(
            [
                colour_high[0:3],
                colour_high[0:3],
                colour_low[0:3],
                jnp.zeros((7, 256), f32),
            ],
            axis=0,
        ).astype(bf16)
        image_high = nt(stacked, high_ref[...])
        image_low = nt(stacked, low_ref[...])
        image = image_high[0:3] + image_high[6:9] + image_low[0:3]
        residuals = []
        total = jnp.zeros((1, 256), f32)
        for k in range(3):
            image_ref[pl.ds(3 * view + k, 1), :] = image[k : k + 1]
            residual = image[k : k + 1] - target_ref[view, k, :, :]
            total = total + residual * residual
            residuals.append(residual * (1.0 / (VIEWS * 256)))
        losses = jnp.where(iota((8, 128), 1) == view, jnp.sum(total, axis=1, keepdims=True), losses)
        error = jnp.concatenate(residuals, axis=0)
        error_high, error_low = [part.astype(f32) for part in split(error)]
        pulled = jnp.concatenate(
            [error_high, error_low, error_high, jnp.zeros((7, 256), f32)], axis=0
        ).astype(bf16)
        tint = nn(pulled, high_ref[...])
        tint_low = nn(pulled, low_ref[...])
        tint_ref[pl.ds(8 * view, 3), :] = (
            tint[0:3] + tint[3:6] + tint_low[0:3]
        )
        pulled_ref[pl.ds(16 * view, 16), :] = pulled
        stacked_ref[pl.ds(16 * view, 16), :] = stacked
    loss_ref[...] = losses


def back_kernel(
    shade_ref,
    keep_ref,
    pulled_ref,
    stacked_ref,
    entry_ref,
    cast_ref,
    behind_ref,
    basis_ref,
    moment_one_hbm,
    moment_two_hbm,
    grads_ref,
    moment_one_ref,
    moment_two_ref,
    logs_ref,
    high_ref,
    low_ref,
    moment_ref,
    sems,
):
    copies = [
        pltpu.make_async_copy(moment_one_hbm, moment_one_ref, sems.at[0]),
        pltpu.make_async_copy(moment_two_hbm, moment_two_ref, sems.at[1]),
    ]
    for copy in copies:
        copy.start()
    basis = basis_ref[...]

    for view in range(VIEWS):
        base = 256 * view
        small = pl.ds(16 * view, 16)
        pull = tn(pulled_ref[small, :], stacked_ref[small, :])
        for part in range(4):
            rows = pl.ds(64 * part, 64)
            there = pl.ds(base + 64 * part, 64)
            weight = jnp.minimum(shade_ref[there, :], 0.99) * keep_ref[there, :]
            high, low = split(pull[64 * part : 64 * part + 64] * weight)
            logs_ref[rows, 0:256] = high
            logs_ref[rows, 256:512] = low
        for part in range(4):
            rows = pl.ds(64 * part, 64)
            there = pl.ds(base + 64 * part, 64)
            behind = nn(logs_ref[rows, :], behind_ref[...])
            shade = shade_ref[there, :]
            alpha = jnp.minimum(shade, 0.99)
            slope = pull[64 * part : 64 * part + 64] * keep_ref[there, :] - behind / (1.0 - alpha)
            passed = jnp.where(shade < 0.99, shade, jnp.where(shade == 0.99, 0.5 * shade, 0.0))
            high, low = split(slope * passed)
            high_ref[rows, :] = high
            low_ref[rows, :] = low
        moments = nn(basis, high_ref[...]) + nn(basis, low_ref[...])
        for half in range(2):
            moment_ref[pl.ds(2 * view + half, 8, stride=8), :] = moments[
                0:8, 128 * half : 128 * half + 128
            ]

    kept = [entry_ref[pl.ds(8 * n, GROUPS), :] for n in range(KEPT)]
    shift_x, shift_y = kept[0:2]
    opacity, qw, qx, qy, qz = kept[6:11]
    conic = kept[11:14]
    scale = kept[14:17]
    screen = (kept[17:20], kept[20:23])
    stretched = (kept[23:26], kept[26:29], kept[29:32])
    camera = [cast_ref[pl.ds(8 * i, GROUPS), :] for i in range(6)]
    affine = (camera[0:3], camera[3:6])
    m_0, m_u, m_v, m_uu, m_uv, m_vv = [
        moment_ref[pl.ds(8 * n, GROUPS), :] for n in range(6)
    ]
    m_x = m_u - shift_x * m_0
    m_y = m_v - shift_y * m_0
    m_xx = m_uu - 2.0 * shift_x * m_u + shift_x * shift_x * m_0
    m_xy = m_uv - shift_x * m_v - shift_y * m_u + shift_x * shift_y * m_0
    m_yy = m_vv - 2.0 * shift_y * m_v + shift_y * shift_y * m_0
    d_mean = (conic[0] * m_x + conic[1] * m_y, conic[1] * m_x + conic[2] * m_y)
    left = (
        (conic[0] * m_xx + conic[1] * m_xy, conic[0] * m_xy + conic[1] * m_yy),
        (conic[1] * m_xx + conic[2] * m_xy, conic[1] * m_xy + conic[2] * m_yy),
    )
    d_a = 0.5 * (left[0][0] * conic[0] + left[0][1] * conic[1])
    d_b = left[0][0] * conic[1] + left[0][1] * conic[2]
    d_c = 0.5 * (left[1][0] * conic[1] + left[1][1] * conic[2])
    d_screen = [
        [2.0 * d_a * screen[0][j] + d_b * screen[1][j] for j in range(3)],
        [2.0 * d_c * screen[1][j] + d_b * screen[0][j] for j in range(3)],
    ]
    d_stretched = [
        [affine[0][i] * d_screen[0][j] + affine[1][i] * d_screen[1][j] for j in range(3)]
        for i in range(3)
    ]
    d_scale = [sum(d_stretched[i][j] * stretched[i][j] for i in range(3)) for j in range(3)]
    r = [[d_stretched[i][j] * scale[j] for j in range(3)] for i in range(3)]
    d_unit = [
        2.0 * (qz * (r[1][0] - r[0][1]) + qy * (r[0][2] - r[2][0]) + qx * (r[2][1] - r[1][2])),
        2.0
        * (
            qy * (r[0][1] + r[1][0])
            + qz * (r[0][2] + r[2][0])
            + qw * (r[2][1] - r[1][2])
            - 2.0 * qx * (r[1][1] + r[2][2])
        ),
        2.0
        * (
            qx * (r[0][1] + r[1][0])
            + qz * (r[1][2] + r[2][1])
            + qw * (r[0][2] - r[2][0])
            - 2.0 * qy * (r[0][0] + r[2][2])
        ),
        2.0
        * (
            qx * (r[0][2] + r[2][0])
            + qy * (r[1][2] + r[2][1])
            + qw * (r[1][0] - r[0][1])
            - 2.0 * qz * (r[0][0] + r[1][1])
        ),
    ]
    unit = (qw, qx, qy, qz)
    radial = sum(unit[i] * d_unit[i] for i in range(4))
    gradients = (
        [affine[0][i] * d_mean[0] + affine[1][i] * d_mean[1] for i in range(3)]
        + d_scale
        + [(d_unit[i] - unit[i] * radial) * qw for i in range(1, 4)]
        + [m_0 * (1.0 - opacity)]
    )
    for n, value in enumerate(gradients):
        high = value.astype(bf16).astype(f32)
        grads_ref[pl.ds(16 * n, GROUPS), :] = high
        grads_ref[pl.ds(16 * n + 8, GROUPS), :] = value - high
    for copy in copies:
        copy.wait()


def scatter_kernel(
    places_ref,
    chosen_ref,
    grads_ref,
    tint_ref,
    loss_ref,
    side_ref,
    far_ref,
    wrap_ref,
    back_ref,
    spread_ref,
):
    kinds_of = GEOMETRY * 32
    for group in range(GROUPS):
        view, half = divmod(group, 2)
        lanes = pl.ds(128 * group, 128)
        chosen = chosen_ref[:, lanes]
        for n in range(GEOMETRY):
            for part in range(2):
                value = grads_ref[pl.ds(16 * n + 8 * part + group, 1), :]
                spread_ref[pl.ds(kinds_of * part + 32 * n, 32), lanes] = (
                    chosen * jnp.broadcast_to(value, (32, 128)).astype(bf16)
                )
        for k in range(3):
            value = tint_ref[pl.ds(8 * view + k, 1), pl.ds(128 * half, 128)]
            high = value.astype(bf16).astype(f32)
            for part, piece in enumerate((high, value - high)):
                spread_ref[pl.ds(2 * kinds_of + 96 * part + 32 * k, 32), lanes] = (
                    chosen * jnp.broadcast_to(piece, (32, 128)).astype(bf16)
                )

    losses = (loss_ref[...] + side_ref[...]) + (far_ref[...] + wrap_ref[...])

    def store(row, value):
        for upper in range(2):
            for side in range(2):
                back_ref[pl.ds(4 * row + 2 * upper + side, 16, stride=SEND), :] = value[
                    16 * upper : 16 * upper + 16, 128 * side : 128 * side + 128
                ]

    dense = nt(spread_ref[0 : 2 * kinds_of, :], places_ref[...])
    for n in range(GEOMETRY):
        store(n, dense[32 * n : 32 * n + 32] + dense[kinds_of + 32 * n : kinds_of + 32 * n + 32])
    for view in range(VIEWS):
        lanes = slice(256 * view, 256 * view + 256)
        dense = nt(spread_ref[2 * kinds_of : 2 * kinds_of + 192, lanes], places_ref[:, lanes])
        for k in range(3):
            store(
                GEOMETRY + 3 * view + k,
                dense[32 * k : 32 * k + 32] + dense[96 + 32 * k : 96 + 32 * k + 32],
            )
    for owner in range(OWNERS):
        back_ref[pl.ds(SEND * owner + ERRORS, 4), :] = losses[0:4]


def fold_kernel(back_ref, total_ref, loss_ref):
    total = back_ref[0:SEND, :]
    for owner in range(1, OWNERS):
        total = total + back_ref[pl.ds(SEND * owner, SEND), :]
    total_ref[...] = total
    loss_ref[...] = total[SEND - 8 : SEND]


def adam_kernel(
    total_ref,
    slope_ref,
    column_ref,
    image_ref,
    params_ref,
    moment_one_ref,
    moment_two_ref,
    params_hbm,
    first_hbm,
    second_hbm,
    rendered_hbm,
    gradient_ref,
    params_out,
    first_out,
    second_out,
    rendered_out,
    sems,
):
    for view in range(VIEWS):
        for k in range(3):
            rendered_out[view, k, :, :] = image_ref[pl.ds(3 * view + k, 1), :]
    copies = [pltpu.make_async_copy(rendered_out, rendered_hbm, sems.at[0])]
    copies[0].start()
    columns = [
        [column_ref[pl.ds(16 * view + 8 * half, 8), :] for half in range(2)]
        for view in range(VIEWS)
    ]
    row = iota((59, 128), 0)
    rates = jnp.where(row < 14, 0.0025, 0.000125)
    rates = jnp.where(row < 11, 0.05, rates)
    rates = jnp.where(row < 10, 0.001, rates)
    rates = jnp.where(row < 6, 0.005, rates)
    rates = jnp.where(row < 3, 0.00016, rates)
    for quarter in range(4):
        lanes = pl.ds(128 * quarter, 128)
        base = 64 * quarter
        gradient_ref[pl.ds(base, 6), :] = total_ref[pl.ds(quarter, 6, stride=4), :]
        w = params_ref[6:7, lanes]
        d_ratio = total_ref[pl.ds(24 + quarter, 3, stride=4), :] / w
        lean = jnp.sum(d_ratio * params_ref[7:10, lanes], axis=0, keepdims=True)
        gradient_ref[pl.ds(base + 6, 1), :] = -lean / w
        gradient_ref[pl.ds(base + 7, 3), :] = d_ratio
        gradient_ref[pl.ds(base + 10, 1), :] = total_ref[pl.ds(36 + quarter, 1), :]
        for k in range(3):
            tints = []
            for view in range(VIEWS):
                place = 4 * (3 * view + k) + quarter
                tint = total_ref[pl.ds(COLOURS + place, 1), :] * slope_ref[pl.ds(place, 1), :]
                tints.append(jnp.broadcast_to(tint, (8, 128)))
            for half in range(2):
                gradient_ref[pl.ds(base + 11 + 24 * half + k, 8, stride=3), :] = sum(
                    columns[view][half] * tints[view] for view in range(VIEWS)
                )
        gradient = gradient_ref[pl.ds(base, 59), :]
        first = 0.9 * moment_one_ref[:, lanes] + 0.1 * gradient
        second = 0.999 * moment_two_ref[:, lanes] + 0.001 * gradient * gradient
        first_out[:, lanes] = first
        second_out[:, lanes] = second
        params_out[:, lanes] = params_ref[:, lanes] - rates * first / (jnp.sqrt(second) + 1e-15)
        pairs = ((params_out, params_hbm), (first_out, first_hbm), (second_out, second_hbm))
        for n, (source, target) in enumerate(pairs):
            copy = pltpu.make_async_copy(
                source.at[:, lanes], target.at[:, lanes], sems.at[1 + 3 * quarter + n]
            )
            copy.start()
            copies.append(copy)
    for copy in copies:
        copy.wait()


VM = pl.BlockSpec(memory_space=pltpu.VMEM)
SM = pl.BlockSpec(memory_space=pltpu.SMEM)
HB = pl.BlockSpec(memory_space=pltpu.HBM)


def shape(*dims):
    return jax.ShapeDtypeStruct(dims, f32)


def swapped(value, partner):
    return lax.ppermute(value, GAUSS, [(i, partner(i)) for i in range(8)])


def in_hbm(array):
    return pltpu.with_memory_space_constraint(array, pltpu.HBM)


def limit(mib):
    return pltpu.CompilerParams(vmem_limit_bytes=mib << 20)


def shards(params, moment_one, moment_two, camera, target, tile_ids, splat_lists, counts):
    wide = shape(59, 512)
    (
        sent,
        slope,
        lane,
        block,
        cast,
        column,
        places,
        chosen,
        before,
        behind,
        basis,
        params,
    ) = pl.pallas_call(
        pack_kernel,
        out_shape=(
            shape(OWNERS * SEND, 128),
            shape(36, 128),
            jax.ShapeDtypeStruct((48, 128), jnp.int32),
            jax.ShapeDtypeStruct((48, 128), jnp.int32),
            shape(88, 128),
            shape(48, 128),
            jax.ShapeDtypeStruct((256, 768), bf16),
            jax.ShapeDtypeStruct((32, 768), bf16),
            jax.ShapeDtypeStruct((512, 256), bf16),
            jax.ShapeDtypeStruct((512, 256), bf16),
            jax.ShapeDtypeStruct((16, 256), bf16),
            wide,
        ),
        in_specs=[HB] * 5,
        out_specs=(VM,) * 12,
        scratch_shapes=[
            pltpu.VMEM((SEND, 128), f32),
            pltpu.VMEM((256, 128), f32),
            pltpu.SMEM((3, 11), f32),
            pltpu.VMEM((VIEWS, 1, 256), jnp.int32),
            pltpu.SMEM((1, 3), jnp.int32),
            pltpu.SMEM((1, 3), jnp.int32),
            pltpu.SemaphoreType.DMA((8,)),
        ],
        compiler_params=limit(6),
        name="pack",
    )(
        in_hbm(params),
        in_hbm(camera),
        in_hbm(splat_lists),
        in_hbm(counts.reshape(1, VIEWS)),
        in_hbm(tile_ids.reshape(1, VIEWS)),
    )
    table = lax.all_to_all(
        sent.reshape(OWNERS, SEND, 128), TILE, split_axis=0, concat_axis=0, tiled=True
    ).reshape(OWNERS * SEND, 128)
    half = jax.ShapeDtypeStruct((48, 256), bf16)
    image, loss, shade, keep, pulled, stacked, tint, entries = pl.pallas_call(
        front_kernel,
        out_shape=(
            shape(16, 256),
            shape(8, 128),
            shape(VIEWS * 256, 256),
            shape(VIEWS * 256, 256),
            half,
            half,
            shape(24, 256),
            shape(8 * KEPT, 128),
        ),
        in_specs=[VM] * 5 + [HB],
        out_specs=(VM,) * 8,
        scratch_shapes=[
            pltpu.VMEM((GROUPS * SEND, 128), f32),
            pltpu.VMEM((48, 256), f32),
            pltpu.VMEM((24, 256), f32),
            pltpu.VMEM((256, 512), bf16),
            pltpu.VMEM((256, 256), bf16),
            pltpu.VMEM((256, 256), bf16),
            pltpu.VMEM((VIEWS, 3, 1, 256), f32),
            pltpu.SemaphoreType.DMA((1,)),
        ],
        compiler_params=limit(16),
        name="front",
    )(table, lane, block, cast, before, in_hbm(target))
    side = swapped(loss, lambda i: i ^ 2)
    far = swapped(loss, lambda i: i ^ 4)
    wrap = swapped(loss, lambda i: i ^ 6)
    grads, moment_one, moment_two = pl.pallas_call(
        back_kernel,
        out_shape=(shape(16 * GEOMETRY, 128), wide, wide),
        in_specs=[VM] * 8 + [HB] * 2,
        out_specs=(VM,) * 3,
        scratch_shapes=[
            pltpu.VMEM((256, 512), bf16),
            pltpu.VMEM((256, 256), bf16),
            pltpu.VMEM((256, 256), bf16),
            pltpu.VMEM((64, 128), f32),
            pltpu.SemaphoreType.DMA((2,)),
        ],
        compiler_params=limit(12),
        cost_estimate=pl.CostEstimate(
            flops=1 << 31, bytes_accessed=1 << 23, transcendentals=1 << 20
        ),
        name="back",
    )(
        shade,
        keep,
        pulled,
        stacked,
        entries,
        cast,
        behind,
        basis,
        in_hbm(moment_one),
        in_hbm(moment_two),
    )
    back = pl.pallas_call(
        scatter_kernel,
        out_shape=shape(OWNERS * SEND, 128),
        in_specs=[VM] * 8,
        out_specs=VM,
        scratch_shapes=[pltpu.VMEM((2 * 32 * GEOMETRY + 192, 768), bf16)],
        compiler_params=limit(12),
        name="scatter",
    )(places, chosen, grads, tint, loss, side, far, wrap)
    arrived = lax.all_to_all(
        back.reshape(OWNERS, SEND, 128), TILE, split_axis=0, concat_axis=0, tiled=True
    ).reshape(OWNERS * SEND, 128)
    total, loss = pl.pallas_call(
        fold_kernel,
        out_shape=(shape(SEND, 128), shape(8, 128)),
        in_specs=[VM],
        out_specs=(VM, VM),
        compiler_params=limit(4),
        name="fold",
    )(arrived)
    core = swapped(loss, lambda i: i ^ 1)
    updated, first, second, rendered = pl.pallas_call(
        adam_kernel,
        out_shape=(wide, wide, wide, shape(VIEWS, 3, 1, 256)),
        in_specs=[VM] * 7,
        out_specs=(HB,) * 4,
        scratch_shapes=[
            pltpu.VMEM((256, 128), f32),
            pltpu.VMEM((59, 512), f32),
            pltpu.VMEM((59, 512), f32),
            pltpu.VMEM((59, 512), f32),
            pltpu.VMEM((VIEWS, 3, 1, 256), f32),
            pltpu.SemaphoreType.DMA((13,)),
        ],
        compiler_params=limit(4),
        cost_estimate=pl.CostEstimate(
            flops=1 << 30, bytes_accessed=1 << 22, transcendentals=1 << 16
        ),
        name="adam",
    )(total, slope, column, image, params, moment_one, moment_two)
    losses = (loss + core)[4, :VIEWS] * (0.5 / (3 * 256 * 128))
    return (updated, first, second, rendered, losses)


def solution(mesh):
    finer = Mesh(mesh.devices.reshape(4, 2, 4, 4), GAUSS_TILE)
    in_specs = (
        P(None, GAUSS_TILE),
        P(None, GAUSS_TILE),
        P(None, GAUSS_TILE),
        P(),
        P(None, None, GAUSS_TILE, None),
        P(None, GAUSS_TILE),
        P(None, GAUSS_TILE, None),
        P(None, GAUSS_TILE),
    )
    out_specs = (
        P(None, GAUSS_TILE),
        P(None, GAUSS_TILE),
        P(None, GAUSS_TILE),
        P(None, None, GAUSS_TILE, None),
        P(),
    )
    return jax.shard_map(
        shards, mesh=finer, in_specs=in_specs, out_specs=out_specs, check_vma=False
    )
```

```python
import jax
import jax.numpy as jnp
from jax import lax
from jax.experimental import pallas as pl
from jax.experimental.pallas import tpu as pltpu
from jax.sharding import Mesh
from jax.sharding import PartitionSpec as P

VIEWS = 3
TILES_WIDE = 4
TILE = ("tile_0", "tile_1")
GAUSS = ("gauss_0", "gauss_1")
GAUSS_TILE = ("gauss_0", "gauss_1", "tile_0", "tile_1")
OWNERS = 16
OWN = 512
GEOMETRY = 10
COLOURS = 4 * GEOMETRY
ERRORS = COLOURS + 36
SEND = ERRORS + 4
GROUPS = 6
KEPT = 32
LOG2E = 1.4426950408889634

band_zero = 0.28209479177387814
band_one = 0.4886025119029199
band_two = (
    1.0925484305920792,
    -1.0925484305920792,
    0.31539156525252005,
    -1.0925484305920792,
    0.5462742152960396,
)
band_three = (
    -0.5900435899266435,
    2.890611442640554,
    -0.4570457994644658,
    0.3731763325901154,
    -0.4570457994644658,
    1.445305721320277,
    -0.5900435899266435,
)

f32 = jnp.float32
bf16 = jnp.bfloat16


def iota(shape, dim):
    return lax.broadcasted_iota(jnp.int32, shape, dim)


def harmonic_halves(camera_ref, view):
    x, y, z = [jnp.full((8, 128), camera_ref[view, 8 + i], f32) for i in range(3)]
    xx, yy, zz = x * x, y * y, z * z
    values = [
        jnp.full((8, 128), band_zero, f32),
        -band_one * y,
        band_one * z,
        -band_one * x,
        band_two[0] * x * y,
        band_two[1] * y * z,
        band_two[2] * (2.0 * zz - xx - yy),
        band_two[3] * x * z,
        band_two[4] * (xx - yy),
        band_three[0] * y * (3.0 * xx - yy),
        band_three[1] * x * y * z,
        band_three[2] * y * (4.0 * zz - xx - yy),
        band_three[3] * z * (2.0 * zz - 3.0 * xx - 3.0 * yy),
        band_three[4] * x * (4.0 * zz - xx - yy),
        band_three[5] * z * (xx - yy),
        band_three[6] * x * (xx - 3.0 * yy),
    ]
    row = iota((8, 128), 0)
    halves = []
    for half in range(2):
        column = values[8 * half]
        for i in range(1, 8):
            column = jnp.where(row == i, values[8 * half + i], column)
        halves.append(column)
    return halves


def per_view(values):
    place = iota((GROUPS, 128), 0)
    return jnp.where(place < 2, values[0], jnp.where(place < 4, values[1], values[2]))


def pack_kernel(
    params_hbm,
    camera_hbm,
    lists_hbm,
    counts_hbm,
    tiles_hbm,
    send_ref,
    slope_ref,
    lane_ref,
    block_ref,
    cast_ref,
    column_ref,
    places_ref,
    chosen_ref,
    before_ref,
    behind_ref,
    basis_ref,
    params_ref,
    pack_ref,
    tall_ref,
    camera_ref,
    lists_ref,
    counts_ref,
    tiles_ref,
    sems,
):
    sources = [camera_hbm, counts_hbm, tiles_hbm, lists_hbm]
    targets = [camera_ref, counts_ref, tiles_ref, lists_ref]
    for quarter in range(4):
        lanes = pl.ds(128 * quarter, 128)
        sources.append(params_hbm.at[:, lanes])
        targets.append(params_ref.at[:, lanes])
    copies = [
        pltpu.make_async_copy(source, target, sems.at[n])
        for n, (source, target) in enumerate(zip(sources, targets))
    ]
    for copy in copies:
        copy.start()

    first = iota((256, 256), 0)
    second = iota((256, 256), 1)
    for ref, strictly in ((before_ref, first < second), (behind_ref, first > second)):
        ones = jnp.where(strictly, 1.0, 0.0).astype(bf16)
        ref[0:256, :] = ones
        ref[256:512, :] = ones
    pixel = iota((16, 256), 1)
    power = iota((16, 256), 0)
    pixel_u = (pixel % 16).astype(f32) - 7.5
    pixel_v = (pixel // 16).astype(f32) - 7.5
    basis = jnp.where(power == 0, 1.0, jnp.where(power == 1, pixel_u, pixel_v))
    basis = jnp.where(power == 3, pixel_u * pixel_u, basis)
    basis = jnp.where(power == 4, pixel_u * pixel_v, basis)
    basis = jnp.where(power == 5, pixel_v * pixel_v, basis)
    basis_ref[...] = jnp.where(power > 5, 0.0, basis).astype(bf16)
    for copy in copies[0:4]:
        copy.wait()
    columns = [harmonic_halves(camera_ref, view) for view in range(VIEWS)]
    quarter = iota((8, 128), 0) & 3
    fine = iota((256, 128), 0)
    coarse = iota((32, 128), 0)
    for group in range(GROUPS):
        view, half = divmod(group, 2)
        local = lists_ref[view, :, 128 * half : 128 * half + 128] & 8191
        spread = jnp.broadcast_to(local, (8, 128))
        lane_ref[pl.ds(8 * group, 8), :] = spread & 127
        block_ref[pl.ds(8 * group, 8), :] = (spread >> 7) - quarter
        lanes = pl.ds(128 * group, 128)
        places_ref[:, lanes] = jnp.where((local & 255) == fine, 1.0, 0.0).astype(bf16)
        owner_part = ((local >> 8) & 1) * 16 + (local >> 9)
        chosen_ref[:, lanes] = jnp.where(owner_part == coarse, 1.0, 0.0).astype(bf16)
    for i in range(8):
        cast_ref[pl.ds(8 * i, GROUPS), :] = per_view(
            [camera_ref[view, i] for view in range(VIEWS)]
        )
    place = iota((GROUPS, 128), 0)
    position = (place & 1) * 128 + iota((GROUPS, 128), 1)
    live = position < per_view([counts_ref[0, view] for view in range(VIEWS)])
    cast_ref[pl.ds(64, GROUPS), :] = jnp.where(live, 1.0, 0.0)
    tile = per_view([tiles_ref[0, view] for view in range(VIEWS)])
    cast_ref[pl.ds(72, GROUPS), :] = (tile % TILES_WIDE * 16 + 8).astype(f32)
    cast_ref[pl.ds(80, GROUPS), :] = (tile // TILES_WIDE * 16 + 8).astype(f32)
    for view in range(VIEWS):
        for half in range(2):
            column_ref[pl.ds(16 * view + 8 * half, 8), :] = columns[view][half]
    for quarter in range(4):
        copies[4 + quarter].wait()
        lanes = pl.ds(128 * quarter, 128)
        pack_ref[pl.ds(quarter, 6, stride=4), :] = params_ref[0:6, lanes]
        pack_ref[pl.ds(24 + quarter, 3, stride=4), :] = (
            params_ref[7:10, lanes] / params_ref[6:7, lanes]
        )
        pack_ref[pl.ds(36 + quarter, 1), :] = params_ref[10:11, lanes]
        tall_ref[pl.ds(64 * quarter, 59), :] = params_ref[:, lanes]
    for k in range(3):
        for quarter in range(4):
            low = tall_ref[pl.ds(64 * quarter + 11 + k, 8, stride=3), :]
            high = tall_ref[pl.ds(64 * quarter + 35 + k, 8, stride=3), :]
            for view in range(VIEWS):
                terms = columns[view][0] * low + columns[view][1] * high
                raw = jnp.sum(terms, axis=0, keepdims=True) + 0.5
                row = 4 * (3 * view + k) + quarter
                pack_ref[pl.ds(COLOURS + row, 1), :] = jnp.maximum(raw, 0.0)
                slope_ref[pl.ds(row, 1), :] = jnp.where(
                    raw > 0.0, 1.0, jnp.where(raw == 0.0, 0.5, 0.0)
                )
    pack_ref[pl.ds(ERRORS, 4), :] = jnp.zeros((4, 128), f32)
    packed = pack_ref[...]
    for owner in range(OWNERS):
        send_ref[pl.ds(SEND * owner, SEND), :] = packed


def split(value):
    high = value.astype(bf16)
    return high, (value - high.astype(f32)).astype(bf16)


def nn(lhs, rhs):
    return lax.dot_general(lhs, rhs, (((1,), (0,)), ((), ())), preferred_element_type=f32)


def nt(lhs, rhs):
    return lax.dot_general(lhs, rhs, (((1,), (1,)), ((), ())), preferred_element_type=f32)


def tn(lhs, rhs):
    return lax.dot_general(lhs, rhs, (((0,), (0,)), ((), ())), preferred_element_type=f32)


def front_kernel(
    table_ref,
    lane_ref,
    block_ref,
    cast_ref,
    before_ref,
    target_hbm,
    image_ref,
    loss_ref,
    shade_ref,
    keep_ref,
    pulled_ref,
    stacked_ref,
    tint_ref,
    entry_ref,
    found_ref,
    rows_ref,
    colour_ref,
    logs_ref,
    high_ref,
    low_ref,
    target_ref,
    sem,
):
    goal = pltpu.make_async_copy(target_hbm, target_ref, sem.at[0])
    goal.start()
    for group in range(GROUPS):
        view, half = divmod(group, 2)
        lane = lane_ref[pl.ds(8 * group, 8), :]
        block = block_ref[pl.ds(8 * group, 8), :]
        first = (COLOURS + 12 * view) // 8
        last = (COLOURS + 12 * view + 11) // 8
        pieces = list(range(5)) + list(range(first, last + 1))
        found = {piece: jnp.zeros((8, 128), f32) for piece in pieces}
        for owner in range(OWNERS):
            here = block == 4 * owner
            for piece in pieces:
                rows = table_ref[pl.ds(SEND * owner + 8 * piece, 8), :]
                picked = jnp.take_along_axis(rows, lane, axis=1, mode="promise_in_bounds")
                found[piece] = jnp.where(here, picked, found[piece])
        for piece in pieces:
            found_ref[pl.ds(SEND * group + 8 * piece, 8), :] = found[piece]

    def entry_row(row):
        parts = [found_ref[pl.ds(4 * row + q, GROUPS, stride=SEND), :] for q in range(4)]
        return (parts[0] + parts[1]) + (parts[2] + parts[3])

    for group in range(GROUPS):
        view, half = divmod(group, 2)
        for k in range(3):
            start = SEND * group + COLOURS + 4 * (3 * view + k)
            value = jnp.sum(found_ref[pl.ds(start, 4), :], axis=0, keepdims=True)
            colour_ref[pl.ds(8 * view + k, 1), pl.ds(128 * half, 128)] = value

    camera = [cast_ref[pl.ds(8 * i, GROUPS), :] for i in range(8)]
    affine = (camera[0:3], camera[3:6])
    centre = [entry_row(i) for i in range(3)]
    scale = [jnp.exp(entry_row(3 + i)) for i in range(3)]
    ratio = [entry_row(6 + i) for i in range(3)]
    logit = entry_row(9)
    inverse_norm = 1.0 / jnp.sqrt(
        1.0 + ratio[0] * ratio[0] + ratio[1] * ratio[1] + ratio[2] * ratio[2]
    )
    qw = inverse_norm
    qx, qy, qz = [component * inverse_norm for component in ratio]
    rotation = [
        [1.0 - 2.0 * (qy * qy + qz * qz), 2.0 * (qx * qy - qw * qz), 2.0 * (qx * qz + qw * qy)],
        [2.0 * (qx * qy + qw * qz), 1.0 - 2.0 * (qx * qx + qz * qz), 2.0 * (qy * qz - qw * qx)],
        [2.0 * (qx * qz - qw * qy), 2.0 * (qy * qz + qw * qx), 1.0 - 2.0 * (qx * qx + qy * qy)],
    ]
    stretched = [[rotation[i][j] * scale[j] for j in range(3)] for i in range(3)]
    screen = [
        [sum(affine[k][i] * stretched[i][j] for i in range(3)) for j in range(3)] for k in range(2)
    ]
    cov_a = sum(screen[0][j] * screen[0][j] for j in range(3)) + 0.3
    cov_b = sum(screen[0][j] * screen[1][j] for j in range(3))
    cov_c = sum(screen[1][j] * screen[1][j] for j in range(3)) + 0.3
    inverse_det = 1.0 / (cov_a * cov_c - cov_b * cov_b)
    live = cast_ref[pl.ds(64, GROUPS), :] > 0.5
    conic = [
        jnp.where(live, value * inverse_det, 0.0) for value in (cov_c, -cov_b, cov_a)
    ]
    mean = [sum(affine[k][i] * centre[i] for i in range(3)) + camera[6 + k] for k in range(2)]
    opacity = 1.0 / (1.0 + jnp.exp(-logit))
    shown = jnp.where(live, opacity, 0.0)
    shift_x = mean[0] - cast_ref[pl.ds(72, GROUPS), :]
    shift_y = mean[1] - cast_ref[pl.ds(80, GROUPS), :]
    kept = (
        [shift_x, shift_y]
        + [(-0.5 * LOG2E) * conic[0], (-LOG2E) * conic[1], (-0.5 * LOG2E) * conic[2]]
        + [shown, opacity, qw, qx, qy, qz]
        + conic
        + scale
        + screen[0]
        + screen[1]
        + stretched[0]
        + stretched[1]
        + stretched[2]
    )
    for n, value in enumerate(kept):
        entry_ref[pl.ds(8 * n, GROUPS), :] = value
    for n in range(6):
        for half in range(2):
            rows_ref[pl.ds(8 * n, VIEWS), pl.ds(128 * half, 128)] = entry_ref[
                pl.ds(8 * n + half, VIEWS, stride=2), :
            ]

    goal.wait()
    offset = iota((16, 256), 0).astype(f32) - 7.5
    losses = jnp.zeros((8, 128), f32)

    for view in range(VIEWS):

        def row(n, view=view):
            return rows_ref[pl.ds(8 * n + view, 1), :]

        mean_u, mean_v = row(0), row(1)
        opaque = jnp.broadcast_to(row(5), (16, 256))
        dx = offset - mean_u
        along = row(2) * dx * dx
        across = row(3) * dx
        upright = row(4)
        base = 256 * view
        for line in range(16):
            dy = (line - 7.5) - mean_v
            exponent = along + (upright * dy * dy + across * dy)
            shade = opaque * jnp.exp2(exponent)
            shade_ref[pl.ds(base + 16 * line, 16), :] = shade
            high, low = split(jnp.log(1.0 - jnp.minimum(shade, 0.99)))
            logs_ref[pl.ds(16 * line, 16), 0:256] = high
            logs_ref[pl.ds(16 * line, 16), 256:512] = low
        for part in range(4):
            rows = pl.ds(64 * part, 64)
            there = pl.ds(base + 64 * part, 64)
            keep = jnp.exp(nn(logs_ref[rows, :], before_ref[...]))
            keep_ref[there, :] = keep
            high, low = split(jnp.minimum(shade_ref[there, :], 0.99) * keep)
            high_ref[rows, :] = high
            low_ref[rows, :] = low
        colour = colour_ref[pl.ds(8 * view, 8), :]
        colour_high, colour_low = [part.astype(f32) for part in split(colour)]
        stacked = jnp.concatenate(
            [
                colour_high[0:3],
                colour_high[0:3],
                colour_low[0:3],
                jnp.zeros((7, 256), f32),
            ],
            axis=0,
        ).astype(bf16)
        image_high = nt(stacked, high_ref[...])
        image_low = nt(stacked, low_ref[...])
        image = image_high[0:3] + image_high[6:9] + image_low[0:3]
        residuals = []
        total = jnp.zeros((1, 256), f32)
        for k in range(3):
            image_ref[pl.ds(3 * view + k, 1), :] = image[k : k + 1]
            residual = image[k : k + 1] - target_ref[view, k, :, :]
            total = total + residual * residual
            residuals.append(residual * (1.0 / (VIEWS * 256)))
        losses = jnp.where(iota((8, 128), 1) == view, jnp.sum(total, axis=1, keepdims=True), losses)
        error = jnp.concatenate(residuals, axis=0)
        error_high, error_low = [part.astype(f32) for part in split(error)]
        pulled = jnp.concatenate(
            [error_high, error_low, error_high, jnp.zeros((7, 256), f32)], axis=0
        ).astype(bf16)
        tint = nn(pulled, high_ref[...])
        tint_low = nn(pulled, low_ref[...])
        tint_ref[pl.ds(8 * view, 3), :] = (
            tint[0:3] + tint[3:6] + tint_low[0:3]
        )
        pulled_ref[pl.ds(16 * view, 16), :] = pulled
        stacked_ref[pl.ds(16 * view, 16), :] = stacked
    loss_ref[...] = losses


def back_kernel(
    shade_ref,
    keep_ref,
    pulled_ref,
    stacked_ref,
    entry_ref,
    cast_ref,
    behind_ref,
    basis_ref,
    moment_one_hbm,
    moment_two_hbm,
    grads_ref,
    moment_one_ref,
    moment_two_ref,
    logs_ref,
    high_ref,
    low_ref,
    moment_ref,
    sems,
):
    copies = [
        pltpu.make_async_copy(moment_one_hbm, moment_one_ref, sems.at[0]),
        pltpu.make_async_copy(moment_two_hbm, moment_two_ref, sems.at[1]),
    ]
    for copy in copies:
        copy.start()
    basis = basis_ref[...]

    for view in range(VIEWS):
        base = 256 * view
        small = pl.ds(16 * view, 16)
        pull = tn(pulled_ref[small, :], stacked_ref[small, :])
        for part in range(4):
            rows = pl.ds(64 * part, 64)
            there = pl.ds(base + 64 * part, 64)
            weight = jnp.minimum(shade_ref[there, :], 0.99) * keep_ref[there, :]
            high, low = split(pull[64 * part : 64 * part + 64] * weight)
            logs_ref[rows, 0:256] = high
            logs_ref[rows, 256:512] = low
        for part in range(4):
            rows = pl.ds(64 * part, 64)
            there = pl.ds(base + 64 * part, 64)
            behind = nn(logs_ref[rows, :], behind_ref[...])
            shade = shade_ref[there, :]
            alpha = jnp.minimum(shade, 0.99)
            slope = pull[64 * part : 64 * part + 64] * keep_ref[there, :] - behind / (1.0 - alpha)
            passed = jnp.where(shade < 0.99, shade, jnp.where(shade == 0.99, 0.5 * shade, 0.0))
            high, low = split(slope * passed)
            high_ref[rows, :] = high
            low_ref[rows, :] = low
        moments = nn(basis, high_ref[...]) + nn(basis, low_ref[...])
        for half in range(2):
            moment_ref[pl.ds(2 * view + half, 8, stride=8), :] = moments[
                0:8, 128 * half : 128 * half + 128
            ]

    kept = [entry_ref[pl.ds(8 * n, GROUPS), :] for n in range(KEPT)]
    shift_x, shift_y = kept[0:2]
    opacity, qw, qx, qy, qz = kept[6:11]
    conic = kept[11:14]
    scale = kept[14:17]
    screen = (kept[17:20], kept[20:23])
    stretched = (kept[23:26], kept[26:29], kept[29:32])
    camera = [cast_ref[pl.ds(8 * i, GROUPS), :] for i in range(6)]
    affine = (camera[0:3], camera[3:6])
    m_0, m_u, m_v, m_uu, m_uv, m_vv = [
        moment_ref[pl.ds(8 * n, GROUPS), :] for n in range(6)
    ]
    m_x = m_u - shift_x * m_0
    m_y = m_v - shift_y * m_0
    m_xx = m_uu - 2.0 * shift_x * m_u + shift_x * shift_x * m_0
    m_xy = m_uv - shift_x * m_v - shift_y * m_u + shift_x * shift_y * m_0
    m_yy = m_vv - 2.0 * shift_y * m_v + shift_y * shift_y * m_0
    d_mean = (conic[0] * m_x + conic[1] * m_y, conic[1] * m_x + conic[2] * m_y)
    left = (
        (conic[0] * m_xx + conic[1] * m_xy, conic[0] * m_xy + conic[1] * m_yy),
        (conic[1] * m_xx + conic[2] * m_xy, conic[1] * m_xy + conic[2] * m_yy),
    )
    d_a = 0.5 * (left[0][0] * conic[0] + left[0][1] * conic[1])
    d_b = left[0][0] * conic[1] + left[0][1] * conic[2]
    d_c = 0.5 * (left[1][0] * conic[1] + left[1][1] * conic[2])
    d_screen = [
        [2.0 * d_a * screen[0][j] + d_b * screen[1][j] for j in range(3)],
        [2.0 * d_c * screen[1][j] + d_b * screen[0][j] for j in range(3)],
    ]
    d_stretched = [
        [affine[0][i] * d_screen[0][j] + affine[1][i] * d_screen[1][j] for j in range(3)]
        for i in range(3)
    ]
    d_scale = [sum(d_stretched[i][j] * stretched[i][j] for i in range(3)) for j in range(3)]
    r = [[d_stretched[i][j] * scale[j] for j in range(3)] for i in range(3)]
    d_unit = [
        2.0 * (qz * (r[1][0] - r[0][1]) + qy * (r[0][2] - r[2][0]) + qx * (r[2][1] - r[1][2])),
        2.0
        * (
            qy * (r[0][1] + r[1][0])
            + qz * (r[0][2] + r[2][0])
            + qw * (r[2][1] - r[1][2])
            - 2.0 * qx * (r[1][1] + r[2][2])
        ),
        2.0
        * (
            qx * (r[0][1] + r[1][0])
            + qz * (r[1][2] + r[2][1])
            + qw * (r[0][2] - r[2][0])
            - 2.0 * qy * (r[0][0] + r[2][2])
        ),
        2.0
        * (
            qx * (r[0][2] + r[2][0])
            + qy * (r[1][2] + r[2][1])
            + qw * (r[1][0] - r[0][1])
            - 2.0 * qz * (r[0][0] + r[1][1])
        ),
    ]
    unit = (qw, qx, qy, qz)
    radial = sum(unit[i] * d_unit[i] for i in range(4))
    gradients = (
        [affine[0][i] * d_mean[0] + affine[1][i] * d_mean[1] for i in range(3)]
        + d_scale
        + [(d_unit[i] - unit[i] * radial) * qw for i in range(1, 4)]
        + [m_0 * (1.0 - opacity)]
    )
    for n, value in enumerate(gradients):
        high = value.astype(bf16).astype(f32)
        grads_ref[pl.ds(16 * n, GROUPS), :] = high
        grads_ref[pl.ds(16 * n + 8, GROUPS), :] = value - high
    for copy in copies:
        copy.wait()


def scatter_kernel(
    places_ref,
    chosen_ref,
    grads_ref,
    tint_ref,
    back_ref,
    spread_ref,
):
    kinds_of = GEOMETRY * 32
    for group in range(GROUPS):
        view, half = divmod(group, 2)
        lanes = pl.ds(128 * group, 128)
        chosen = chosen_ref[:, lanes]
        for n in range(GEOMETRY):
            for part in range(2):
                value = grads_ref[pl.ds(16 * n + 8 * part + group, 1), :]
                spread_ref[pl.ds(kinds_of * part + 32 * n, 32), lanes] = (
                    chosen * jnp.broadcast_to(value, (32, 128)).astype(bf16)
                )
        for k in range(3):
            value = tint_ref[pl.ds(8 * view + k, 1), pl.ds(128 * half, 128)]
            high = value.astype(bf16).astype(f32)
            for part, piece in enumerate((high, value - high)):
                spread_ref[pl.ds(2 * kinds_of + 96 * part + 32 * k, 32), lanes] = (
                    chosen * jnp.broadcast_to(piece, (32, 128)).astype(bf16)
                )

    def store(row, value):
        for upper in range(2):
            for side in range(2):
                back_ref[pl.ds(4 * row + 2 * upper + side, 16, stride=SEND), :] = value[
                    16 * upper : 16 * upper + 16, 128 * side : 128 * side + 128
                ]

    dense = nt(spread_ref[0 : 2 * kinds_of, :], places_ref[...])
    for n in range(GEOMETRY):
        store(n, dense[32 * n : 32 * n + 32] + dense[kinds_of + 32 * n : kinds_of + 32 * n + 32])
    for view in range(VIEWS):
        lanes = slice(256 * view, 256 * view + 256)
        dense = nt(spread_ref[2 * kinds_of : 2 * kinds_of + 192, lanes], places_ref[:, lanes])
        for k in range(3):
            store(
                GEOMETRY + 3 * view + k,
                dense[32 * k : 32 * k + 32] + dense[96 + 32 * k : 96 + 32 * k + 32],
            )
    for owner in range(OWNERS):
        back_ref[pl.ds(SEND * owner + ERRORS, 4), :] = jnp.zeros((4, 128), f32)


def pair_kernel(mine_ref, theirs_ref, sum_ref):
    sum_ref[...] = mine_ref[...] + theirs_ref[...]


def note_kernel(back_ref, mine_ref, theirs_ref, noted_ref):
    losses = mine_ref[0:4, :] + theirs_ref[0:4, :]
    noted_ref[...] = back_ref[...]
    for owner in range(OWNERS):
        noted_ref[pl.ds(SEND * owner + ERRORS, 4), :] = losses


def fold_kernel(back_ref, total_ref, loss_ref):
    total = back_ref[0:SEND, :]
    for owner in range(1, OWNERS):
        total = total + back_ref[pl.ds(SEND * owner, SEND), :]
    total_ref[...] = total
    loss_ref[...] = total[SEND - 8 : SEND]


def adam_kernel(
    total_ref,
    slope_ref,
    column_ref,
    image_ref,
    params_ref,
    moment_one_ref,
    moment_two_ref,
    params_hbm,
    first_hbm,
    second_hbm,
    rendered_hbm,
    gradient_ref,
    params_out,
    first_out,
    second_out,
    rendered_out,
    sems,
):
    for view in range(VIEWS):
        for k in range(3):
            rendered_out[view, k, :, :] = image_ref[pl.ds(3 * view + k, 1), :]
    copies = [pltpu.make_async_copy(rendered_out, rendered_hbm, sems.at[0])]
    copies[0].start()
    columns = [
        [column_ref[pl.ds(16 * view + 8 * half, 8), :] for half in range(2)]
        for view in range(VIEWS)
    ]
    row = iota((59, 128), 0)
    rates = jnp.where(row < 14, 0.0025, 0.000125)
    rates = jnp.where(row < 11, 0.05, rates)
    rates = jnp.where(row < 10, 0.001, rates)
    rates = jnp.where(row < 6, 0.005, rates)
    rates = jnp.where(row < 3, 0.00016, rates)
    for quarter in range(4):
        lanes = pl.ds(128 * quarter, 128)
        base = 64 * quarter
        gradient_ref[pl.ds(base, 6), :] = total_ref[pl.ds(quarter, 6, stride=4), :]
        w = params_ref[6:7, lanes]
        d_ratio = total_ref[pl.ds(24 + quarter, 3, stride=4), :] / w
        lean = jnp.sum(d_ratio * params_ref[7:10, lanes], axis=0, keepdims=True)
        gradient_ref[pl.ds(base + 6, 1), :] = -lean / w
        gradient_ref[pl.ds(base + 7, 3), :] = d_ratio
        gradient_ref[pl.ds(base + 10, 1), :] = total_ref[pl.ds(36 + quarter, 1), :]
        for k in range(3):
            tints = []
            for view in range(VIEWS):
                place = 4 * (3 * view + k) + quarter
                tint = total_ref[pl.ds(COLOURS + place, 1), :] * slope_ref[pl.ds(place, 1), :]
                tints.append(jnp.broadcast_to(tint, (8, 128)))
            for half in range(2):
                gradient_ref[pl.ds(base + 11 + 24 * half + k, 8, stride=3), :] = sum(
                    columns[view][half] * tints[view] for view in range(VIEWS)
                )
        gradient = gradient_ref[pl.ds(base, 59), :]
        first = 0.9 * moment_one_ref[:, lanes] + 0.1 * gradient
        second = 0.999 * moment_two_ref[:, lanes] + 0.001 * gradient * gradient
        first_out[:, lanes] = first
        second_out[:, lanes] = second
        params_out[:, lanes] = params_ref[:, lanes] - rates * first / (jnp.sqrt(second) + 1e-15)
        pairs = ((params_out, params_hbm), (first_out, first_hbm), (second_out, second_hbm))
        for n, (source, target) in enumerate(pairs):
            copy = pltpu.make_async_copy(
                source.at[:, lanes], target.at[:, lanes], sems.at[1 + 3 * quarter + n]
            )
            copy.start()
            copies.append(copy)
    for copy in copies:
        copy.wait()


VM = pl.BlockSpec(memory_space=pltpu.VMEM)
SM = pl.BlockSpec(memory_space=pltpu.SMEM)
HB = pl.BlockSpec(memory_space=pltpu.HBM)


def shape(*dims):
    return jax.ShapeDtypeStruct(dims, f32)


def swapped(value, partner):
    return lax.ppermute(value, GAUSS, [(i, partner(i)) for i in range(8)])


def in_hbm(array):
    return pltpu.with_memory_space_constraint(array, pltpu.HBM)


def limit(mib):
    return pltpu.CompilerParams(vmem_limit_bytes=mib << 20)


def shards(params, moment_one, moment_two, camera, target, tile_ids, splat_lists, counts):
    wide = shape(59, 512)
    (
        sent,
        slope,
        lane,
        block,
        cast,
        column,
        places,
        chosen,
        before,
        behind,
        basis,
        params,
    ) = pl.pallas_call(
        pack_kernel,
        out_shape=(
            shape(OWNERS * SEND, 128),
            shape(36, 128),
            jax.ShapeDtypeStruct((48, 128), jnp.int32),
            jax.ShapeDtypeStruct((48, 128), jnp.int32),
            shape(88, 128),
            shape(48, 128),
            jax.ShapeDtypeStruct((256, 768), bf16),
            jax.ShapeDtypeStruct((32, 768), bf16),
            jax.ShapeDtypeStruct((512, 256), bf16),
            jax.ShapeDtypeStruct((512, 256), bf16),
            jax.ShapeDtypeStruct((16, 256), bf16),
            wide,
        ),
        in_specs=[HB] * 5,
        out_specs=(VM,) * 12,
        scratch_shapes=[
            pltpu.VMEM((SEND, 128), f32),
            pltpu.VMEM((256, 128), f32),
            pltpu.SMEM((3, 11), f32),
            pltpu.VMEM((VIEWS, 1, 256), jnp.int32),
            pltpu.SMEM((1, 3), jnp.int32),
            pltpu.SMEM((1, 3), jnp.int32),
            pltpu.SemaphoreType.DMA((8,)),
        ],
        compiler_params=limit(6),
        name="pack",
    )(
        in_hbm(params),
        in_hbm(camera),
        in_hbm(splat_lists),
        in_hbm(counts.reshape(1, VIEWS)),
        in_hbm(tile_ids.reshape(1, VIEWS)),
    )
    table = lax.all_to_all(
        sent.reshape(OWNERS, SEND, 128), TILE, split_axis=0, concat_axis=0, tiled=True
    ).reshape(OWNERS * SEND, 128)
    half = jax.ShapeDtypeStruct((48, 256), bf16)
    image, loss, shade, keep, pulled, stacked, tint, entries = pl.pallas_call(
        front_kernel,
        out_shape=(
            shape(16, 256),
            shape(8, 128),
            shape(VIEWS * 256, 256),
            shape(VIEWS * 256, 256),
            half,
            half,
            shape(24, 256),
            shape(8 * KEPT, 128),
        ),
        in_specs=[VM] * 5 + [HB],
        out_specs=(VM,) * 8,
        scratch_shapes=[
            pltpu.VMEM((GROUPS * SEND, 128), f32),
            pltpu.VMEM((48, 256), f32),
            pltpu.VMEM((24, 256), f32),
            pltpu.VMEM((256, 512), bf16),
            pltpu.VMEM((256, 256), bf16),
            pltpu.VMEM((256, 256), bf16),
            pltpu.VMEM((VIEWS, 3, 1, 256), f32),
            pltpu.SemaphoreType.DMA((1,)),
        ],
        compiler_params=pltpu.CompilerParams(
            vmem_limit_bytes=16 << 20
        ),
        name="front",
    )(table, lane, block, cast, before, in_hbm(target))
    side = swapped(loss, lambda i: i ^ 2)
    grads, moment_one, moment_two = pl.pallas_call(
        back_kernel,
        out_shape=(shape(16 * GEOMETRY, 128), wide, wide),
        in_specs=[VM] * 8 + [HB] * 2,
        out_specs=(VM,) * 3,
        scratch_shapes=[
            pltpu.VMEM((256, 512), bf16),
            pltpu.VMEM((256, 256), bf16),
            pltpu.VMEM((256, 256), bf16),
            pltpu.VMEM((64, 128), f32),
            pltpu.SemaphoreType.DMA((2,)),
        ],
        compiler_params=limit(12),
        cost_estimate=pl.CostEstimate(
            flops=1 << 31, bytes_accessed=1 << 23, transcendentals=1 << 20
        ),
        name="back",
    )(
        shade,
        keep,
        pulled,
        stacked,
        entries,
        cast,
        behind,
        basis,
        in_hbm(moment_one),
        in_hbm(moment_two),
    )
    pair = pl.pallas_call(
        pair_kernel,
        out_shape=shape(8, 128),
        in_specs=[VM] * 2,
        out_specs=VM,
        compiler_params=limit(2),
        name="pair",
    )(loss, side)
    wrap = swapped(pair, lambda i: i ^ 6)
    back = pl.pallas_call(
        scatter_kernel,
        out_shape=shape(OWNERS * SEND, 128),
        in_specs=[VM] * 4,
        out_specs=VM,
        scratch_shapes=[pltpu.VMEM((2 * 32 * GEOMETRY + 192, 768), bf16)],
        compiler_params=limit(12),
        cost_estimate=pl.CostEstimate(
            flops=1 << 31, bytes_accessed=1 << 23, transcendentals=1 << 20
        ),
        name="scatter",
    )(places, chosen, grads, tint)
    back = pl.pallas_call(
        note_kernel,
        out_shape=shape(OWNERS * SEND, 128),
        in_specs=[VM] * 3,
        out_specs=VM,
        compiler_params=limit(4),
        name="note",
    )(back, pair, wrap)
    arrived = lax.all_to_all(
        back.reshape(OWNERS, SEND, 128), TILE, split_axis=0, concat_axis=0, tiled=True
    ).reshape(OWNERS * SEND, 128)
    total, loss = pl.pallas_call(
        fold_kernel,
        out_shape=(shape(SEND, 128), shape(8, 128)),
        in_specs=[VM],
        out_specs=(VM, VM),
        compiler_params=limit(4),
        name="fold",
    )(arrived)
    core = swapped(loss, lambda i: i ^ 1)
    updated, first, second, rendered = pl.pallas_call(
        adam_kernel,
        out_shape=(wide, wide, wide, shape(VIEWS, 3, 1, 256)),
        in_specs=[VM] * 7,
        out_specs=(HB,) * 4,
        scratch_shapes=[
            pltpu.VMEM((256, 128), f32),
            pltpu.VMEM((59, 512), f32),
            pltpu.VMEM((59, 512), f32),
            pltpu.VMEM((59, 512), f32),
            pltpu.VMEM((VIEWS, 3, 1, 256), f32),
            pltpu.SemaphoreType.DMA((13,)),
        ],
        compiler_params=limit(4),
        cost_estimate=pl.CostEstimate(
            flops=1 << 30, bytes_accessed=1 << 22, transcendentals=1 << 16
        ),
        name="adam",
    )(total, slope, column, image, params, moment_one, moment_two)
    losses = (loss + core)[4, :VIEWS] * (0.5 / (3 * 256 * 128))
    return (updated, first, second, rendered, losses)


def solution(mesh):
    finer = Mesh(mesh.devices.reshape(4, 2, 4, 4), GAUSS_TILE)
    in_specs = (
        P(None, GAUSS_TILE),
        P(None, GAUSS_TILE),
        P(None, GAUSS_TILE),
        P(),
        P(None, None, GAUSS_TILE, None),
        P(None, GAUSS_TILE),
        P(None, GAUSS_TILE, None),
        P(None, GAUSS_TILE),
    )
    out_specs = (
        P(None, GAUSS_TILE),
        P(None, GAUSS_TILE),
        P(None, GAUSS_TILE),
        P(None, None, GAUSS_TILE, None),
        P(),
    )
    return jax.shard_map(
        shards, mesh=finer, in_specs=in_specs, out_specs=out_specs, check_vma=False
    )
```

```python
import jax
import jax.numpy as jnp
from jax import lax
from jax.experimental import pallas as pl
from jax.experimental.pallas import tpu as pltpu
from jax.sharding import Mesh
from jax.sharding import PartitionSpec as P

VIEWS = 3
TILES_WIDE = 4
TILE = ("tile_0", "tile_1")
GAUSS = ("gauss_0", "gauss_1")
GAUSS_TILE = ("gauss_0", "gauss_1", "tile_0", "tile_1")
OWNERS = 16
OWN = 512
GEOMETRY = 10
COLOURS = 4 * GEOMETRY
ERRORS = COLOURS + 36
SEND = ERRORS + 4
GROUPS = 6
KEPT = 32
LOG2E = 1.4426950408889634

band_zero = 0.28209479177387814
band_one = 0.4886025119029199
band_two = (
    1.0925484305920792,
    -1.0925484305920792,
    0.31539156525252005,
    -1.0925484305920792,
    0.5462742152960396,
)
band_three = (
    -0.5900435899266435,
    2.890611442640554,
    -0.4570457994644658,
    0.3731763325901154,
    -0.4570457994644658,
    1.445305721320277,
    -0.5900435899266435,
)

f32 = jnp.float32
bf16 = jnp.bfloat16


def iota(shape, dim):
    return lax.broadcasted_iota(jnp.int32, shape, dim)


def harmonic_halves(camera_ref, view):
    x, y, z = [jnp.full((8, 128), camera_ref[view, 8 + i], f32) for i in range(3)]
    xx, yy, zz = x * x, y * y, z * z
    values = [
        jnp.full((8, 128), band_zero, f32),
        -band_one * y,
        band_one * z,
        -band_one * x,
        band_two[0] * x * y,
        band_two[1] * y * z,
        band_two[2] * (2.0 * zz - xx - yy),
        band_two[3] * x * z,
        band_two[4] * (xx - yy),
        band_three[0] * y * (3.0 * xx - yy),
        band_three[1] * x * y * z,
        band_three[2] * y * (4.0 * zz - xx - yy),
        band_three[3] * z * (2.0 * zz - 3.0 * xx - 3.0 * yy),
        band_three[4] * x * (4.0 * zz - xx - yy),
        band_three[5] * z * (xx - yy),
        band_three[6] * x * (xx - 3.0 * yy),
    ]
    row = iota((8, 128), 0)
    halves = []
    for half in range(2):
        column = values[8 * half]
        for i in range(1, 8):
            column = jnp.where(row == i, values[8 * half + i], column)
        halves.append(column)
    return halves


def per_view(values):
    place = iota((GROUPS, 128), 0)
    return jnp.where(place < 2, values[0], jnp.where(place < 4, values[1], values[2]))


def pack_kernel(
    params_hbm,
    camera_hbm,
    lists_hbm,
    counts_hbm,
    tiles_hbm,
    send_ref,
    slope_ref,
    lane_ref,
    block_ref,
    cast_ref,
    column_ref,
    places_ref,
    chosen_ref,
    before_ref,
    behind_ref,
    basis_ref,
    params_ref,
    pack_ref,
    tall_ref,
    camera_ref,
    lists_ref,
    counts_ref,
    tiles_ref,
    sems,
):
    sources = [camera_hbm, counts_hbm, tiles_hbm, lists_hbm]
    targets = [camera_ref, counts_ref, tiles_ref, lists_ref]
    for quarter in range(4):
        lanes = pl.ds(128 * quarter, 128)
        sources.append(params_hbm.at[:, lanes])
        targets.append(params_ref.at[:, lanes])
    copies = [
        pltpu.make_async_copy(source, target, sems.at[n])
        for n, (source, target) in enumerate(zip(sources, targets))
    ]
    for copy in copies:
        copy.start()

    first = iota((256, 256), 0)
    second = iota((256, 256), 1)
    for ref, strictly in ((before_ref, first < second), (behind_ref, first > second)):
        ones = jnp.where(strictly, 1.0, 0.0).astype(bf16)
        ref[0:256, :] = ones
        ref[256:512, :] = ones
    pixel = iota((16, 256), 1)
    power = iota((16, 256), 0)
    pixel_u = (pixel % 16).astype(f32) - 7.5
    pixel_v = (pixel // 16).astype(f32) - 7.5
    basis = jnp.where(power == 0, 1.0, jnp.where(power == 1, pixel_u, pixel_v))
    basis = jnp.where(power == 3, pixel_u * pixel_u, basis)
    basis = jnp.where(power == 4, pixel_u * pixel_v, basis)
    basis = jnp.where(power == 5, pixel_v * pixel_v, basis)
    basis_ref[...] = jnp.where(power > 5, 0.0, basis).astype(bf16)
    for copy in copies[0:4]:
        copy.wait()
    columns = [harmonic_halves(camera_ref, view) for view in range(VIEWS)]
    quarter = iota((8, 128), 0) & 3
    fine = iota((256, 128), 0)
    coarse = iota((32, 128), 0)
    for group in range(GROUPS):
        view, half = divmod(group, 2)
        local = lists_ref[view, :, 128 * half : 128 * half + 128] & 8191
        spread = jnp.broadcast_to(local, (8, 128))
        lane_ref[pl.ds(8 * group, 8), :] = spread & 127
        block_ref[pl.ds(8 * group, 8), :] = (spread >> 7) - quarter
        lanes = pl.ds(128 * group, 128)
        places_ref[:, lanes] = jnp.where((local & 255) == fine, 1.0, 0.0).astype(bf16)
        owner_part = ((local >> 8) & 1) * 16 + (local >> 9)
        chosen_ref[:, lanes] = jnp.where(owner_part == coarse, 1.0, 0.0).astype(bf16)
    for i in range(8):
        cast_ref[pl.ds(8 * i, GROUPS), :] = per_view(
            [camera_ref[view, i] for view in range(VIEWS)]
        )
    place = iota((GROUPS, 128), 0)
    position = (place & 1) * 128 + iota((GROUPS, 128), 1)
    live = position < per_view([counts_ref[0, view] for view in range(VIEWS)])
    cast_ref[pl.ds(64, GROUPS), :] = jnp.where(live, 1.0, 0.0)
    tile = per_view([tiles_ref[0, view] for view in range(VIEWS)])
    cast_ref[pl.ds(72, GROUPS), :] = (tile % TILES_WIDE * 16 + 8).astype(f32)
    cast_ref[pl.ds(80, GROUPS), :] = (tile // TILES_WIDE * 16 + 8).astype(f32)
    for view in range(VIEWS):
        for half in range(2):
            column_ref[pl.ds(16 * view + 8 * half, 8), :] = columns[view][half]
    for quarter in range(4):
        copies[4 + quarter].wait()
        lanes = pl.ds(128 * quarter, 128)
        pack_ref[pl.ds(quarter, 6, stride=4), :] = params_ref[0:6, lanes]
        pack_ref[pl.ds(24 + quarter, 3, stride=4), :] = (
            params_ref[7:10, lanes] / params_ref[6:7, lanes]
        )
        pack_ref[pl.ds(36 + quarter, 1), :] = params_ref[10:11, lanes]
        tall_ref[pl.ds(64 * quarter, 59), :] = params_ref[:, lanes]
    for k in range(3):
        for quarter in range(4):
            low = tall_ref[pl.ds(64 * quarter + 11 + k, 8, stride=3), :]
            high = tall_ref[pl.ds(64 * quarter + 35 + k, 8, stride=3), :]
            for view in range(VIEWS):
                terms = columns[view][0] * low + columns[view][1] * high
                raw = jnp.sum(terms, axis=0, keepdims=True) + 0.5
                row = 4 * (3 * view + k) + quarter
                pack_ref[pl.ds(COLOURS + row, 1), :] = jnp.maximum(raw, 0.0)
                slope_ref[pl.ds(row, 1), :] = jnp.where(
                    raw > 0.0, 1.0, jnp.where(raw == 0.0, 0.5, 0.0)
                )
    pack_ref[pl.ds(ERRORS, 4), :] = jnp.zeros((4, 128), f32)
    packed = pack_ref[...]
    for owner in range(OWNERS):
        send_ref[pl.ds(SEND * owner, SEND), :] = packed


def split(value):
    high = value.astype(bf16)
    return high, (value - high.astype(f32)).astype(bf16)


def nn(lhs, rhs):
    return lax.dot_general(lhs, rhs, (((1,), (0,)), ((), ())), preferred_element_type=f32)


def nt(lhs, rhs):
    return lax.dot_general(lhs, rhs, (((1,), (1,)), ((), ())), preferred_element_type=f32)


def tn(lhs, rhs):
    return lax.dot_general(lhs, rhs, (((0,), (0,)), ((), ())), preferred_element_type=f32)


def front_kernel(
    table_ref,
    lane_ref,
    block_ref,
    cast_ref,
    before_ref,
    target_hbm,
    image_ref,
    loss_ref,
    shade_ref,
    keep_ref,
    pulled_ref,
    stacked_ref,
    high_ref,
    low_ref,
    entry_ref,
    found_ref,
    rows_ref,
    colour_ref,
    logs_ref,
    target_ref,
    sem,
):
    goal = pltpu.make_async_copy(target_hbm, target_ref, sem.at[0])
    goal.start()
    for group in range(GROUPS):
        view, half = divmod(group, 2)
        lane = lane_ref[pl.ds(8 * group, 8), :]
        block = block_ref[pl.ds(8 * group, 8), :]
        first = (COLOURS + 12 * view) // 8
        last = (COLOURS + 12 * view + 11) // 8
        pieces = list(range(5)) + list(range(first, last + 1))
        found = {piece: jnp.zeros((8, 128), f32) for piece in pieces}
        for owner in range(OWNERS):
            here = block == 4 * owner
            for piece in pieces:
                rows = table_ref[pl.ds(SEND * owner + 8 * piece, 8), :]
                picked = jnp.take_along_axis(rows, lane, axis=1, mode="promise_in_bounds")
                found[piece] = jnp.where(here, picked, found[piece])
        for piece in pieces:
            found_ref[pl.ds(SEND * group + 8 * piece, 8), :] = found[piece]

    def entry_row(row):
        parts = [found_ref[pl.ds(4 * row + q, GROUPS, stride=SEND), :] for q in range(4)]
        return (parts[0] + parts[1]) + (parts[2] + parts[3])

    for group in range(GROUPS):
        view, half = divmod(group, 2)
        for k in range(3):
            start = SEND * group + COLOURS + 4 * (3 * view + k)
            value = jnp.sum(found_ref[pl.ds(start, 4), :], axis=0, keepdims=True)
            colour_ref[pl.ds(8 * view + k, 1), pl.ds(128 * half, 128)] = value

    camera = [cast_ref[pl.ds(8 * i, GROUPS), :] for i in range(8)]
    affine = (camera[0:3], camera[3:6])
    centre = [entry_row(i) for i in range(3)]
    scale = [jnp.exp(entry_row(3 + i)) for i in range(3)]
    ratio = [entry_row(6 + i) for i in range(3)]
    logit = entry_row(9)
    inverse_norm = 1.0 / jnp.sqrt(
        1.0 + ratio[0] * ratio[0] + ratio[1] * ratio[1] + ratio[2] * ratio[2]
    )
    qw = inverse_norm
    qx, qy, qz = [component * inverse_norm for component in ratio]
    rotation = [
        [1.0 - 2.0 * (qy * qy + qz * qz), 2.0 * (qx * qy - qw * qz), 2.0 * (qx * qz + qw * qy)],
        [2.0 * (qx * qy + qw * qz), 1.0 - 2.0 * (qx * qx + qz * qz), 2.0 * (qy * qz - qw * qx)],
        [2.0 * (qx * qz - qw * qy), 2.0 * (qy * qz + qw * qx), 1.0 - 2.0 * (qx * qx + qy * qy)],
    ]
    stretched = [[rotation[i][j] * scale[j] for j in range(3)] for i in range(3)]
    screen = [
        [sum(affine[k][i] * stretched[i][j] for i in range(3)) for j in range(3)] for k in range(2)
    ]
    cov_a = sum(screen[0][j] * screen[0][j] for j in range(3)) + 0.3
    cov_b = sum(screen[0][j] * screen[1][j] for j in range(3))
    cov_c = sum(screen[1][j] * screen[1][j] for j in range(3)) + 0.3
    inverse_det = 1.0 / (cov_a * cov_c - cov_b * cov_b)
    live = cast_ref[pl.ds(64, GROUPS), :] > 0.5
    conic = [
        jnp.where(live, value * inverse_det, 0.0) for value in (cov_c, -cov_b, cov_a)
    ]
    mean = [sum(affine[k][i] * centre[i] for i in range(3)) + camera[6 + k] for k in range(2)]
    opacity = 1.0 / (1.0 + jnp.exp(-logit))
    shown = jnp.where(live, opacity, 0.0)
    shift_x = mean[0] - cast_ref[pl.ds(72, GROUPS), :]
    shift_y = mean[1] - cast_ref[pl.ds(80, GROUPS), :]
    kept = (
        [shift_x, shift_y]
        + [(-0.5 * LOG2E) * conic[0], (-LOG2E) * conic[1], (-0.5 * LOG2E) * conic[2]]
        + [shown, opacity, qw, qx, qy, qz]
        + conic
        + scale
        + screen[0]
        + screen[1]
        + stretched[0]
        + stretched[1]
        + stretched[2]
    )
    for n, value in enumerate(kept):
        entry_ref[pl.ds(8 * n, GROUPS), :] = value
    for n in range(6):
        for half in range(2):
            rows_ref[pl.ds(8 * n, VIEWS), pl.ds(128 * half, 128)] = entry_ref[
                pl.ds(8 * n + half, VIEWS, stride=2), :
            ]

    goal.wait()
    offset = iota((16, 256), 0).astype(f32) - 7.5
    losses = jnp.zeros((8, 128), f32)

    for view in range(VIEWS):

        def row(n, view=view):
            return rows_ref[pl.ds(8 * n + view, 1), :]

        mean_u, mean_v = row(0), row(1)
        opaque = jnp.broadcast_to(row(5), (16, 256))
        dx = offset - mean_u
        along = row(2) * dx * dx
        across = row(3) * dx
        upright = row(4)
        base = 256 * view
        for line in range(16):
            dy = (line - 7.5) - mean_v
            exponent = along + (upright * dy * dy + across * dy)
            shade = opaque * jnp.exp2(exponent)
            shade_ref[pl.ds(base + 16 * line, 16), :] = shade
            high, low = split(jnp.log(1.0 - jnp.minimum(shade, 0.99)))
            logs_ref[pl.ds(16 * line, 16), 0:256] = high
            logs_ref[pl.ds(16 * line, 16), 256:512] = low
        for part in range(4):
            rows = pl.ds(64 * part, 64)
            there = pl.ds(base + 64 * part, 64)
            keep = jnp.exp(nn(logs_ref[rows, :], before_ref[...]))
            keep_ref[there, :] = keep
            high, low = split(jnp.minimum(shade_ref[there, :], 0.99) * keep)
            high_ref[there, :] = high
            low_ref[there, :] = low
        colour = colour_ref[pl.ds(8 * view, 8), :]
        colour_high, colour_low = [part.astype(f32) for part in split(colour)]
        stacked = jnp.concatenate(
            [
                colour_high[0:3],
                colour_high[0:3],
                colour_low[0:3],
                jnp.zeros((7, 256), f32),
            ],
            axis=0,
        ).astype(bf16)
        image_high = nt(stacked, high_ref[pl.ds(base, 256), :])
        image_low = nt(stacked, low_ref[pl.ds(base, 256), :])
        image = image_high[0:3] + image_high[6:9] + image_low[0:3]
        residuals = []
        total = jnp.zeros((1, 256), f32)
        for k in range(3):
            image_ref[pl.ds(3 * view + k, 1), :] = image[k : k + 1]
            residual = image[k : k + 1] - target_ref[view, k, :, :]
            total = total + residual * residual
            residuals.append(residual * (1.0 / (VIEWS * 256)))
        losses = jnp.where(iota((8, 128), 1) == view, jnp.sum(total, axis=1, keepdims=True), losses)
        error = jnp.concatenate(residuals, axis=0)
        error_high, error_low = [part.astype(f32) for part in split(error)]
        pulled = jnp.concatenate(
            [error_high, error_low, error_high, jnp.zeros((7, 256), f32)], axis=0
        ).astype(bf16)
        pulled_ref[pl.ds(16 * view, 16), :] = pulled
        stacked_ref[pl.ds(16 * view, 16), :] = stacked
    loss_ref[...] = losses


def back_kernel(
    shade_ref,
    keep_ref,
    pulled_ref,
    stacked_ref,
    weight_high_ref,
    weight_low_ref,
    entry_ref,
    cast_ref,
    behind_ref,
    basis_ref,
    moment_one_hbm,
    moment_two_hbm,
    grads_ref,
    tint_ref,
    moment_one_ref,
    moment_two_ref,
    logs_ref,
    high_ref,
    low_ref,
    moment_ref,
    sems,
):
    copies = [
        pltpu.make_async_copy(moment_one_hbm, moment_one_ref, sems.at[0]),
        pltpu.make_async_copy(moment_two_hbm, moment_two_ref, sems.at[1]),
    ]
    for copy in copies:
        copy.start()
    basis = basis_ref[...]

    for view in range(VIEWS):
        base = 256 * view
        small = pl.ds(16 * view, 16)
        pulled = pulled_ref[small, :]
        pull = tn(pulled, stacked_ref[small, :])
        tint = nn(pulled, weight_high_ref[pl.ds(base, 256), :])
        tint_low = nn(pulled, weight_low_ref[pl.ds(base, 256), :])
        tint_ref[pl.ds(8 * view, 3), :] = tint[0:3] + tint[3:6] + tint_low[0:3]
        for part in range(4):
            rows = pl.ds(64 * part, 64)
            there = pl.ds(base + 64 * part, 64)
            weight = jnp.minimum(shade_ref[there, :], 0.99) * keep_ref[there, :]
            high, low = split(pull[64 * part : 64 * part + 64] * weight)
            logs_ref[rows, 0:256] = high
            logs_ref[rows, 256:512] = low
        for part in range(4):
            rows = pl.ds(64 * part, 64)
            there = pl.ds(base + 64 * part, 64)
            behind = nn(logs_ref[rows, :], behind_ref[...])
            shade = shade_ref[there, :]
            alpha = jnp.minimum(shade, 0.99)
            slope = pull[64 * part : 64 * part + 64] * keep_ref[there, :] - behind / (1.0 - alpha)
            passed = jnp.where(shade < 0.99, shade, jnp.where(shade == 0.99, 0.5 * shade, 0.0))
            high, low = split(slope * passed)
            high_ref[rows, :] = high
            low_ref[rows, :] = low
        moments = nn(basis, high_ref[...]) + nn(basis, low_ref[...])
        for half in range(2):
            moment_ref[pl.ds(2 * view + half, 8, stride=8), :] = moments[
                0:8, 128 * half : 128 * half + 128
            ]

    kept = [entry_ref[pl.ds(8 * n, GROUPS), :] for n in range(KEPT)]
    shift_x, shift_y = kept[0:2]
    opacity, qw, qx, qy, qz = kept[6:11]
    conic = kept[11:14]
    scale = kept[14:17]
    screen = (kept[17:20], kept[20:23])
    stretched = (kept[23:26], kept[26:29], kept[29:32])
    camera = [cast_ref[pl.ds(8 * i, GROUPS), :] for i in range(6)]
    affine = (camera[0:3], camera[3:6])
    m_0, m_u, m_v, m_uu, m_uv, m_vv = [
        moment_ref[pl.ds(8 * n, GROUPS), :] for n in range(6)
    ]
    m_x = m_u - shift_x * m_0
    m_y = m_v - shift_y * m_0
    m_xx = m_uu - 2.0 * shift_x * m_u + shift_x * shift_x * m_0
    m_xy = m_uv - shift_x * m_v - shift_y * m_u + shift_x * shift_y * m_0
    m_yy = m_vv - 2.0 * shift_y * m_v + shift_y * shift_y * m_0
    d_mean = (conic[0] * m_x + conic[1] * m_y, conic[1] * m_x + conic[2] * m_y)
    left = (
        (conic[0] * m_xx + conic[1] * m_xy, conic[0] * m_xy + conic[1] * m_yy),
        (conic[1] * m_xx + conic[2] * m_xy, conic[1] * m_xy + conic[2] * m_yy),
    )
    d_a = 0.5 * (left[0][0] * conic[0] + left[0][1] * conic[1])
    d_b = left[0][0] * conic[1] + left[0][1] * conic[2]
    d_c = 0.5 * (left[1][0] * conic[1] + left[1][1] * conic[2])
    d_screen = [
        [2.0 * d_a * screen[0][j] + d_b * screen[1][j] for j in range(3)],
        [2.0 * d_c * screen[1][j] + d_b * screen[0][j] for j in range(3)],
    ]
    d_stretched = [
        [affine[0][i] * d_screen[0][j] + affine[1][i] * d_screen[1][j] for j in range(3)]
        for i in range(3)
    ]
    d_scale = [sum(d_stretched[i][j] * stretched[i][j] for i in range(3)) for j in range(3)]
    r = [[d_stretched[i][j] * scale[j] for j in range(3)] for i in range(3)]
    d_unit = [
        2.0 * (qz * (r[1][0] - r[0][1]) + qy * (r[0][2] - r[2][0]) + qx * (r[2][1] - r[1][2])),
        2.0
        * (
            qy * (r[0][1] + r[1][0])
            + qz * (r[0][2] + r[2][0])
            + qw * (r[2][1] - r[1][2])
            - 2.0 * qx * (r[1][1] + r[2][2])
        ),
        2.0
        * (
            qx * (r[0][1] + r[1][0])
            + qz * (r[1][2] + r[2][1])
            + qw * (r[0][2] - r[2][0])
            - 2.0 * qy * (r[0][0] + r[2][2])
        ),
        2.0
        * (
            qx * (r[0][2] + r[2][0])
            + qy * (r[1][2] + r[2][1])
            + qw * (r[1][0] - r[0][1])
            - 2.0 * qz * (r[0][0] + r[1][1])
        ),
    ]
    unit = (qw, qx, qy, qz)
    radial = sum(unit[i] * d_unit[i] for i in range(4))
    gradients = (
        [affine[0][i] * d_mean[0] + affine[1][i] * d_mean[1] for i in range(3)]
        + d_scale
        + [(d_unit[i] - unit[i] * radial) * qw for i in range(1, 4)]
        + [m_0 * (1.0 - opacity)]
    )
    for n, value in enumerate(gradients):
        high = value.astype(bf16).astype(f32)
        grads_ref[pl.ds(16 * n, GROUPS), :] = high
        grads_ref[pl.ds(16 * n + 8, GROUPS), :] = value - high
    for copy in copies:
        copy.wait()


def scatter_kernel(
    places_ref,
    chosen_ref,
    grads_ref,
    tint_ref,
    back_ref,
    spread_ref,
):
    kinds_of = GEOMETRY * 32
    for group in range(GROUPS):
        view, half = divmod(group, 2)
        lanes = pl.ds(128 * group, 128)
        chosen = chosen_ref[:, lanes]
        for n in range(GEOMETRY):
            for part in range(2):
                value = grads_ref[pl.ds(16 * n + 8 * part + group, 1), :]
                spread_ref[pl.ds(kinds_of * part + 32 * n, 32), lanes] = (
                    chosen * jnp.broadcast_to(value, (32, 128)).astype(bf16)
                )
        for k in range(3):
            value = tint_ref[pl.ds(8 * view + k, 1), pl.ds(128 * half, 128)]
            high = value.astype(bf16).astype(f32)
            for part, piece in enumerate((high, value - high)):
                spread_ref[pl.ds(2 * kinds_of + 96 * part + 32 * k, 32), lanes] = (
                    chosen * jnp.broadcast_to(piece, (32, 128)).astype(bf16)
                )

    def store(row, value):
        for upper in range(2):
            for side in range(2):
                back_ref[pl.ds(4 * row + 2 * upper + side, 16, stride=SEND), :] = value[
                    16 * upper : 16 * upper + 16, 128 * side : 128 * side + 128
                ]

    dense = nt(spread_ref[0 : 2 * kinds_of, :], places_ref[...])
    for n in range(GEOMETRY):
        store(n, dense[32 * n : 32 * n + 32] + dense[kinds_of + 32 * n : kinds_of + 32 * n + 32])
    for view in range(VIEWS):
        lanes = slice(256 * view, 256 * view + 256)
        dense = nt(spread_ref[2 * kinds_of : 2 * kinds_of + 192, lanes], places_ref[:, lanes])
        for k in range(3):
            store(
                GEOMETRY + 3 * view + k,
                dense[32 * k : 32 * k + 32] + dense[96 + 32 * k : 96 + 32 * k + 32],
            )
    for owner in range(OWNERS):
        back_ref[pl.ds(SEND * owner + ERRORS, 4), :] = jnp.zeros((4, 128), f32)


def pair_kernel(mine_ref, theirs_ref, sum_ref):
    sum_ref[...] = mine_ref[...] + theirs_ref[...]


def note_kernel(back_ref, mine_ref, theirs_ref, noted_ref):
    losses = mine_ref[0:4, :] + theirs_ref[0:4, :]
    noted_ref[...] = back_ref[...]
    for owner in range(OWNERS):
        noted_ref[pl.ds(SEND * owner + ERRORS, 4), :] = losses


def fold_kernel(back_ref, total_ref, loss_ref):
    total = back_ref[0:SEND, :]
    for owner in range(1, OWNERS):
        total = total + back_ref[pl.ds(SEND * owner, SEND), :]
    total_ref[...] = total
    loss_ref[...] = total[SEND - 8 : SEND]


def adam_kernel(
    total_ref,
    slope_ref,
    column_ref,
    image_ref,
    params_ref,
    moment_one_ref,
    moment_two_ref,
    params_hbm,
    first_hbm,
    second_hbm,
    rendered_hbm,
    gradient_ref,
    params_out,
    first_out,
    second_out,
    rendered_out,
    sems,
):
    for view in range(VIEWS):
        for k in range(3):
            rendered_out[view, k, :, :] = image_ref[pl.ds(3 * view + k, 1), :]
    copies = [pltpu.make_async_copy(rendered_out, rendered_hbm, sems.at[0])]
    copies[0].start()
    columns = [
        [column_ref[pl.ds(16 * view + 8 * half, 8), :] for half in range(2)]
        for view in range(VIEWS)
    ]
    row = iota((59, 128), 0)
    rates = jnp.where(row < 14, 0.0025, 0.000125)
    rates = jnp.where(row < 11, 0.05, rates)
    rates = jnp.where(row < 10, 0.001, rates)
    rates = jnp.where(row < 6, 0.005, rates)
    rates = jnp.where(row < 3, 0.00016, rates)
    for quarter in range(4):
        lanes = pl.ds(128 * quarter, 128)
        base = 64 * quarter
        gradient_ref[pl.ds(base, 6), :] = total_ref[pl.ds(quarter, 6, stride=4), :]
        w = params_ref[6:7, lanes]
        d_ratio = total_ref[pl.ds(24 + quarter, 3, stride=4), :] / w
        lean = jnp.sum(d_ratio * params_ref[7:10, lanes], axis=0, keepdims=True)
        gradient_ref[pl.ds(base + 6, 1), :] = -lean / w
        gradient_ref[pl.ds(base + 7, 3), :] = d_ratio
        gradient_ref[pl.ds(base + 10, 1), :] = total_ref[pl.ds(36 + quarter, 1), :]
        for k in range(3):
            tints = []
            for view in range(VIEWS):
                place = 4 * (3 * view + k) + quarter
                tint = total_ref[pl.ds(COLOURS + place, 1), :] * slope_ref[pl.ds(place, 1), :]
                tints.append(jnp.broadcast_to(tint, (8, 128)))
            for half in range(2):
                gradient_ref[pl.ds(base + 11 + 24 * half + k, 8, stride=3), :] = sum(
                    columns[view][half] * tints[view] for view in range(VIEWS)
                )
        gradient = gradient_ref[pl.ds(base, 59), :]
        first = 0.9 * moment_one_ref[:, lanes] + 0.1 * gradient
        second = 0.999 * moment_two_ref[:, lanes] + 0.001 * gradient * gradient
        first_out[:, lanes] = first
        second_out[:, lanes] = second
        params_out[:, lanes] = params_ref[:, lanes] - rates * first / (jnp.sqrt(second) + 1e-15)
        pairs = ((params_out, params_hbm), (first_out, first_hbm), (second_out, second_hbm))
        for n, (source, target) in enumerate(pairs):
            copy = pltpu.make_async_copy(
                source.at[:, lanes], target.at[:, lanes], sems.at[1 + 3 * quarter + n]
            )
            copy.start()
            copies.append(copy)
    for copy in copies:
        copy.wait()


VM = pl.BlockSpec(memory_space=pltpu.VMEM)
SM = pl.BlockSpec(memory_space=pltpu.SMEM)
HB = pl.BlockSpec(memory_space=pltpu.HBM)


def shape(*dims):
    return jax.ShapeDtypeStruct(dims, f32)


def swapped(value, partner):
    return lax.ppermute(value, GAUSS, [(i, partner(i)) for i in range(8)])


def in_hbm(array):
    return pltpu.with_memory_space_constraint(array, pltpu.HBM)


def limit(mib):
    return pltpu.CompilerParams(vmem_limit_bytes=mib << 20)


def shards(params, moment_one, moment_two, camera, target, tile_ids, splat_lists, counts):
    wide = shape(59, 512)
    (
        sent,
        slope,
        lane,
        block,
        cast,
        column,
        places,
        chosen,
        before,
        behind,
        basis,
        params,
    ) = pl.pallas_call(
        pack_kernel,
        out_shape=(
            shape(OWNERS * SEND, 128),
            shape(36, 128),
            jax.ShapeDtypeStruct((48, 128), jnp.int32),
            jax.ShapeDtypeStruct((48, 128), jnp.int32),
            shape(88, 128),
            shape(48, 128),
            jax.ShapeDtypeStruct((256, 768), bf16),
            jax.ShapeDtypeStruct((32, 768), bf16),
            jax.ShapeDtypeStruct((512, 256), bf16),
            jax.ShapeDtypeStruct((512, 256), bf16),
            jax.ShapeDtypeStruct((16, 256), bf16),
            wide,
        ),
        in_specs=[HB] * 5,
        out_specs=(VM,) * 12,
        scratch_shapes=[
            pltpu.VMEM((SEND, 128), f32),
            pltpu.VMEM((256, 128), f32),
            pltpu.SMEM((3, 11), f32),
            pltpu.VMEM((VIEWS, 1, 256), jnp.int32),
            pltpu.SMEM((1, 3), jnp.int32),
            pltpu.SMEM((1, 3), jnp.int32),
            pltpu.SemaphoreType.DMA((8,)),
        ],
        compiler_params=limit(6),
        name="pack",
    )(
        in_hbm(params),
        in_hbm(camera),
        in_hbm(splat_lists),
        in_hbm(counts.reshape(1, VIEWS)),
        in_hbm(tile_ids.reshape(1, VIEWS)),
    )
    table = lax.all_to_all(
        sent.reshape(OWNERS, SEND, 128), TILE, split_axis=0, concat_axis=0, tiled=True
    ).reshape(OWNERS * SEND, 128)
    half = jax.ShapeDtypeStruct((48, 256), bf16)
    image, loss, shade, keep, pulled, stacked, high, low, entries = pl.pallas_call(
        front_kernel,
        out_shape=(
            shape(16, 256),
            shape(8, 128),
            shape(VIEWS * 256, 256),
            shape(VIEWS * 256, 256),
            half,
            half,
            jax.ShapeDtypeStruct((VIEWS * 256, 256), bf16),
            jax.ShapeDtypeStruct((VIEWS * 256, 256), bf16),
            shape(8 * KEPT, 128),
        ),
        in_specs=[VM] * 5 + [HB],
        out_specs=(VM,) * 9,
        scratch_shapes=[
            pltpu.VMEM((GROUPS * SEND, 128), f32),
            pltpu.VMEM((48, 256), f32),
            pltpu.VMEM((24, 256), f32),
            pltpu.VMEM((256, 512), bf16),
            pltpu.VMEM((VIEWS, 3, 1, 256), f32),
            pltpu.SemaphoreType.DMA((1,)),
        ],
        compiler_params=pltpu.CompilerParams(
            vmem_limit_bytes=16 << 20
        ),
        name="front",
    )(table, lane, block, cast, before, in_hbm(target))
    side = swapped(loss, lambda i: i ^ 2)
    grads, tint, moment_one, moment_two = pl.pallas_call(
        back_kernel,
        out_shape=(shape(16 * GEOMETRY, 128), shape(24, 256), wide, wide),
        in_specs=[VM] * 10 + [HB] * 2,
        out_specs=(VM,) * 4,
        scratch_shapes=[
            pltpu.VMEM((256, 512), bf16),
            pltpu.VMEM((256, 256), bf16),
            pltpu.VMEM((256, 256), bf16),
            pltpu.VMEM((64, 128), f32),
            pltpu.SemaphoreType.DMA((2,)),
        ],
        compiler_params=limit(12),
        cost_estimate=pl.CostEstimate(
            flops=1 << 31, bytes_accessed=1 << 23, transcendentals=1 << 20
        ),
        name="back",
    )(
        shade,
        keep,
        pulled,
        stacked,
        high,
        low,
        entries,
        cast,
        behind,
        basis,
        in_hbm(moment_one),
        in_hbm(moment_two),
    )
    pair = pl.pallas_call(
        pair_kernel,
        out_shape=shape(8, 128),
        in_specs=[VM] * 2,
        out_specs=VM,
        compiler_params=limit(2),
        name="pair",
    )(loss, side)
    wrap = swapped(pair, lambda i: i ^ 6)
    back = pl.pallas_call(
        scatter_kernel,
        out_shape=shape(OWNERS * SEND, 128),
        in_specs=[VM] * 4,
        out_specs=VM,
        scratch_shapes=[pltpu.VMEM((2 * 32 * GEOMETRY + 192, 768), bf16)],
        compiler_params=limit(12),
        cost_estimate=pl.CostEstimate(
            flops=1 << 31, bytes_accessed=1 << 23, transcendentals=1 << 20
        ),
        name="scatter",
    )(places, chosen, grads, tint)
    back = pl.pallas_call(
        note_kernel,
        out_shape=shape(OWNERS * SEND, 128),
        in_specs=[VM] * 3,
        out_specs=VM,
        compiler_params=limit(4),
        name="note",
    )(back, pair, wrap)
    arrived = lax.all_to_all(
        back.reshape(OWNERS, SEND, 128), TILE, split_axis=0, concat_axis=0, tiled=True
    ).reshape(OWNERS * SEND, 128)
    total, loss = pl.pallas_call(
        fold_kernel,
        out_shape=(shape(SEND, 128), shape(8, 128)),
        in_specs=[VM],
        out_specs=(VM, VM),
        compiler_params=limit(4),
        name="fold",
    )(arrived)
    core = swapped(loss, lambda i: i ^ 1)
    updated, first, second, rendered = pl.pallas_call(
        adam_kernel,
        out_shape=(wide, wide, wide, shape(VIEWS, 3, 1, 256)),
        in_specs=[VM] * 7,
        out_specs=(HB,) * 4,
        scratch_shapes=[
            pltpu.VMEM((256, 128), f32),
            pltpu.VMEM((59, 512), f32),
            pltpu.VMEM((59, 512), f32),
            pltpu.VMEM((59, 512), f32),
            pltpu.VMEM((VIEWS, 3, 1, 256), f32),
            pltpu.SemaphoreType.DMA((13,)),
        ],
        compiler_params=limit(4),
        cost_estimate=pl.CostEstimate(
            flops=1 << 30, bytes_accessed=1 << 22, transcendentals=1 << 16
        ),
        name="adam",
    )(total, slope, column, image, params, moment_one, moment_two)
    losses = (loss + core)[4, :VIEWS] * (0.5 / (3 * 256 * 128))
    return (updated, first, second, rendered, losses)


def solution(mesh):
    finer = Mesh(mesh.devices.reshape(4, 2, 4, 4), GAUSS_TILE)
    in_specs = (
        P(None, GAUSS_TILE),
        P(None, GAUSS_TILE),
        P(None, GAUSS_TILE),
        P(),
        P(None, None, GAUSS_TILE, None),
        P(None, GAUSS_TILE),
        P(None, GAUSS_TILE, None),
        P(None, GAUSS_TILE),
    )
    out_specs = (
        P(None, GAUSS_TILE),
        P(None, GAUSS_TILE),
        P(None, GAUSS_TILE),
        P(None, None, GAUSS_TILE, None),
        P(),
    )
    return jax.shard_map(
        shards, mesh=finer, in_specs=in_specs, out_specs=out_specs, check_vma=False
    )
```

```python
import jax
import jax.numpy as jnp
from jax import lax
from jax.experimental import pallas as pl
from jax.experimental.pallas import tpu as pltpu
from jax.sharding import Mesh
from jax.sharding import PartitionSpec as P

VIEWS = 3
TILES_WIDE = 4
TILE = ("tile_0", "tile_1")
GAUSS = ("gauss_0", "gauss_1")
GAUSS_TILE = ("gauss_0", "gauss_1", "tile_0", "tile_1")
OWNERS = 16
OWN = 512
GEOMETRY = 10
COLOURS = 4 * GEOMETRY
ERRORS = COLOURS + 36
SEND = ERRORS + 4
GROUPS = 6
KEPT = 32
LOG2E = 1.4426950408889634

band_zero = 0.28209479177387814
band_one = 0.4886025119029199
band_two = (
    1.0925484305920792,
    -1.0925484305920792,
    0.31539156525252005,
    -1.0925484305920792,
    0.5462742152960396,
)
band_three = (
    -0.5900435899266435,
    2.890611442640554,
    -0.4570457994644658,
    0.3731763325901154,
    -0.4570457994644658,
    1.445305721320277,
    -0.5900435899266435,
)

f32 = jnp.float32
bf16 = jnp.bfloat16


def iota(shape, dim):
    return lax.broadcasted_iota(jnp.int32, shape, dim)


def harmonic_halves(camera_ref, view):
    x, y, z = [jnp.full((8, 128), camera_ref[view, 8 + i], f32) for i in range(3)]
    xx, yy, zz = x * x, y * y, z * z
    values = [
        jnp.full((8, 128), band_zero, f32),
        -band_one * y,
        band_one * z,
        -band_one * x,
        band_two[0] * x * y,
        band_two[1] * y * z,
        band_two[2] * (2.0 * zz - xx - yy),
        band_two[3] * x * z,
        band_two[4] * (xx - yy),
        band_three[0] * y * (3.0 * xx - yy),
        band_three[1] * x * y * z,
        band_three[2] * y * (4.0 * zz - xx - yy),
        band_three[3] * z * (2.0 * zz - 3.0 * xx - 3.0 * yy),
        band_three[4] * x * (4.0 * zz - xx - yy),
        band_three[5] * z * (xx - yy),
        band_three[6] * x * (xx - 3.0 * yy),
    ]
    row = iota((8, 128), 0)
    halves = []
    for half in range(2):
        column = values[8 * half]
        for i in range(1, 8):
            column = jnp.where(row == i, values[8 * half + i], column)
        halves.append(column)
    return halves


def per_view(values):
    place = iota((GROUPS, 128), 0)
    return jnp.where(place < 2, values[0], jnp.where(place < 4, values[1], values[2]))


def pack_kernel(
    params_hbm,
    camera_hbm,
    lists_hbm,
    counts_hbm,
    tiles_hbm,
    send_ref,
    slope_ref,
    lane_ref,
    block_ref,
    cast_ref,
    column_ref,
    places_ref,
    chosen_ref,
    before_ref,
    behind_ref,
    basis_ref,
    params_ref,
    pack_ref,
    tall_ref,
    camera_ref,
    lists_ref,
    counts_ref,
    tiles_ref,
    sems,
):
    sources = [camera_hbm, counts_hbm, tiles_hbm, lists_hbm]
    targets = [camera_ref, counts_ref, tiles_ref, lists_ref]
    for quarter in range(4):
        lanes = pl.ds(128 * quarter, 128)
        sources.append(params_hbm.at[:, lanes])
        targets.append(params_ref.at[:, lanes])
    copies = [
        pltpu.make_async_copy(source, target, sems.at[n])
        for n, (source, target) in enumerate(zip(sources, targets))
    ]
    for copy in copies:
        copy.start()

    first = iota((256, 256), 0)
    second = iota((256, 256), 1)
    for ref, strictly in ((before_ref, first < second), (behind_ref, first > second)):
        ones = jnp.where(strictly, 1.0, 0.0).astype(bf16)
        ref[0:256, :] = ones
        ref[256:512, :] = ones
    pixel = iota((16, 256), 1)
    power = iota((16, 256), 0)
    pixel_u = (pixel % 16).astype(f32) - 7.5
    pixel_v = (pixel // 16).astype(f32) - 7.5
    basis = jnp.where(power == 0, 1.0, jnp.where(power == 1, pixel_u, pixel_v))
    basis = jnp.where(power == 3, pixel_u * pixel_u, basis)
    basis = jnp.where(power == 4, pixel_u * pixel_v, basis)
    basis = jnp.where(power == 5, pixel_v * pixel_v, basis)
    basis_ref[...] = jnp.where(power > 5, 0.0, basis).astype(bf16)
    for copy in copies[0:4]:
        copy.wait()
    columns = [harmonic_halves(camera_ref, view) for view in range(VIEWS)]
    quarter = iota((8, 128), 0) & 3
    fine = iota((256, 128), 0)
    coarse = iota((32, 128), 0)
    for group in range(GROUPS):
        view, half = divmod(group, 2)
        local = lists_ref[view, :, 128 * half : 128 * half + 128] & 8191
        spread = jnp.broadcast_to(local, (8, 128))
        lane_ref[pl.ds(8 * group, 8), :] = spread & 127
        block_ref[pl.ds(8 * group, 8), :] = (spread >> 7) - quarter
        lanes = pl.ds(128 * group, 128)
        places_ref[:, lanes] = jnp.where((local & 255) == fine, 1.0, 0.0).astype(bf16)
        owner_part = ((local >> 8) & 1) * 16 + (local >> 9)
        chosen_ref[:, lanes] = jnp.where(owner_part == coarse, 1.0, 0.0).astype(bf16)
    for i in range(8):
        cast_ref[pl.ds(8 * i, GROUPS), :] = per_view(
            [camera_ref[view, i] for view in range(VIEWS)]
        )
    place = iota((GROUPS, 128), 0)
    position = (place & 1) * 128 + iota((GROUPS, 128), 1)
    live = position < per_view([counts_ref[0, view] for view in range(VIEWS)])
    cast_ref[pl.ds(64, GROUPS), :] = jnp.where(live, 1.0, 0.0)
    tile = per_view([tiles_ref[0, view] for view in range(VIEWS)])
    cast_ref[pl.ds(72, GROUPS), :] = (tile % TILES_WIDE * 16 + 8).astype(f32)
    cast_ref[pl.ds(80, GROUPS), :] = (tile // TILES_WIDE * 16 + 8).astype(f32)
    for view in range(VIEWS):
        for half in range(2):
            column_ref[pl.ds(16 * view + 8 * half, 8), :] = columns[view][half]
    for quarter in range(4):
        copies[4 + quarter].wait()
        lanes = pl.ds(128 * quarter, 128)
        pack_ref[pl.ds(quarter, 6, stride=4), :] = params_ref[0:6, lanes]
        pack_ref[pl.ds(24 + quarter, 3, stride=4), :] = (
            params_ref[7:10, lanes] / params_ref[6:7, lanes]
        )
        pack_ref[pl.ds(36 + quarter, 1), :] = params_ref[10:11, lanes]
        tall_ref[pl.ds(64 * quarter, 59), :] = params_ref[:, lanes]
    for k in range(3):
        for quarter in range(4):
            low = tall_ref[pl.ds(64 * quarter + 11 + k, 8, stride=3), :]
            high = tall_ref[pl.ds(64 * quarter + 35 + k, 8, stride=3), :]
            for view in range(VIEWS):
                terms = columns[view][0] * low + columns[view][1] * high
                raw = jnp.sum(terms, axis=0, keepdims=True) + 0.5
                row = 4 * (3 * view + k) + quarter
                pack_ref[pl.ds(COLOURS + row, 1), :] = jnp.maximum(raw, 0.0)
                slope_ref[pl.ds(row, 1), :] = jnp.where(
                    raw > 0.0, 1.0, jnp.where(raw == 0.0, 0.5, 0.0)
                )
    pack_ref[pl.ds(ERRORS, 4), :] = jnp.zeros((4, 128), f32)
    packed = pack_ref[...]
    for owner in range(OWNERS):
        send_ref[pl.ds(SEND * owner, SEND), :] = packed


def split(value):
    high = value.astype(bf16)
    return high, (value - high.astype(f32)).astype(bf16)


def nn(lhs, rhs):
    return lax.dot_general(lhs, rhs, (((1,), (0,)), ((), ())), preferred_element_type=f32)


def nt(lhs, rhs):
    return lax.dot_general(lhs, rhs, (((1,), (1,)), ((), ())), preferred_element_type=f32)


def tn(lhs, rhs):
    return lax.dot_general(lhs, rhs, (((0,), (0,)), ((), ())), preferred_element_type=f32)


def front_kernel(
    table_ref,
    lane_ref,
    block_ref,
    cast_ref,
    before_ref,
    target_hbm,
    image_ref,
    loss_ref,
    shade_ref,
    keep_ref,
    pulled_ref,
    stacked_ref,
    high_ref,
    low_ref,
    entry_ref,
    found_ref,
    rows_ref,
    colour_ref,
    logs_ref,
    target_ref,
    sem,
):
    goal = pltpu.make_async_copy(target_hbm, target_ref, sem.at[0])
    goal.start()
    for group in range(GROUPS):
        view, half = divmod(group, 2)
        lane = lane_ref[pl.ds(8 * group, 8), :]
        block = block_ref[pl.ds(8 * group, 8), :]
        first = (COLOURS + 12 * view) // 8
        last = (COLOURS + 12 * view + 11) // 8
        pieces = list(range(5)) + list(range(first, last + 1))
        found = {piece: jnp.zeros((8, 128), f32) for piece in pieces}
        for owner in range(OWNERS):
            here = block == 4 * owner
            for piece in pieces:
                rows = table_ref[pl.ds(SEND * owner + 8 * piece, 8), :]
                picked = jnp.take_along_axis(rows, lane, axis=1, mode="promise_in_bounds")
                found[piece] = jnp.where(here, picked, found[piece])
        for piece in pieces:
            found_ref[pl.ds(SEND * group + 8 * piece, 8), :] = found[piece]

    def entry_row(row):
        parts = [found_ref[pl.ds(4 * row + q, GROUPS, stride=SEND), :] for q in range(4)]
        return (parts[0] + parts[1]) + (parts[2] + parts[3])

    for group in range(GROUPS):
        view, half = divmod(group, 2)
        for k in range(3):
            start = SEND * group + COLOURS + 4 * (3 * view + k)
            value = jnp.sum(found_ref[pl.ds(start, 4), :], axis=0, keepdims=True)
            colour_ref[pl.ds(8 * view + k, 1), pl.ds(128 * half, 128)] = value

    camera = [cast_ref[pl.ds(8 * i, GROUPS), :] for i in range(8)]
    affine = (camera[0:3], camera[3:6])
    centre = [entry_row(i) for i in range(3)]
    scale = [jnp.exp(entry_row(3 + i)) for i in range(3)]
    ratio = [entry_row(6 + i) for i in range(3)]
    logit = entry_row(9)
    inverse_norm = 1.0 / jnp.sqrt(
        1.0 + ratio[0] * ratio[0] + ratio[1] * ratio[1] + ratio[2] * ratio[2]
    )
    qw = inverse_norm
    qx, qy, qz = [component * inverse_norm for component in ratio]
    rotation = [
        [1.0 - 2.0 * (qy * qy + qz * qz), 2.0 * (qx * qy - qw * qz), 2.0 * (qx * qz + qw * qy)],
        [2.0 * (qx * qy + qw * qz), 1.0 - 2.0 * (qx * qx + qz * qz), 2.0 * (qy * qz - qw * qx)],
        [2.0 * (qx * qz - qw * qy), 2.0 * (qy * qz + qw * qx), 1.0 - 2.0 * (qx * qx + qy * qy)],
    ]
    stretched = [[rotation[i][j] * scale[j] for j in range(3)] for i in range(3)]
    screen = [
        [sum(affine[k][i] * stretched[i][j] for i in range(3)) for j in range(3)] for k in range(2)
    ]
    cov_a = sum(screen[0][j] * screen[0][j] for j in range(3)) + 0.3
    cov_b = sum(screen[0][j] * screen[1][j] for j in range(3))
    cov_c = sum(screen[1][j] * screen[1][j] for j in range(3)) + 0.3
    inverse_det = 1.0 / (cov_a * cov_c - cov_b * cov_b)
    live = cast_ref[pl.ds(64, GROUPS), :] > 0.5
    conic = [
        jnp.where(live, value * inverse_det, 0.0) for value in (cov_c, -cov_b, cov_a)
    ]
    mean = [sum(affine[k][i] * centre[i] for i in range(3)) + camera[6 + k] for k in range(2)]
    opacity = 1.0 / (1.0 + jnp.exp(-logit))
    shown = jnp.where(live, opacity, 0.0)
    shift_x = mean[0] - cast_ref[pl.ds(72, GROUPS), :]
    shift_y = mean[1] - cast_ref[pl.ds(80, GROUPS), :]
    kept = (
        [shift_x, shift_y]
        + [(-0.5 * LOG2E) * conic[0], (-LOG2E) * conic[1], (-0.5 * LOG2E) * conic[2]]
        + [shown, opacity, qw, qx, qy, qz]
        + conic
        + scale
        + screen[0]
        + screen[1]
        + stretched[0]
        + stretched[1]
        + stretched[2]
    )
    for n, value in enumerate(kept):
        entry_ref[pl.ds(8 * n, GROUPS), :] = value
    for n in range(6):
        for half in range(2):
            rows_ref[pl.ds(8 * n, VIEWS), pl.ds(128 * half, 128)] = entry_ref[
                pl.ds(8 * n + half, VIEWS, stride=2), :
            ]

    goal.wait()
    offset = iota((16, 256), 0).astype(f32) - 7.5
    losses = jnp.zeros((8, 128), f32)

    for view in range(VIEWS):

        def row(n, view=view):
            return rows_ref[pl.ds(8 * n + view, 1), :]

        mean_u, mean_v = row(0), row(1)
        opaque = jnp.broadcast_to(row(5), (16, 256))
        dx = offset - mean_u
        along = row(2) * dx * dx
        across = row(3) * dx
        upright = row(4)
        base = 256 * view
        for line in range(16):
            dy = (line - 7.5) - mean_v
            exponent = along + (upright * dy * dy + across * dy)
            shade = opaque * jnp.exp2(exponent)
            shade_ref[pl.ds(base + 16 * line, 16), :] = shade
            high, low = split(jnp.log(1.0 - jnp.minimum(shade, 0.99)))
            logs_ref[pl.ds(16 * line, 16), 0:256] = high
            logs_ref[pl.ds(16 * line, 16), 256:512] = low
        for part in range(4):
            rows = pl.ds(64 * part, 64)
            there = pl.ds(base + 64 * part, 64)
            keep = jnp.exp(nn(logs_ref[rows, :], before_ref[...]))
            keep_ref[there, :] = keep
            high, low = split(jnp.minimum(shade_ref[there, :], 0.99) * keep)
            high_ref[there, :] = high
            low_ref[there, :] = low
        colour = colour_ref[pl.ds(8 * view, 8), :]
        colour_high, colour_low = [part.astype(f32) for part in split(colour)]
        stacked = jnp.concatenate(
            [
                colour_high[0:3],
                colour_high[0:3],
                colour_low[0:3],
                jnp.zeros((7, 256), f32),
            ],
            axis=0,
        ).astype(bf16)
        image_high = nt(stacked, high_ref[pl.ds(base, 256), :])
        image_low = nt(stacked, low_ref[pl.ds(base, 256), :])
        image = image_high[0:3] + image_high[6:9] + image_low[0:3]
        residuals = []
        total = jnp.zeros((1, 256), f32)
        for k in range(3):
            image_ref[pl.ds(3 * view + k, 1), :] = image[k : k + 1]
            residual = image[k : k + 1] - target_ref[view, k, :, :]
            total = total + residual * residual
            residuals.append(residual * (1.0 / (VIEWS * 256)))
        losses = jnp.where(iota((8, 128), 1) == view, jnp.sum(total, axis=1, keepdims=True), losses)
        error = jnp.concatenate(residuals, axis=0)
        error_high, error_low = [part.astype(f32) for part in split(error)]
        pulled = jnp.concatenate(
            [error_high, error_low, error_high, jnp.zeros((7, 256), f32)], axis=0
        ).astype(bf16)
        pulled_ref[pl.ds(16 * view, 16), :] = pulled
        stacked_ref[pl.ds(16 * view, 16), :] = stacked
    loss_ref[...] = losses


def back_kernel(
    shade_ref,
    keep_ref,
    pulled_ref,
    stacked_ref,
    weight_high_ref,
    weight_low_ref,
    entry_ref,
    cast_ref,
    behind_ref,
    basis_ref,
    moment_one_hbm,
    moment_two_hbm,
    grads_ref,
    tint_ref,
    moment_one_ref,
    moment_two_ref,
    logs_ref,
    high_ref,
    low_ref,
    moment_ref,
    sems,
):
    copies = [
        pltpu.make_async_copy(moment_one_hbm, moment_one_ref, sems.at[0]),
        pltpu.make_async_copy(moment_two_hbm, moment_two_ref, sems.at[1]),
    ]
    for copy in copies:
        copy.start()
    basis = basis_ref[...]

    for view in range(VIEWS):
        base = 256 * view
        small = pl.ds(16 * view, 16)
        pulled = pulled_ref[small, :]
        pull = tn(pulled, stacked_ref[small, :])
        tint = nn(pulled, weight_high_ref[pl.ds(base, 256), :])
        tint_low = nn(pulled, weight_low_ref[pl.ds(base, 256), :])
        tint_ref[pl.ds(8 * view, 3), :] = tint[0:3] + tint[3:6] + tint_low[0:3]
        for part in range(4):
            rows = pl.ds(64 * part, 64)
            there = pl.ds(base + 64 * part, 64)
            weight = jnp.minimum(shade_ref[there, :], 0.99) * keep_ref[there, :]
            high, low = split(pull[64 * part : 64 * part + 64] * weight)
            logs_ref[rows, 0:256] = high
            logs_ref[rows, 256:512] = low
        for part in range(4):
            rows = pl.ds(64 * part, 64)
            there = pl.ds(base + 64 * part, 64)
            behind = nn(logs_ref[rows, :], behind_ref[...])
            shade = shade_ref[there, :]
            alpha = jnp.minimum(shade, 0.99)
            slope = pull[64 * part : 64 * part + 64] * keep_ref[there, :] - behind / (1.0 - alpha)
            passed = jnp.where(shade < 0.99, shade, jnp.where(shade == 0.99, 0.5 * shade, 0.0))
            high, low = split(slope * passed)
            high_ref[rows, :] = high
            low_ref[rows, :] = low
        moments = nn(basis, high_ref[...]) + nn(basis, low_ref[...])
        for half in range(2):
            moment_ref[pl.ds(2 * view + half, 8, stride=8), :] = moments[
                0:8, 128 * half : 128 * half + 128
            ]

    kept = [entry_ref[pl.ds(8 * n, GROUPS), :] for n in range(KEPT)]
    shift_x, shift_y = kept[0:2]
    opacity, qw, qx, qy, qz = kept[6:11]
    conic = kept[11:14]
    scale = kept[14:17]
    screen = (kept[17:20], kept[20:23])
    stretched = (kept[23:26], kept[26:29], kept[29:32])
    camera = [cast_ref[pl.ds(8 * i, GROUPS), :] for i in range(6)]
    affine = (camera[0:3], camera[3:6])
    m_0, m_u, m_v, m_uu, m_uv, m_vv = [
        moment_ref[pl.ds(8 * n, GROUPS), :] for n in range(6)
    ]
    m_x = m_u - shift_x * m_0
    m_y = m_v - shift_y * m_0
    m_xx = m_uu - 2.0 * shift_x * m_u + shift_x * shift_x * m_0
    m_xy = m_uv - shift_x * m_v - shift_y * m_u + shift_x * shift_y * m_0
    m_yy = m_vv - 2.0 * shift_y * m_v + shift_y * shift_y * m_0
    d_mean = (conic[0] * m_x + conic[1] * m_y, conic[1] * m_x + conic[2] * m_y)
    left = (
        (conic[0] * m_xx + conic[1] * m_xy, conic[0] * m_xy + conic[1] * m_yy),
        (conic[1] * m_xx + conic[2] * m_xy, conic[1] * m_xy + conic[2] * m_yy),
    )
    d_a = 0.5 * (left[0][0] * conic[0] + left[0][1] * conic[1])
    d_b = left[0][0] * conic[1] + left[0][1] * conic[2]
    d_c = 0.5 * (left[1][0] * conic[1] + left[1][1] * conic[2])
    d_screen = [
        [2.0 * d_a * screen[0][j] + d_b * screen[1][j] for j in range(3)],
        [2.0 * d_c * screen[1][j] + d_b * screen[0][j] for j in range(3)],
    ]
    d_stretched = [
        [affine[0][i] * d_screen[0][j] + affine[1][i] * d_screen[1][j] for j in range(3)]
        for i in range(3)
    ]
    d_scale = [sum(d_stretched[i][j] * stretched[i][j] for i in range(3)) for j in range(3)]
    r = [[d_stretched[i][j] * scale[j] for j in range(3)] for i in range(3)]
    d_unit = [
        2.0 * (qz * (r[1][0] - r[0][1]) + qy * (r[0][2] - r[2][0]) + qx * (r[2][1] - r[1][2])),
        2.0
        * (
            qy * (r[0][1] + r[1][0])
            + qz * (r[0][2] + r[2][0])
            + qw * (r[2][1] - r[1][2])
            - 2.0 * qx * (r[1][1] + r[2][2])
        ),
        2.0
        * (
            qx * (r[0][1] + r[1][0])
            + qz * (r[1][2] + r[2][1])
            + qw * (r[0][2] - r[2][0])
            - 2.0 * qy * (r[0][0] + r[2][2])
        ),
        2.0
        * (
            qx * (r[0][2] + r[2][0])
            + qy * (r[1][2] + r[2][1])
            + qw * (r[1][0] - r[0][1])
            - 2.0 * qz * (r[0][0] + r[1][1])
        ),
    ]
    unit = (qw, qx, qy, qz)
    radial = sum(unit[i] * d_unit[i] for i in range(4))
    gradients = (
        [affine[0][i] * d_mean[0] + affine[1][i] * d_mean[1] for i in range(3)]
        + d_scale
        + [(d_unit[i] - unit[i] * radial) * qw for i in range(1, 4)]
        + [m_0 * (1.0 - opacity)]
    )
    for n, value in enumerate(gradients):
        high = value.astype(bf16).astype(f32)
        grads_ref[pl.ds(16 * n, GROUPS), :] = high
        grads_ref[pl.ds(16 * n + 8, GROUPS), :] = value - high
    for copy in copies:
        copy.wait()


def scatter_kernel(
    places_ref,
    chosen_ref,
    grads_ref,
    tint_ref,
    back_ref,
    spread_ref,
):
    kinds_of = GEOMETRY * 32
    for group in range(GROUPS):
        view, half = divmod(group, 2)
        lanes = pl.ds(128 * group, 128)
        chosen = chosen_ref[:, lanes]
        for n in range(GEOMETRY):
            for part in range(2):
                value = grads_ref[pl.ds(16 * n + 8 * part + group, 1), :]
                spread_ref[pl.ds(kinds_of * part + 32 * n, 32), lanes] = (
                    chosen * jnp.broadcast_to(value, (32, 128)).astype(bf16)
                )
        for k in range(3):
            value = tint_ref[pl.ds(8 * view + k, 1), pl.ds(128 * half, 128)]
            high = value.astype(bf16).astype(f32)
            for part, piece in enumerate((high, value - high)):
                spread_ref[pl.ds(2 * kinds_of + 96 * part + 32 * k, 32), lanes] = (
                    chosen * jnp.broadcast_to(piece, (32, 128)).astype(bf16)
                )

    def store(row, value):
        for upper in range(2):
            for side in range(2):
                back_ref[pl.ds(4 * row + 2 * upper + side, 16, stride=SEND), :] = value[
                    16 * upper : 16 * upper + 16, 128 * side : 128 * side + 128
                ]

    dense = nt(spread_ref[0 : 2 * kinds_of, :], places_ref[...])
    for n in range(GEOMETRY):
        store(n, dense[32 * n : 32 * n + 32] + dense[kinds_of + 32 * n : kinds_of + 32 * n + 32])
    for view in range(VIEWS):
        lanes = slice(256 * view, 256 * view + 256)
        dense = nt(spread_ref[2 * kinds_of : 2 * kinds_of + 192, lanes], places_ref[:, lanes])
        for k in range(3):
            store(
                GEOMETRY + 3 * view + k,
                dense[32 * k : 32 * k + 32] + dense[96 + 32 * k : 96 + 32 * k + 32],
            )
    for owner in range(OWNERS):
        back_ref[pl.ds(SEND * owner + ERRORS, 4), :] = jnp.zeros((4, 128), f32)


def pair_kernel(mine_ref, theirs_ref, sum_ref):
    sum_ref[...] = mine_ref[...] + theirs_ref[...]


def note_kernel(back_ref, mine_ref, theirs_ref, noted_ref):
    losses = mine_ref[0:4, :] + theirs_ref[0:4, :]
    noted_ref[...] = back_ref[...]
    for owner in range(OWNERS):
        noted_ref[pl.ds(SEND * owner + ERRORS, 4), :] = losses


def fold_kernel(back_ref, total_ref, loss_ref):
    total = back_ref[0:SEND, :]
    for owner in range(1, OWNERS):
        total = total + back_ref[pl.ds(SEND * owner, SEND), :]
    total_ref[...] = total
    loss_ref[...] = total[SEND - 8 : SEND]


def adam_kernel(
    total_ref,
    slope_ref,
    column_ref,
    image_ref,
    params_ref,
    moment_one_ref,
    moment_two_ref,
    params_hbm,
    first_hbm,
    second_hbm,
    rendered_hbm,
    gradient_ref,
    params_out,
    first_out,
    second_out,
    rendered_out,
    sems,
):
    for view in range(VIEWS):
        for k in range(3):
            rendered_out[view, k, :, :] = image_ref[pl.ds(3 * view + k, 1), :]
    copies = [pltpu.make_async_copy(rendered_out, rendered_hbm, sems.at[0])]
    copies[0].start()
    columns = [
        [column_ref[pl.ds(16 * view + 8 * half, 8), :] for half in range(2)]
        for view in range(VIEWS)
    ]
    row = iota((59, 128), 0)
    rates = jnp.where(row < 14, 0.0025, 0.000125)
    rates = jnp.where(row < 11, 0.05, rates)
    rates = jnp.where(row < 10, 0.001, rates)
    rates = jnp.where(row < 6, 0.005, rates)
    rates = jnp.where(row < 3, 0.00016, rates)
    for quarter in range(4):
        lanes = pl.ds(128 * quarter, 128)
        base = 64 * quarter
        gradient_ref[pl.ds(base, 6), :] = total_ref[pl.ds(quarter, 6, stride=4), :]
        w = params_ref[6:7, lanes]
        d_ratio = total_ref[pl.ds(24 + quarter, 3, stride=4), :] / w
        lean = jnp.sum(d_ratio * params_ref[7:10, lanes], axis=0, keepdims=True)
        gradient_ref[pl.ds(base + 6, 1), :] = -lean / w
        gradient_ref[pl.ds(base + 7, 3), :] = d_ratio
        gradient_ref[pl.ds(base + 10, 1), :] = total_ref[pl.ds(36 + quarter, 1), :]
        for k in range(3):
            tints = []
            for view in range(VIEWS):
                place = 4 * (3 * view + k) + quarter
                tint = total_ref[pl.ds(COLOURS + place, 1), :] * slope_ref[pl.ds(place, 1), :]
                tints.append(jnp.broadcast_to(tint, (8, 128)))
            for half in range(2):
                gradient_ref[pl.ds(base + 11 + 24 * half + k, 8, stride=3), :] = sum(
                    columns[view][half] * tints[view] for view in range(VIEWS)
                )
        gradient = gradient_ref[pl.ds(base, 59), :]
        first = 0.9 * moment_one_ref[:, lanes] + 0.1 * gradient
        second = 0.999 * moment_two_ref[:, lanes] + 0.001 * gradient * gradient
        first_out[:, lanes] = first
        second_out[:, lanes] = second
        params_out[:, lanes] = params_ref[:, lanes] - rates * first / (jnp.sqrt(second) + 1e-15)
        pairs = ((params_out, params_hbm), (first_out, first_hbm), (second_out, second_hbm))
        for n, (source, target) in enumerate(pairs):
            copy = pltpu.make_async_copy(
                source.at[:, lanes], target.at[:, lanes], sems.at[1 + 3 * quarter + n]
            )
            copy.start()
            copies.append(copy)
    for copy in copies:
        copy.wait()


VM = pl.BlockSpec(memory_space=pltpu.VMEM)
SM = pl.BlockSpec(memory_space=pltpu.SMEM)
HB = pl.BlockSpec(memory_space=pltpu.HBM)


def shape(*dims):
    return jax.ShapeDtypeStruct(dims, f32)


def swapped(value, partner):
    return lax.ppermute(value, GAUSS, [(i, partner(i)) for i in range(8)])


def in_hbm(array):
    return pltpu.with_memory_space_constraint(array, pltpu.HBM)


def limit(mib):
    return pltpu.CompilerParams(vmem_limit_bytes=mib << 20)


def shards(params, moment_one, moment_two, camera, target, tile_ids, splat_lists, counts):
    wide = shape(59, 512)
    (
        sent,
        slope,
        lane,
        block,
        cast,
        column,
        places,
        chosen,
        before,
        behind,
        basis,
        params,
    ) = pl.pallas_call(
        pack_kernel,
        out_shape=(
            shape(OWNERS * SEND, 128),
            shape(36, 128),
            jax.ShapeDtypeStruct((48, 128), jnp.int32),
            jax.ShapeDtypeStruct((48, 128), jnp.int32),
            shape(88, 128),
            shape(48, 128),
            jax.ShapeDtypeStruct((256, 768), bf16),
            jax.ShapeDtypeStruct((32, 768), bf16),
            jax.ShapeDtypeStruct((512, 256), bf16),
            jax.ShapeDtypeStruct((512, 256), bf16),
            jax.ShapeDtypeStruct((16, 256), bf16),
            wide,
        ),
        in_specs=[HB] * 5,
        out_specs=(VM,) * 12,
        scratch_shapes=[
            pltpu.VMEM((SEND, 128), f32),
            pltpu.VMEM((256, 128), f32),
            pltpu.SMEM((3, 11), f32),
            pltpu.VMEM((VIEWS, 1, 256), jnp.int32),
            pltpu.SMEM((1, 3), jnp.int32),
            pltpu.SMEM((1, 3), jnp.int32),
            pltpu.SemaphoreType.DMA((8,)),
        ],
        compiler_params=limit(6),
        name="pack",
    )(
        in_hbm(params),
        in_hbm(camera),
        in_hbm(splat_lists),
        in_hbm(counts.reshape(1, VIEWS)),
        in_hbm(tile_ids.reshape(1, VIEWS)),
    )
    table = lax.all_to_all(
        sent.reshape(OWNERS, SEND, 128), TILE, split_axis=0, concat_axis=0, tiled=True
    ).reshape(OWNERS * SEND, 128)
    half = jax.ShapeDtypeStruct((48, 256), bf16)
    image, loss, shade, keep, pulled, stacked, high, low, entries = pl.pallas_call(
        front_kernel,
        out_shape=(
            shape(16, 256),
            shape(8, 128),
            shape(VIEWS * 256, 256),
            shape(VIEWS * 256, 256),
            half,
            half,
            jax.ShapeDtypeStruct((VIEWS * 256, 256), bf16),
            jax.ShapeDtypeStruct((VIEWS * 256, 256), bf16),
            shape(8 * KEPT, 128),
        ),
        in_specs=[VM] * 5 + [HB],
        out_specs=(VM,) * 9,
        scratch_shapes=[
            pltpu.VMEM((8 * SEND, 128), f32),
            pltpu.VMEM((48, 256), f32),
            pltpu.VMEM((24, 256), f32),
            pltpu.VMEM((256, 512), bf16),
            pltpu.VMEM((VIEWS, 3, 1, 256), f32),
            pltpu.SemaphoreType.DMA((1,)),
        ],
        compiler_params=pltpu.CompilerParams(
            vmem_limit_bytes=16 << 20
        ),
        name="front",
    )(table, lane, block, cast, before, in_hbm(target))
    side = swapped(loss, lambda i: i ^ 2)
    grads, tint, moment_one, moment_two = pl.pallas_call(
        back_kernel,
        out_shape=(shape(16 * GEOMETRY, 128), shape(24, 256), wide, wide),
        in_specs=[VM] * 10 + [HB] * 2,
        out_specs=(VM,) * 4,
        scratch_shapes=[
            pltpu.VMEM((256, 512), bf16),
            pltpu.VMEM((256, 256), bf16),
            pltpu.VMEM((256, 256), bf16),
            pltpu.VMEM((64, 128), f32),
            pltpu.SemaphoreType.DMA((2,)),
        ],
        compiler_params=limit(12),
        cost_estimate=pl.CostEstimate(
            flops=1 << 31, bytes_accessed=1 << 23, transcendentals=1 << 20
        ),
        name="back",
    )(
        shade,
        keep,
        pulled,
        stacked,
        high,
        low,
        entries,
        cast,
        behind,
        basis,
        in_hbm(moment_one),
        in_hbm(moment_two),
    )
    pair = pl.pallas_call(
        pair_kernel,
        out_shape=shape(8, 128),
        in_specs=[VM] * 2,
        out_specs=VM,
        compiler_params=limit(2),
        name="pair",
    )(loss, side)
    wrap = swapped(pair, lambda i: i ^ 6)
    back = pl.pallas_call(
        scatter_kernel,
        out_shape=shape(OWNERS * SEND, 128),
        in_specs=[VM] * 4,
        out_specs=VM,
        scratch_shapes=[pltpu.VMEM((2 * 32 * GEOMETRY + 192, 768), bf16)],
        compiler_params=limit(12),
        cost_estimate=pl.CostEstimate(
            flops=1 << 31, bytes_accessed=1 << 23, transcendentals=1 << 20
        ),
        name="scatter",
    )(places, chosen, grads, tint)
    back = pl.pallas_call(
        note_kernel,
        out_shape=shape(OWNERS * SEND, 128),
        in_specs=[VM] * 3,
        out_specs=VM,
        compiler_params=limit(4),
        name="note",
    )(back, pair, wrap)
    arrived = lax.all_to_all(
        back.reshape(OWNERS, SEND, 128), TILE, split_axis=0, concat_axis=0, tiled=True
    ).reshape(OWNERS * SEND, 128)
    total, loss = pl.pallas_call(
        fold_kernel,
        out_shape=(shape(SEND, 128), shape(8, 128)),
        in_specs=[VM],
        out_specs=(VM, VM),
        compiler_params=limit(4),
        name="fold",
    )(arrived)
    core = swapped(loss, lambda i: i ^ 1)
    updated, first, second, rendered = pl.pallas_call(
        adam_kernel,
        out_shape=(wide, wide, wide, shape(VIEWS, 3, 1, 256)),
        in_specs=[VM] * 7,
        out_specs=(HB,) * 4,
        scratch_shapes=[
            pltpu.VMEM((256, 128), f32),
            pltpu.VMEM((59, 512), f32),
            pltpu.VMEM((59, 512), f32),
            pltpu.VMEM((59, 512), f32),
            pltpu.VMEM((VIEWS, 3, 1, 256), f32),
            pltpu.SemaphoreType.DMA((13,)),
        ],
        compiler_params=limit(4),
        cost_estimate=pl.CostEstimate(
            flops=1 << 30, bytes_accessed=1 << 22, transcendentals=1 << 16
        ),
        name="adam",
    )(total, slope, column, image, params, moment_one, moment_two)
    losses = (loss + core)[4, :VIEWS] * (0.5 / (3 * 256 * 128))
    return (updated, first, second, rendered, losses)


def solution(mesh):
    finer = Mesh(mesh.devices.reshape(4, 2, 4, 4), GAUSS_TILE)
    in_specs = (
        P(None, GAUSS_TILE),
        P(None, GAUSS_TILE),
        P(None, GAUSS_TILE),
        P(),
        P(None, None, GAUSS_TILE, None),
        P(None, GAUSS_TILE),
        P(None, GAUSS_TILE, None),
        P(None, GAUSS_TILE),
    )
    out_specs = (
        P(None, GAUSS_TILE),
        P(None, GAUSS_TILE),
        P(None, GAUSS_TILE),
        P(None, None, GAUSS_TILE, None),
        P(),
    )
    return jax.shard_map(
        shards, mesh=finer, in_specs=in_specs, out_specs=out_specs, check_vma=False
    )
```
